32 devices in a mesh: dp: 4 (over z), mp: 8 (over y, x, core).
Axes of the slice: x: 2, y: 2, z: 4, core: 2. Of those that a mesh axis runs over, the one named last changes fastest.
Arguments:
- tokens: bfloat16 [8192, 2048], P(('dp', 'mp')), may hold values from -6 to 6
- segment: int32 [8192], P('dp'), may hold values from 0 to 2, as said below
- valid: int32 [8192], replicated, may hold values from 0 to 1
- gain_attn: float32 [2048], replicated, may hold values from 0.5 to 1.5
- w_query: bfloat16 [2048, 2048], P(None, 'mp'), may hold values from -0.125 to 0.125
- w_key: bfloat16 [2048, 2048], P(None, 'mp'), may hold values from -0.125 to 0.125
- w_value: bfloat16 [2048, 2048], P(None, 'mp'), may hold values from -0.125 to 0.125
- w_out: bfloat16 [2048, 2048], P('mp'), may hold values from -3 to 3
- gain_mlp: float32 [2048], replicated, may hold values from 0.5 to 1.5
- w_up: bfloat16 [2048, 8192], P(None, 'mp'), may hold values from -0.125 to 0.125
- w_down: bfloat16 [8192, 2048], P('mp'), may hold values from -0.0625 to 0.0625
- grad_out: bfloat16 [8192, 2048], P(('dp', 'mp')), may hold values from -6 to 6
Outputs:
- out_tokens: bfloat16 [8192, 2048], P(('dp', 'mp'))
- grad_tokens: bfloat16 [8192, 2048], P(('dp', 'mp'))
- grad_gain_attn: float32 [2048], P(('dp', 'mp'))
- grad_query: float32 [2048, 2048], P('dp', 'mp')
- grad_key: float32 [2048, 2048], P('dp', 'mp')
- grad_value: float32 [2048, 2048], P('dp', 'mp')
- grad_out_proj: float32 [2048, 2048], P('mp', 'dp')
- grad_gain_mlp: float32 [2048], P(('dp', 'mp'))
- grad_up: float32 [2048, 8192], P('dp', 'mp')
- grad_down: float32 [8192, 2048], P('mp', 'dp')
- rms_stream: float32 [], replicated
- rms_attn: float32 [], replicated
- rms_mlp: float32 [], replicated
The draws below stay inside these ranges and needn't reach their ends.
Inputs may be any that keep to these rules, and one draw needn't show every extreme that they name: `segment`: within each slot the clip numbers never fall; clip 1 starts before position 128 of the slot and clip 2 starts at or after position 1921.
All inputs are finite; a program needn't handle non-finite values.
Results may differ from the reference program's by a relative error of at most 0.022.
Values may be sent and summed in bfloat16 or wider, within the bound.
A program may use at most 512 MiB of HBM per device.

```python
import jax
import jax.numpy as jnp
from jax import lax

D = 2048
HEADS = 16
HD = 128
FF = 8192
TOK_DEV = 256
SEQ = 2048
TOKENS = 8192
N_DP = 4


def draw_segment(key, part):
    first_key, second_key = jax.random.split(key)
    groups = TOKENS // SEQ
    opening = jax.random.randint(first_key, (groups, 1), 1, TOK_DEV // 2)
    closing = jax.random.randint(second_key, (groups, 1), SEQ - TOK_DEV // 2 + 1, SEQ)
    position = jnp.arange(SEQ, dtype=jnp.int32)[None, :]
    numbers = (position >= opening).astype(jnp.int32) + (position >= closing).astype(jnp.int32)
    return numbers.reshape(TOKENS)


def draw_valid(key, part):
    position = jnp.arange(TOKENS, dtype=jnp.int32)
    threshold = 30 + 65 * position // max(TOKENS - 1, 1)
    ticket = jax.random.randint(key, (TOKENS,), 0, 100)
    return (ticket < threshold).astype(jnp.int32)


def levels(own_key, dims, cuts, least, high):
    factor_of = 1.0
    for dim, blocks in cuts:
        heights = jax.random.uniform(jax.random.fold_in(jax.random.fold_in(own_key, 6), dim), (blocks,), jnp.float32, least / len(cuts), high / len(cuts))
        factor_of = factor_of * jnp.repeat(jnp.exp(heights), dims[dim] // blocks).reshape((-1,) + (1,) * (len(dims) - 1 - dim))
    return factor_of


def normal_values(rng, dims, deviation, most, pieces=(), kind=jnp.bfloat16):
    values = deviation * jax.random.normal(rng, dims, jnp.float32)
    if pieces:
        values = values * levels(rng, dims, pieces, -0.22, 0.18)
    return jnp.clip(values, -most, most).astype(kind)


def setup_inputs(seed: int = 0) -> dict:
    seeds = jax.random.split(jax.random.key(seed), 13)
    tokens = normal_values(seeds[0], (TOKENS, D), 1.0, 6.0, ((0, 32),))
    segment = draw_segment(jax.random.fold_in(seeds[12], 71), 0)
    valid = draw_valid(jax.random.fold_in(seeds[12], 71), 0)
    gain_attn = jnp.clip(1.0 + 0.1 * jax.random.normal(seeds[3], (D,), jnp.float32), 0.5, 1.5)
    w_query = normal_values(seeds[4], (D, D), D ** -0.5, 0.125, ((1, 8),))
    w_key = normal_values(seeds[5], (D, D), D ** -0.5, 0.125, ((1, 8),))
    w_value = normal_values(seeds[6], (D, D), D ** -0.5, 0.125, ((1, 8),))
    w_out = normal_values(seeds[7], (D, D), (max(1, 4 * D // SEQ)) ** -0.5, 3.0, ((0, 8),))
    gain_mlp = jnp.clip(1.0 + 0.1 * jax.random.normal(seeds[8], (D,), jnp.float32), 0.5, 1.5)
    w_up = normal_values(seeds[9], (D, FF), D ** -0.5, 0.125, ((1, 8),))
    w_down = normal_values(seeds[10], (FF, D), FF ** -0.5, 0.0625, ((0, 8),))
    grad_out = normal_values(seeds[11], (TOKENS, D), 1.0, 6.0, ((0, 32),))
    return dict(tokens=tokens, segment=segment, valid=valid, gain_attn=gain_attn, w_query=w_query, w_key=w_key, w_value=w_value, w_out=w_out, gain_mlp=gain_mlp, w_up=w_up, w_down=w_down, grad_out=grad_out)


@jax.custom_vjp
def low(v):
    return lax.optimization_barrier(v.astype(jnp.bfloat16)).astype(jnp.float32)

@jax.custom_vjp
def low_back(v):
    return v

def low_keep(v):
    return (low(v), None)

def low_pass(kept, grad):
    return (grad,)

def back_keep(v):
    return (v, None)

def back_low(kept, grad):
    return (low(grad),)
low.defvjp(low_keep, low_pass)
low_back.defvjp(back_keep, back_low)
EPSILON = 1e-05
NEGATIVE = -1e+30
HIGHEST = lax.Precision.HIGHEST

def norm_rows(values, norm_gain):
    scale = lax.rsqrt(lax.optimization_barrier(jnp.mean(values * values, axis=-1, keepdims=True)) + EPSILON)
    return values * scale * norm_gain

def block_mask(first_row, row_count, segment_rows, valid_rows):
    rows_here = first_row + jnp.arange(row_count, dtype=jnp.int32)
    columns = jnp.arange(segment_rows.shape[0], dtype=jnp.int32)
    segment_here = lax.dynamic_slice_in_dim(segment_rows, first_row, row_count)
    same_clip = segment_here[:, None] == segment_rows[None, :]
    earlier = (columns[None, :] < rows_here[:, None]) & (valid_rows[None, :] > 0)
    itself = columns[None, :] == rows_here[:, None]
    return same_clip & (earlier | itself)

def forward(inputs, weights, segment_rows, valid_rows):
    gain_attn, w_query, w_key, w_value, w_out, gain_mlp, w_up, w_down = weights
    normed_attn = low(norm_rows(inputs, gain_attn))

    def project(matrix):
        return low_back(low(jnp.dot(normed_attn, matrix, precision=HIGHEST))).reshape(SEQ, HEADS, HD)
    queries = project(w_query)
    keys_all = project(w_key)
    values_all = project(w_value)
    block_rows = min(512, SEQ)

    def one_block(first_row):
        query_block = lax.dynamic_slice_in_dim(queries, first_row, block_rows, 0)
        scores = low_back(jnp.einsum('qhd,khd->hqk', query_block, keys_all, precision=HIGHEST) * HD ** (-0.5))
        allowed = block_mask(first_row, block_rows, segment_rows, valid_rows)
        scores = jnp.where(allowed[None], scores, NEGATIVE)
        largest = lax.optimization_barrier(jnp.max(scores, axis=-1, keepdims=True))
        powers = jnp.exp(scores - largest)
        attention = powers / lax.optimization_barrier(jnp.sum(powers, axis=-1, keepdims=True))
        return jnp.einsum('hqk,khd->qhd', low(attention), values_all, precision=HIGHEST)
    starts = jnp.arange(SEQ // block_rows, dtype=jnp.int32) * block_rows
    mixed = lax.map(jax.checkpoint(one_block), starts).reshape(SEQ, D)
    mixed = low_back(low(mixed))
    attn_branch = low_back(jnp.dot(mixed, w_out, precision=HIGHEST))
    residual = inputs + attn_branch
    normed_mlp = low(norm_rows(residual, gain_mlp))
    hidden_pre = low_back(jnp.dot(normed_mlp, w_up, precision=HIGHEST))
    hidden = low(jax.nn.gelu(hidden_pre, approximate=True))
    mlp_branch = low_back(jnp.dot(hidden, w_down, precision=HIGHEST))
    return (residual + mlp_branch, (attn_branch, mlp_branch))

def reference(tokens, segment, valid, gain_attn, w_query, w_key, w_value, w_out, gain_mlp, w_up, w_down, grad_out):
    parameters = tuple((matrix.astype(jnp.float32) for matrix in (gain_attn, w_query, w_key, w_value, w_out, gain_mlp, w_up, w_down)))
    token_groups = tokens.astype(jnp.float32).reshape(N_DP, SEQ, D)
    grad_groups = grad_out.astype(jnp.float32).reshape(N_DP, SEQ, D)
    segment_groups = segment.reshape(N_DP, SEQ)
    valid_groups = valid.reshape(N_DP, SEQ)

    def one_group(running, group_item):
        token_rows, grad_rows, segment_rows, valid_rows = group_item

        def layer(inputs, *weights):
            return forward(inputs, weights, segment_rows, valid_rows)
        stream, backward, branches = jax.vjp(layer, token_rows, *parameters, has_aux=True)
        gradients = backward(grad_rows)
        mask_rows = valid_rows.astype(jnp.float32)[:, None]
        squares = (jnp.sum(mask_rows * stream * stream), jnp.sum(mask_rows * branches[0] * branches[0]), jnp.sum(mask_rows * branches[1] * branches[1]))
        new_grads = tuple((earlier + latest for earlier, latest in zip(running[0], gradients[1:])))
        new_squares = tuple((earlier + latest for earlier, latest in zip(running[1], squares)))
        return ((new_grads, new_squares), (stream.astype(jnp.bfloat16), gradients[0].astype(jnp.bfloat16)))
    start_grads = tuple((jnp.zeros_like(matrix) for matrix in parameters))
    start_squares = (jnp.zeros((), jnp.float32), jnp.zeros((), jnp.float32), jnp.zeros((), jnp.float32))
    (weight_grads, squares), (streams, input_grads) = lax.scan(one_group, (start_grads, start_squares), (token_groups, grad_groups, segment_groups, valid_groups))
    counted = jnp.maximum(jnp.sum(valid).astype(jnp.float32) * D, 1.0)
    return (streams.reshape(TOKENS, D), input_grads.reshape(TOKENS, D), weight_grads[0], weight_grads[1], weight_grads[2], weight_grads[3], weight_grads[4], weight_grads[5], weight_grads[6], weight_grads[7], jnp.sqrt(squares[0] / counted), jnp.sqrt(squares[1] / counted), jnp.sqrt(squares[2] / counted))
```

```python
import functools
import jax, jax.numpy as jnp
from jax import lax
from jax.experimental import pallas as pl
from jax.experimental.pallas import tpu as pltpu
HD=128
NEGATIVE=-1e30
LOG2E=1.4426950408889634

def attn_fwd_body(blk, nb, order_ref, q_ref, k_ref, v_ref, rk_ref, ck_ref, mix_ref, lse_ref, ks, vs):
    c = HD ** -0.5 * LOG2E
    for a in range(nb):
        pos = pl.multiple_of(order_ref[a] * blk, blk)
        ks[a*blk:(a+1)*blk, :] = k_ref[pl.ds(pos, blk), :]
        vs[a*blk:(a+1)*blk, :] = v_ref[pl.ds(pos, blk), :]
    tri_r = lax.broadcasted_iota(jnp.int32, (blk, blk), 0)
    tri_c = lax.broadcasted_iota(jnp.int32, (blk, blk), 1)
    for a in range(nb):
        L = (a+1)*blk
        pos = pl.multiple_of(order_ref[a] * blk, blk)
        q = q_ref[pl.ds(pos, blk), :]
        s = lax.dot_general(q, ks[:L, :], (((1,), (1,)), ((), ())), preferred_element_type=jnp.float32)
        rk = rk_ref[a*blk:(a+1)*blk, :]
        ck = ck_ref[:, :L]
        ok = rk == ck
        sd = s[:, L-blk:]
        okd = ok[:, L-blk:]
        okd = (okd & (tri_c < tri_r)) | (tri_c == tri_r)
        sd = jnp.where(okd, sd, NEGATIVE)
        if a:
            so = jnp.where(ok[:, :L-blk], s[:, :L-blk], NEGATIVE)
            m = jnp.maximum(jnp.max(so, axis=1, keepdims=True), jnp.max(sd, axis=1, keepdims=True))
            po = jnp.exp2((so - m) * c)
            pd = jnp.exp2((sd - m) * c)
            l = jnp.sum(po, axis=1, keepdims=True) + jnp.sum(pd, axis=1, keepdims=True)
            o = jnp.dot(po.astype(jnp.bfloat16), vs[:L-blk, :], preferred_element_type=jnp.float32) + jnp.dot(pd.astype(jnp.bfloat16), vs[L-blk:L, :], preferred_element_type=jnp.float32)
        else:
            m = jnp.max(sd, axis=1, keepdims=True)
            pd = jnp.exp2((sd - m) * c)
            l = jnp.sum(pd, axis=1, keepdims=True)
            o = jnp.dot(pd.astype(jnp.bfloat16), vs[L-blk:L, :], preferred_element_type=jnp.float32)
        o = o / l
        mix_ref[pl.ds(pos, blk), :] = o.astype(jnp.bfloat16)
        lse_ref[0, a*blk:(a+1)*blk, :] = m * c + jnp.log2(l)

def attn_fwd(qkv, order, rowkey, colkey, heads, blk=256):
    S = qkv.shape[0]; nb = S // blk
    return pl.pallas_call(
        functools.partial(attn_fwd_body, blk, nb), name="attn_fwd",
        grid_spec=pltpu.PrefetchScalarGridSpec(num_scalar_prefetch=1, grid=(heads,),
            in_specs=[pl.BlockSpec((S, HD), lambda h, o: (0, h)),
                      pl.BlockSpec((S, HD), lambda h, o: (0, heads + h)),
                      pl.BlockSpec((S, HD), lambda h, o: (0, 2*heads + h)),
                      pl.BlockSpec((S, 1), lambda h, o: (0, 0)),
                      pl.BlockSpec((1, S), lambda h, o: (0, 0))],
            out_specs=[pl.BlockSpec((S, HD), lambda h, o: (0, h)),
                       pl.BlockSpec((1, S, 1), lambda h, o: (h, 0, 0))],
            scratch_shapes=[pltpu.VMEM((S, HD), jnp.bfloat16)]*2),
        out_shape=[jax.ShapeDtypeStruct((S, heads*HD), jnp.bfloat16), jax.ShapeDtypeStruct((heads, S, 1), jnp.float32)],
        compiler_params=pltpu.CompilerParams(vmem_limit_bytes=40*2**20),
        cost_estimate=pl.CostEstimate(flops=4*S*S*HD*heads//2, bytes_accessed=8*S*HD*heads, transcendentals=S*S*heads//2),
    )(order, qkv, qkv, qkv, rowkey, colkey)

def attn_bwd_body(blk, nb, order_ref, q_ref, k_ref, v_ref, do_ref, mix_ref, lse_ref, rk_ref, ck_ref, dq_ref, dk_ref, dv_ref, ks, vs, dks, dvs):
    scale = HD ** -0.5
    c = scale * LOG2E
    for a in range(nb):
        pos = pl.multiple_of(order_ref[a] * blk, blk)
        ks[a*blk:(a+1)*blk, :] = k_ref[pl.ds(pos, blk), :]
        vs[a*blk:(a+1)*blk, :] = v_ref[pl.ds(pos, blk), :]
    tri_r = lax.broadcasted_iota(jnp.int32, (blk, blk), 0)
    tri_c = lax.broadcasted_iota(jnp.int32, (blk, blk), 1)
    nt = (((1,), (1,)), ((), ()))
    tn = (((0,), (0,)), ((), ()))
    f32 = jnp.float32
    for a in reversed(range(nb)):
        L = (a+1)*blk; Lo = L - blk
        pos = pl.multiple_of(order_ref[a] * blk, blk)
        q = q_ref[pl.ds(pos, blk), :]
        do = do_ref[pl.ds(pos, blk), :]
        delta = jnp.sum(do.astype(f32) * mix_ref[pl.ds(pos, blk), :].astype(f32), axis=1, keepdims=True)
        s = lax.dot_general(q, ks[:L, :], nt, preferred_element_type=f32)
        dp = lax.dot_general(do, vs[:L, :], nt, preferred_element_type=f32)
        rk = rk_ref[a*blk:(a+1)*blk, :]
        ck = ck_ref[:, :L]
        ok = rk == ck
        lse = lse_ref[0, a*blk:(a+1)*blk, :]
        okd = (ok[:, Lo:] & (tri_c < tri_r)) | (tri_c == tri_r)
        p = jnp.exp2(s * c - lse)
        pd = jnp.where(okd, p[:, Lo:], 0.0)
        dsd = (pd * (dp[:, Lo:] - delta)).astype(jnp.bfloat16)
        pd = pd.astype(jnp.bfloat16)
        dq = jnp.dot(dsd, ks[Lo:L, :], preferred_element_type=f32)
        dkd = lax.dot_general(dsd, q, tn, preferred_element_type=f32)
        dvd = lax.dot_general(pd, do, tn, preferred_element_type=f32)
        if a == nb - 1:
            dks[Lo:L, :] = dkd
            dvs[Lo:L, :] = dvd
        else:
            dks[Lo:L, :] += dkd
            dvs[Lo:L, :] += dvd
        if a:
            po = jnp.where(ok[:, :Lo], p[:, :Lo], 0.0)
            dso = (po * (dp[:, :Lo] - delta)).astype(jnp.bfloat16)
            po = po.astype(jnp.bfloat16)
            dq += jnp.dot(dso, ks[:Lo, :], preferred_element_type=f32)
            dko = lax.dot_general(dso, q, tn, preferred_element_type=f32)
            dvo = lax.dot_general(po, do, tn, preferred_element_type=f32)
            if a == nb - 1:
                dks[:Lo, :] = dko
                dvs[:Lo, :] = dvo
            else:
                dks[:Lo, :] += dko
                dvs[:Lo, :] += dvo
        dq_ref[pl.ds(pos, blk), :] = (dq * scale).astype(jnp.bfloat16)
    for a in range(nb):
        pos = pl.multiple_of(order_ref[a] * blk, blk)
        dk_ref[pl.ds(pos, blk), :] = (dks[a*blk:(a+1)*blk, :] * scale).astype(jnp.bfloat16)
        dv_ref[pl.ds(pos, blk), :] = dvs[a*blk:(a+1)*blk, :].astype(jnp.bfloat16)

def attn_bwd(qkv, do, mixed, lse, order, rowkey, colkey, heads, blk=256):
    S = qkv.shape[0]; nb = S // blk
    bs = lambda off: pl.BlockSpec((S, HD), lambda h, o: (0, off*heads + h))
    return pl.pallas_call(
        functools.partial(attn_bwd_body, blk, nb), name="attn_bwd",
        grid_spec=pltpu.PrefetchScalarGridSpec(num_scalar_prefetch=1, grid=(heads,),
            in_specs=[bs(0), bs(1), bs(2), bs(0), bs(0),
                      pl.BlockSpec((1, S, 1), lambda h, o: (h, 0, 0)),
                      pl.BlockSpec((S, 1), lambda h, o: (0, 0)),
                      pl.BlockSpec((1, S), lambda h, o: (0, 0))],
            out_specs=[bs(0), bs(0), bs(0)],
            scratch_shapes=[pltpu.VMEM((S, HD), jnp.bfloat16)]*2 + [pltpu.VMEM((S, HD), jnp.float32)]*2),
        out_shape=[jax.ShapeDtypeStruct((S, heads*HD), jnp.bfloat16)]*3,
        compiler_params=pltpu.CompilerParams(vmem_limit_bytes=48*2**20),
        cost_estimate=pl.CostEstimate(flops=10*S*S*HD*heads//2, bytes_accessed=16*S*HD*heads, transcendentals=S*S*heads//2),
    )(order, qkv, qkv, qkv, do, mixed, lse, rowkey, colkey)

from jax.sharding import PartitionSpec as P

EPSILON = 1e-05
BF = jnp.bfloat16
F32 = jnp.float32


def row_scale(values):
    return lax.rsqrt(jnp.mean(values * values, axis=-1, keepdims=True) + EPSILON)


def norm_rows(values, norm_gain):
    return values * row_scale(values) * norm_gain


def norm_back(values, norm_gain, grad_norm):
    scale = row_scale(values)
    normal = values * scale
    grad_hat = grad_norm * norm_gain
    inner = jnp.mean(grad_hat * normal, axis=-1, keepdims=True)
    return scale * (grad_hat - normal * inner)


def gelu_fn(values):
    return jax.nn.gelu(values, approximate=True)


def dot_nn(a, b):
    return jnp.dot(a, b, preferred_element_type=F32)


def dot_tn(a, b):
    return lax.dot_general(a, b, (((0,), (0,)), ((), ())), preferred_element_type=F32)


def dot_nt(a, b):
    return lax.dot_general(a, b, (((1,), (1,)), ((), ())), preferred_element_type=F32)


def after(value, *others):
    return lax.optimization_barrier((value,) + others)[0]


def swap_bits(r):
    return (r & 1) | ((r & 2) << 1) | ((r & 4) >> 1)


class Cube:
    def __init__(self, me):
        self.me = me
        self.core = me % 2
        self.sib = [(i, i ^ 1) for i in range(8)]
        self.first = [(i, i ^ (2 if i % 2 else 4)) for i in range(8)]
        self.second = [(i, i ^ (4 if i % 2 else 2)) for i in range(8)]
        mask = jnp.bitwise_xor(jnp.arange(8, dtype=jnp.int32), me)
        swapped = (mask & 1) | ((mask & 2) << 1) | ((mask & 4) >> 1)
        self.order = jnp.where(self.core == 0, mask, swapped).astype(jnp.int32)

    def gather(self, own):
        half = own.shape[0] // 2
        send = lambda v, p: lax.ppermute(v, "mp", p)
        p4, p2, p1 = send(own, self.first), send(own, self.second), send(own, self.sib)
        p6 = jnp.concatenate([send(p2[:half], self.first), send(p4[half:], self.second)])
        p5, p3 = send(p2, self.sib), send(p4, self.sib)
        p7 = send(p6, self.sib)
        return [[own, p1], [p2, p3], [p4, p5], [p6, p7]]

    def scatter(self, product, width, chunks):
        half = width // 2
        step = half // chunks
        core = self.core
        send = lambda v, p: lax.ppermute(v, "mp", p)
        mine, other = [], []
        for j in range(chunks):
            away = product((1 - core) * half + j * step, step).astype(BF)
            came = send(away, self.sib)
            keep = product(core * half + j * step, step)
            rows = keep.shape[0] // 8
            cut = lambda v, a, b: v[a * rows:b * rows].astype(F32)
            came = jnp.concatenate([came[k * rows:(k + 1) * rows] for k in (1, 0, 5, 4, 3, 2, 7, 6)])
            one = send((cut(keep, 4, 8) + cut(came, 4, 8)).astype(BF), self.first)
            two = send((cut(keep, 2, 4) + cut(came, 2, 4) + cut(one, 2, 4)).astype(BF), self.second)
            total = cut(keep, 0, 2) + cut(came, 0, 2) + cut(one, 0, 2) + cut(two, 0, 2)
            mine.append(total[:rows])
            other.append(send(total[rows:].astype(BF), self.sib).astype(F32))
        mine, other = jnp.concatenate(mine, 1), jnp.concatenate(other, 1)
        low = jnp.where(core == 0, mine, other)
        high = jnp.where(core == 0, other, mine)
        return jnp.concatenate([low, high], 1)

    def total(self, vector):
        send = lambda v, axis, n, bit: lax.ppermute(v, axis, [(i, i ^ bit) for i in range(n)])
        for bit in (1, 2, 4):
            vector = vector + send(vector, "mp", 8, bit)
        n_dp = lax.axis_size("dp")
        bit = 1
        while bit < n_dp:
            vector = vector + send(vector, "dp", n_dp, bit)
            bit *= 2
        return vector


class Plain:
    def __init__(self, me, count):
        self.order = jnp.arange(count, dtype=jnp.int32)

    def gather(self, own):
        return [[lax.all_gather(own, "mp", axis=0, tiled=True)]]

    def scatter(self, product, width, chunks):
        return lax.psum_scatter(product(0, width).astype(BF), "mp", scatter_dimension=0, tiled=True).astype(F32)

    def total(self, vector):
        return lax.psum(vector, ("dp", "mp"))


def take(array, start, size, axis):
    if size == array.shape[axis]:
        return array
    return lax.dynamic_slice_in_dim(array, start, size, axis)


def stack(groups):
    flat = [block for group in groups for block in group]
    return jnp.concatenate(flat) if len(flat) > 1 else flat[0]


def joined(group):
    return jnp.concatenate(group) if len(group) > 1 else group[0]


def on_device(tokens, segment, valid, gain_attn, w_query, w_key, w_value, w_out, gain_mlp, w_up, w_down, grad_out):
    own_rows, width = tokens.shape
    seq_rows = segment.shape[0]
    heads = w_query.shape[1] // HD
    n_dp, n_mp = lax.axis_size("dp"), lax.axis_size("mp")
    dp, me = lax.axis_index("dp"), lax.axis_index("mp")
    net = Cube(me) if n_mp == 8 and n_dp & (n_dp - 1) == 0 else Plain(me, seq_rows // own_rows)
    chunks = 2
    valid_group = lax.dynamic_slice_in_dim(valid, dp * seq_rows, seq_rows)
    valid_own = lax.dynamic_slice_in_dim(valid_group, me * own_rows, own_rows)
    row_key = segment[:, None]
    col_key = jnp.where(valid_group > 0, segment, -1)[None, :]
    tokens32 = tokens.astype(F32)
    w_qkv = jnp.concatenate([w_query, w_key, w_value], 1)

    normed_groups = net.gather(norm_rows(tokens32, gain_attn).astype(BF))
    qkv = joined([dot_nn(joined(g), w_qkv).astype(BF) for g in normed_groups])
    normed = stack(normed_groups)

    mixed, lse = attn_fwd(qkv, net.order, row_key, col_key, heads, own_rows)
    grad_groups = net.gather(after(grad_out, qkv))
    attn_own = net.scatter(lambda a, n: dot_nn(mixed, take(w_out, a, n, 1)), width, chunks)
    residual = tokens32 + attn_own
    mlp_groups = net.gather(norm_rows(residual, gain_mlp).astype(BF))

    hidden, grad_pre = [], []
    for group, grads in zip(mlp_groups, grad_groups):
        pre = dot_nn(joined(group), w_up)
        grad_hidden = dot_nt(joined(grads), w_down)
        value, back = jax.vjp(gelu_fn, pre)
        hidden.append(value.astype(BF))
        grad_pre.append(back(grad_hidden)[0].astype(BF))
    hidden, grad_pre = joined(hidden), joined(grad_pre)
    normed_mlp, grad_rows = stack(mlp_groups), stack(grad_groups)

    grad_down = lax.psum_scatter(dot_tn(hidden, grad_rows).astype(BF), "dp", scatter_dimension=1, tiled=True).astype(F32)
    grad_normed = net.scatter(lambda a, n: dot_nt(grad_pre, take(w_up, a, n, 0)), width, chunks)
    part_up = dot_tn(normed_mlp, grad_pre)
    grad_up = lax.psum_scatter(part_up.astype(BF), "dp", scatter_dimension=0, tiled=True).astype(F32)
    gain_mlp_part = jnp.sum(part_up * w_up.astype(F32), axis=1) / gain_mlp

    grad_residual = grad_out.astype(F32) + norm_back(residual, gain_mlp, grad_normed)
    branch_groups = net.gather(grad_residual.astype(BF))
    grad_mixed = joined([dot_nt(joined(g), w_out).astype(BF) for g in branch_groups])
    grad_branch = stack(branch_groups)
    grad_out_proj = lax.psum_scatter(
        dot_tn(mixed, grad_branch).astype(BF), "dp", scatter_dimension=1, tiled=True
    ).astype(F32)
    late_hidden = after(hidden, grad_mixed)
    mlp_own = net.scatter(lambda a, n: dot_nn(late_hidden, take(w_down, a, n, 1)), width, chunks)
    stream = residual + mlp_own
    mask_own = valid_own.astype(F32)[:, None]

    grads_qkv = jnp.concatenate(
        attn_bwd(qkv, grad_mixed, mixed, lse, net.order, row_key, col_key, heads, own_rows), 1
    )
    part_qkv = dot_tn(normed, grads_qkv)
    grad_qkv = lax.psum_scatter(part_qkv.astype(BF), "dp", scatter_dimension=0, tiled=True).astype(F32)
    gain_attn_part = jnp.sum(part_qkv * w_qkv.astype(F32), axis=1) / gain_attn
    grad_normed_attn = net.scatter(lambda a, n: dot_nt(grads_qkv, take(w_qkv, a, n, 0)), width, chunks)
    grad_tokens = (grad_residual + norm_back(tokens32, gain_attn, grad_normed_attn)).astype(BF)

    squares = jnp.stack([jnp.sum(mask_own * part * part) for part in (stream, attn_own, mlp_own)])
    summed = net.total(jnp.concatenate([gain_attn_part, gain_mlp_part, squares]))
    counted = jnp.maximum(jnp.sum(valid).astype(F32) * width, 1.0)
    gain_rows = width // (n_dp * n_mp)
    place = (dp * n_mp + me) * gain_rows
    rms = jnp.sqrt(summed[2 * width:] / counted)
    shard = heads * HD
    return (
        stream.astype(BF),
        grad_tokens,
        lax.dynamic_slice_in_dim(summed[:width], place, gain_rows),
        grad_qkv[:, :shard],
        grad_qkv[:, shard:2 * shard],
        grad_qkv[:, 2 * shard:],
        grad_out_proj,
        lax.dynamic_slice_in_dim(summed[width:2 * width], place, gain_rows),
        grad_up,
        grad_down,
        rms[0],
        rms[1],
        rms[2],
    )


def solution(mesh):
    tokens_spec = P(("dp", "mp"), None)
    cols, rows = P(None, "mp"), P("mp", None)
    return jax.shard_map(
        on_device,
        mesh=mesh,
        in_specs=(tokens_spec, P("dp"), P(), P(), cols, cols, cols, rows, P(), cols, rows, tokens_spec),
        out_specs=(
            tokens_spec,
            tokens_spec,
            P(("dp", "mp")),
            P("dp", "mp"),
            P("dp", "mp"),
            P("dp", "mp"),
            P("mp", "dp"),
            P(("dp", "mp")),
            P("dp", "mp"),
            P("mp", "dp"),
            P(),
            P(),
            P(),
        ),
        check_vma=False,
    )
```

```python
import functools
import jax, jax.numpy as jnp
from jax import lax
from jax.experimental import pallas as pl
from jax.experimental.pallas import tpu as pltpu
HD=128
NEGATIVE=-1e30
LOG2E=1.4426950408889634

def attn_fwd_body(blk, nb, order_ref, q_ref, k_ref, v_ref, rk_ref, ck_ref, mix_ref, lse_ref, ks, vs):
    c = HD ** -0.5 * LOG2E
    for a in range(nb):
        pos = pl.multiple_of(order_ref[a] * blk, blk)
        ks[a*blk:(a+1)*blk, :] = k_ref[pl.ds(pos, blk), :]
        vs[a*blk:(a+1)*blk, :] = v_ref[pl.ds(pos, blk), :]
    tri_r = lax.broadcasted_iota(jnp.int32, (blk, blk), 0)
    tri_c = lax.broadcasted_iota(jnp.int32, (blk, blk), 1)
    for a in range(nb):
        L = (a+1)*blk
        pos = pl.multiple_of(order_ref[a] * blk, blk)
        q = q_ref[pl.ds(pos, blk), :]
        s = lax.dot_general(q, ks[:L, :], (((1,), (1,)), ((), ())), preferred_element_type=jnp.float32)
        rk = rk_ref[a*blk:(a+1)*blk, :]
        ck = ck_ref[:, :L]
        ok = rk == ck
        sd = s[:, L-blk:]
        okd = ok[:, L-blk:]
        okd = (okd & (tri_c < tri_r)) | (tri_c == tri_r)
        sd = jnp.where(okd, sd, NEGATIVE)
        if a:
            so = jnp.where(ok[:, :L-blk], s[:, :L-blk], NEGATIVE)
            m = jnp.maximum(jnp.max(so, axis=1, keepdims=True), jnp.max(sd, axis=1, keepdims=True))
            po = jnp.exp2((so - m) * c)
            pd = jnp.exp2((sd - m) * c)
            l = jnp.sum(po, axis=1, keepdims=True) + jnp.sum(pd, axis=1, keepdims=True)
            o = jnp.dot(po.astype(jnp.bfloat16), vs[:L-blk, :], preferred_element_type=jnp.float32) + jnp.dot(pd.astype(jnp.bfloat16), vs[L-blk:L, :], preferred_element_type=jnp.float32)
        else:
            m = jnp.max(sd, axis=1, keepdims=True)
            pd = jnp.exp2((sd - m) * c)
            l = jnp.sum(pd, axis=1, keepdims=True)
            o = jnp.dot(pd.astype(jnp.bfloat16), vs[L-blk:L, :], preferred_element_type=jnp.float32)
        o = o / l
        mix_ref[pl.ds(pos, blk), :] = o.astype(jnp.bfloat16)
        lse_ref[0, a*blk:(a+1)*blk, :] = m * c + jnp.log2(l)

def attn_fwd(qkv, order, rowkey, colkey, heads, blk=256):
    S = qkv.shape[0]; nb = S // blk
    return pl.pallas_call(
        functools.partial(attn_fwd_body, blk, nb), name="attn_fwd",
        grid_spec=pltpu.PrefetchScalarGridSpec(num_scalar_prefetch=1, grid=(heads,),
            in_specs=[pl.BlockSpec((S, HD), lambda h, o: (0, h)),
                      pl.BlockSpec((S, HD), lambda h, o: (0, heads + h)),
                      pl.BlockSpec((S, HD), lambda h, o: (0, 2*heads + h)),
                      pl.BlockSpec((S, 1), lambda h, o: (0, 0)),
                      pl.BlockSpec((1, S), lambda h, o: (0, 0))],
            out_specs=[pl.BlockSpec((S, HD), lambda h, o: (0, h)),
                       pl.BlockSpec((1, S, 1), lambda h, o: (h, 0, 0))],
            scratch_shapes=[pltpu.VMEM((S, HD), jnp.bfloat16)]*2),
        out_shape=[jax.ShapeDtypeStruct((S, heads*HD), jnp.bfloat16), jax.ShapeDtypeStruct((heads, S, 1), jnp.float32)],
        compiler_params=pltpu.CompilerParams(vmem_limit_bytes=40*2**20),
        cost_estimate=pl.CostEstimate(flops=4*S*S*HD*heads//2, bytes_accessed=8*S*HD*heads, transcendentals=S*S*heads//2),
    )(order, qkv, qkv, qkv, rowkey, colkey)

def attn_bwd_body(blk, nb, order_ref, q_ref, k_ref, v_ref, do_ref, mix_ref, lse_ref, rk_ref, ck_ref, dq_ref, dk_ref, dv_ref, ks, vs, dks, dvs):
    scale = HD ** -0.5
    c = scale * LOG2E
    for a in range(nb):
        pos = pl.multiple_of(order_ref[a] * blk, blk)
        ks[a*blk:(a+1)*blk, :] = k_ref[pl.ds(pos, blk), :]
        vs[a*blk:(a+1)*blk, :] = v_ref[pl.ds(pos, blk), :]
    tri_r = lax.broadcasted_iota(jnp.int32, (blk, blk), 0)
    tri_c = lax.broadcasted_iota(jnp.int32, (blk, blk), 1)
    nt = (((1,), (1,)), ((), ()))
    tn = (((0,), (0,)), ((), ()))
    f32 = jnp.float32
    for a in reversed(range(nb)):
        L = (a+1)*blk; Lo = L - blk
        pos = pl.multiple_of(order_ref[a] * blk, blk)
        q = q_ref[pl.ds(pos, blk), :]
        do = do_ref[pl.ds(pos, blk), :]
        delta = jnp.sum(do.astype(f32) * mix_ref[pl.ds(pos, blk), :].astype(f32), axis=1, keepdims=True)
        s = lax.dot_general(q, ks[:L, :], nt, preferred_element_type=f32)
        dp = lax.dot_general(do, vs[:L, :], nt, preferred_element_type=f32)
        rk = rk_ref[a*blk:(a+1)*blk, :]
        ck = ck_ref[:, :L]
        ok = rk == ck
        lse = lse_ref[0, a*blk:(a+1)*blk, :]
        okd = (ok[:, Lo:] & (tri_c < tri_r)) | (tri_c == tri_r)
        p = jnp.exp2(s * c - lse)
        pd = jnp.where(okd, p[:, Lo:], 0.0)
        dsd = (pd * (dp[:, Lo:] - delta)).astype(jnp.bfloat16)
        pd = pd.astype(jnp.bfloat16)
        dq = jnp.dot(dsd, ks[Lo:L, :], preferred_element_type=f32)
        dkd = lax.dot_general(dsd, q, tn, preferred_element_type=f32)
        dvd = lax.dot_general(pd, do, tn, preferred_element_type=f32)
        if a == nb - 1:
            dks[Lo:L, :] = dkd
            dvs[Lo:L, :] = dvd
        else:
            dks[Lo:L, :] += dkd
            dvs[Lo:L, :] += dvd
        if a:
            po = jnp.where(ok[:, :Lo], p[:, :Lo], 0.0)
            dso = (po * (dp[:, :Lo] - delta)).astype(jnp.bfloat16)
            po = po.astype(jnp.bfloat16)
            dq += jnp.dot(dso, ks[:Lo, :], preferred_element_type=f32)
            dko = lax.dot_general(dso, q, tn, preferred_element_type=f32)
            dvo = lax.dot_general(po, do, tn, preferred_element_type=f32)
            if a == nb - 1:
                dks[:Lo, :] = dko
                dvs[:Lo, :] = dvo
            else:
                dks[:Lo, :] += dko
                dvs[:Lo, :] += dvo
        dq_ref[pl.ds(pos, blk), :] = (dq * scale).astype(jnp.bfloat16)
    for a in range(nb):
        pos = pl.multiple_of(order_ref[a] * blk, blk)
        dk_ref[pl.ds(pos, blk), :] = (dks[a*blk:(a+1)*blk, :] * scale).astype(jnp.bfloat16)
        dv_ref[pl.ds(pos, blk), :] = dvs[a*blk:(a+1)*blk, :].astype(jnp.bfloat16)

def attn_bwd(qkv, do, mixed, lse, order, rowkey, colkey, heads, blk=256):
    S = qkv.shape[0]; nb = S // blk
    bs = lambda off: pl.BlockSpec((S, HD), lambda h, o: (0, off*heads + h))
    return pl.pallas_call(
        functools.partial(attn_bwd_body, blk, nb), name="attn_bwd",
        grid_spec=pltpu.PrefetchScalarGridSpec(num_scalar_prefetch=1, grid=(heads,),
            in_specs=[bs(0), bs(1), bs(2), bs(0), bs(0),
                      pl.BlockSpec((1, S, 1), lambda h, o: (h, 0, 0)),
                      pl.BlockSpec((S, 1), lambda h, o: (0, 0)),
                      pl.BlockSpec((1, S), lambda h, o: (0, 0))],
            out_specs=[bs(0), bs(0), bs(0)],
            scratch_shapes=[pltpu.VMEM((S, HD), jnp.bfloat16)]*2 + [pltpu.VMEM((S, HD), jnp.float32)]*2),
        out_shape=[jax.ShapeDtypeStruct((S, heads*HD), jnp.bfloat16)]*3,
        compiler_params=pltpu.CompilerParams(vmem_limit_bytes=48*2**20),
        cost_estimate=pl.CostEstimate(flops=10*S*S*HD*heads//2, bytes_accessed=16*S*HD*heads, transcendentals=S*S*heads//2),
    )(order, qkv, qkv, qkv, do, mixed, lse, rowkey, colkey)

from jax.sharding import PartitionSpec as P

EPSILON = 1e-05
BF = jnp.bfloat16
F32 = jnp.float32


def row_scale(values):
    return lax.rsqrt(jnp.mean(values * values, axis=-1, keepdims=True) + EPSILON)


def norm_rows(values, norm_gain):
    return values * row_scale(values) * norm_gain


def norm_back(values, norm_gain, grad_norm):
    scale = row_scale(values)
    normal = values * scale
    grad_hat = grad_norm * norm_gain
    inner = jnp.mean(grad_hat * normal, axis=-1, keepdims=True)
    return scale * (grad_hat - normal * inner)


def gelu_fn(values):
    return jax.nn.gelu(values, approximate=True)


def dot_nn(a, b):
    return jnp.dot(a, b, preferred_element_type=F32)


def dot_tn(a, b):
    return lax.dot_general(a, b, (((0,), (0,)), ((), ())), preferred_element_type=F32)


def dot_nt(a, b):
    return lax.dot_general(a, b, (((1,), (1,)), ((), ())), preferred_element_type=F32)


def after(value, *others):
    return lax.optimization_barrier((value,) + others)[0]


def swap_bits(r):
    return (r & 1) | ((r & 2) << 1) | ((r & 4) >> 1)


MESH = pl.DeviceIdType.MESH
HBM_SPACE = pl.ANY
VMEM_SPACE = pltpu.VMEM


def neighbours():
    dp, me = lax.axis_index("dp"), lax.axis_index("mp")
    core, along_x, along_y = me % 2, (me // 2) % 2, me // 4
    by_x, by_y = me + 2 - 4 * along_x, me + 4 - 8 * along_y
    first = (1 - core) * by_y + core * by_x
    second = (1 - core) * by_x + core * by_y
    return core, (dp, me + 1 - 2 * core), (dp, first), (dp, second)


def greet(*others):
    barrier = pltpu.get_barrier_semaphore()
    for other in others:
        pl.semaphore_signal(barrier, inc=1, device_id=other, device_id_type=MESH)
    pl.semaphore_wait(barrier, len(others))


class Gather:
    COPIES = 11

    def __init__(self, buf, sends, recvs, sib, first, second):
        rows = buf.shape[1]
        low, high, whole = pl.ds(0, rows // 2), pl.ds(rows // 2, rows // 2), pl.ds(0, rows)

        def copy(i, source, target, part, device):
            return pltpu.make_async_remote_copy(
                src_ref=buf.at[source, part], dst_ref=buf.at[target, part],
                send_sem=sends.at[i], recv_sem=recvs.at[i], device_id=device, device_id_type=MESH,
            )

        self.copies = [
            copy(0, 0, 4, high, first), copy(1, 0, 4, low, first),
            copy(2, 0, 2, low, second), copy(3, 0, 2, high, second),
            copy(4, 0, 1, whole, sib),
            copy(5, 2, 6, low, first), copy(6, 4, 6, high, second),
            copy(7, 4, 3, whole, sib), copy(8, 2, 5, whole, sib),
            copy(9, 6, 7, low, sib), copy(10, 6, 7, high, sib),
        ]

    def start(self):
        for i in (0, 2, 1, 3, 4):
            self.copies[i].start()

    def pair(self):
        self.copies[4].wait_recv()

    def forward(self):
        for arrived, onward in ((2, 5), (0, 6)):
            self.copies[arrived].wait_recv()
            self.copies[onward].start()
        for arrived, onward in ((1, 7), (3, 8)):
            self.copies[arrived].wait_recv()
            self.copies[onward].start()

    def middle(self):
        self.copies[7].wait_recv()
        self.copies[8].wait_recv()

    def finish(self):
        for arrived, onward in ((5, 9), (6, 10)):
            self.copies[arrived].wait_recv()
            self.copies[onward].start()
        self.copies[9].wait_recv()
        self.copies[10].wait_recv()

    def drain(self):
        for one in self.copies:
            one.wait_send()


def norm_store(rows_ref, gain_ref, store, step=32):
    def some(i, carry):
        part = pl.ds(pl.multiple_of(i * step, step), step)
        store(part, norm_rows(rows_ref[part, :].astype(F32), gain_ref[...]).astype(BF))
        return carry

    lax.fori_loop(0, rows_ref.shape[0] // step, some, 0)


def project_body(tok_hbm, gain_ref, wq_hbm, wk_hbm, wv_hbm, qkv_hbm, normed_hbm, tok_ref, w_ref, qkv_ref, buf, sends, recvs, locals_):
    core, sib, first, second = neighbours()
    rows = tok_ref.shape[0]
    width = wq_hbm.shape[1]
    fetch = [pltpu.make_async_copy(tok_hbm, tok_ref, locals_.at[16])]
    for k, w_hbm in enumerate((wq_hbm, wk_hbm, wv_hbm)):
        fetch.append(pltpu.make_async_copy(w_hbm, w_ref.at[:, pl.ds(k * width, width)], locals_.at[17 + k]))
    for one in fetch:
        one.start()
    greet(sib, first, second)
    fetch[0].wait()

    def keep(part, value):
        buf[0, part, :] = value

    norm_store(tok_ref, gain_ref, keep)
    ring = Gather(buf, sends, recvs, sib, first, second)
    ring.start()
    for one in fetch[1:]:
        one.wait()

    def moved(s):
        at = pl.ds(pl.multiple_of(s * rows, rows), rows)
        return (
            pltpu.make_async_copy(buf.at[s], normed_hbm.at[at], locals_.at[s]),
            pltpu.make_async_copy(qkv_ref.at[at], qkv_hbm.at[at], locals_.at[8 + s]),
        )

    def slot(s, carry):
        at = pl.ds(pl.multiple_of(s * rows, rows), rows)
        normed_out, qkv_out = moved(s)
        normed_out.start()
        qkv_ref[at, :] = dot_nn(buf[s], w_ref[...]).astype(BF)
        qkv_out.start()
        return carry

    ring.pair()
    lax.fori_loop(0, 2, slot, 0)
    ring.forward()
    ring.middle()
    lax.fori_loop(2, 6, slot, 0)
    ring.finish()
    lax.fori_loop(6, 8, slot, 0)
    for s in range(8):
        for one in moved(s):
            one.wait()
    ring.drain()


def project(tokens, gain, w_query, w_key, w_value):
    rows, width = tokens.shape
    cols = w_query.shape[1]
    hbm = pl.BlockSpec(memory_space=HBM_SPACE)
    return pl.pallas_call(
        project_body, name="gather_project",
        in_specs=[hbm, pl.BlockSpec(memory_space=VMEM_SPACE), hbm, hbm, hbm],
        out_specs=[hbm, hbm],
        out_shape=[jax.ShapeDtypeStruct((8 * rows, 3 * cols), BF), jax.ShapeDtypeStruct((8 * rows, width), BF)],
        scratch_shapes=[
            pltpu.VMEM((rows, width), BF), pltpu.VMEM((width, 3 * cols), BF), pltpu.VMEM((8 * rows, 3 * cols), BF),
            pltpu.VMEM((8, rows, width), BF), pltpu.SemaphoreType.DMA((11,)), pltpu.SemaphoreType.DMA((11,)),
            pltpu.SemaphoreType.DMA((20,)),
        ],
        compiler_params=pltpu.CompilerParams(collective_id=1, has_side_effects=True, vmem_limit_bytes=58 * 2**20),
        cost_estimate=pl.CostEstimate(flops=2 * 8 * rows * width * 3 * cols, bytes_accessed=60 * 2**20, transcendentals=0),
    )(tokens, gain[None, :], w_query, w_key, w_value)


class Cube:
    def __init__(self, me):
        self.me = me
        self.core = me % 2
        self.sib = [(i, i ^ 1) for i in range(8)]
        self.first = [(i, i ^ (2 if i % 2 else 4)) for i in range(8)]
        self.second = [(i, i ^ (4 if i % 2 else 2)) for i in range(8)]
        mask = jnp.bitwise_xor(jnp.arange(8, dtype=jnp.int32), me)
        swapped = (mask & 1) | ((mask & 2) << 1) | ((mask & 4) >> 1)
        self.order = jnp.where(self.core == 0, mask, swapped).astype(jnp.int32)

    def gather(self, own):
        half = own.shape[0] // 2
        send = lambda v, p: lax.ppermute(v, "mp", p)
        p4, p2, p1 = send(own, self.first), send(own, self.second), send(own, self.sib)
        p6 = jnp.concatenate([send(p2[:half], self.first), send(p4[half:], self.second)])
        p5, p3 = send(p2, self.sib), send(p4, self.sib)
        p7 = send(p6, self.sib)
        return [[own, p1], [p2, p3], [p4, p5], [p6, p7]]

    def scatter(self, product, width, chunks):
        half = width // 2
        step = half // chunks
        core = self.core
        send = lambda v, p: lax.ppermute(v, "mp", p)
        mine, other = [], []
        for j in range(chunks):
            away = product((1 - core) * half + j * step, step).astype(BF)
            came = send(away, self.sib)
            keep = product(core * half + j * step, step)
            rows = keep.shape[0] // 8
            cut = lambda v, a, b: v[a * rows:b * rows].astype(F32)
            came = jnp.concatenate([came[k * rows:(k + 1) * rows] for k in (1, 0, 5, 4, 3, 2, 7, 6)])
            one = send((cut(keep, 4, 8) + cut(came, 4, 8)).astype(BF), self.first)
            two = send((cut(keep, 2, 4) + cut(came, 2, 4) + cut(one, 2, 4)).astype(BF), self.second)
            total = cut(keep, 0, 2) + cut(came, 0, 2) + cut(one, 0, 2) + cut(two, 0, 2)
            mine.append(total[:rows])
            other.append(send(total[rows:].astype(BF), self.sib).astype(F32))
        mine, other = jnp.concatenate(mine, 1), jnp.concatenate(other, 1)
        low = jnp.where(core == 0, mine, other)
        high = jnp.where(core == 0, other, mine)
        return jnp.concatenate([low, high], 1)

    def total(self, vector):
        send = lambda v, axis, n, bit: lax.ppermute(v, axis, [(i, i ^ bit) for i in range(n)])
        for bit in (1, 2, 4):
            vector = vector + send(vector, "mp", 8, bit)
        n_dp = lax.axis_size("dp")
        bit = 1
        while bit < n_dp:
            vector = vector + send(vector, "dp", n_dp, bit)
            bit *= 2
        return vector


class Plain:
    def __init__(self, me, count):
        self.order = jnp.arange(count, dtype=jnp.int32)

    def gather(self, own):
        return [[lax.all_gather(own, "mp", axis=0, tiled=True)]]

    def scatter(self, product, width, chunks):
        return lax.psum_scatter(product(0, width).astype(BF), "mp", scatter_dimension=0, tiled=True).astype(F32)

    def total(self, vector):
        return lax.psum(vector, ("dp", "mp"))


def take(array, start, size, axis):
    if size == array.shape[axis]:
        return array
    return lax.dynamic_slice_in_dim(array, start, size, axis)


def stack(groups):
    flat = [block for group in groups for block in group]
    return jnp.concatenate(flat) if len(flat) > 1 else flat[0]


def joined(group):
    return jnp.concatenate(group) if len(group) > 1 else group[0]


def on_device(tokens, segment, valid, gain_attn, w_query, w_key, w_value, w_out, gain_mlp, w_up, w_down, grad_out):
    own_rows, width = tokens.shape
    seq_rows = segment.shape[0]
    heads = w_query.shape[1] // HD
    n_dp, n_mp = lax.axis_size("dp"), lax.axis_size("mp")
    dp, me = lax.axis_index("dp"), lax.axis_index("mp")
    net = Cube(me) if n_mp == 8 and n_dp & (n_dp - 1) == 0 else Plain(me, seq_rows // own_rows)
    chunks = 2
    valid_group = lax.dynamic_slice_in_dim(valid, dp * seq_rows, seq_rows)
    valid_own = lax.dynamic_slice_in_dim(valid_group, me * own_rows, own_rows)
    row_key = segment[:, None]
    col_key = jnp.where(valid_group > 0, segment, -1)[None, :]
    tokens32 = tokens.astype(F32)
    w_qkv = jnp.concatenate([w_query, w_key, w_value], 1)

    if isinstance(net, Cube):
        qkv, normed = project(tokens, gain_attn, w_query, w_key, w_value)
    else:
        normed_groups = net.gather(norm_rows(tokens32, gain_attn).astype(BF))
        qkv = joined([dot_nn(joined(g), w_qkv).astype(BF) for g in normed_groups])
        normed = stack(normed_groups)

    mixed, lse = attn_fwd(qkv, net.order, row_key, col_key, heads, own_rows)
    grad_groups = net.gather(after(grad_out, qkv))
    attn_own = net.scatter(lambda a, n: dot_nn(mixed, take(w_out, a, n, 1)), width, chunks)
    residual = tokens32 + attn_own
    mlp_groups = net.gather(norm_rows(residual, gain_mlp).astype(BF))

    hidden, grad_pre = [], []
    for group, grads in zip(mlp_groups, grad_groups):
        pre = dot_nn(joined(group), w_up)
        grad_hidden = dot_nt(joined(grads), w_down)
        value, back = jax.vjp(gelu_fn, pre)
        hidden.append(value.astype(BF))
        grad_pre.append(back(grad_hidden)[0].astype(BF))
    hidden, grad_pre = joined(hidden), joined(grad_pre)
    normed_mlp, grad_rows = stack(mlp_groups), stack(grad_groups)

    grad_down = lax.psum_scatter(dot_tn(hidden, grad_rows).astype(BF), "dp", scatter_dimension=1, tiled=True).astype(F32)
    grad_normed = net.scatter(lambda a, n: dot_nt(grad_pre, take(w_up, a, n, 0)), width, chunks)
    part_up = dot_tn(normed_mlp, grad_pre)
    grad_up = lax.psum_scatter(part_up.astype(BF), "dp", scatter_dimension=0, tiled=True).astype(F32)
    gain_mlp_part = jnp.sum(part_up * w_up.astype(F32), axis=1) / gain_mlp

    grad_residual = grad_out.astype(F32) + norm_back(residual, gain_mlp, grad_normed)
    branch_groups = net.gather(grad_residual.astype(BF))
    grad_mixed = joined([dot_nt(joined(g), w_out).astype(BF) for g in branch_groups])
    grad_branch = stack(branch_groups)
    grad_out_proj = lax.psum_scatter(
        dot_tn(mixed, grad_branch).astype(BF), "dp", scatter_dimension=1, tiled=True
    ).astype(F32)
    late_hidden = after(hidden, grad_mixed)
    mlp_own = net.scatter(lambda a, n: dot_nn(late_hidden, take(w_down, a, n, 1)), width, chunks)
    stream = residual + mlp_own
    mask_own = valid_own.astype(F32)[:, None]

    grads_qkv = jnp.concatenate(
        attn_bwd(qkv, grad_mixed, mixed, lse, net.order, row_key, col_key, heads, own_rows), 1
    )
    part_qkv = dot_tn(normed, grads_qkv)
    grad_qkv = lax.psum_scatter(part_qkv.astype(BF), "dp", scatter_dimension=0, tiled=True).astype(F32)
    gain_attn_part = jnp.sum(part_qkv * w_qkv.astype(F32), axis=1) / gain_attn
    grad_normed_attn = net.scatter(lambda a, n: dot_nt(grads_qkv, take(w_qkv, a, n, 0)), width, chunks)
    grad_tokens = (grad_residual + norm_back(tokens32, gain_attn, grad_normed_attn)).astype(BF)

    squares = jnp.stack([jnp.sum(mask_own * part * part) for part in (stream, attn_own, mlp_own)])
    summed = net.total(jnp.concatenate([gain_attn_part, gain_mlp_part, squares]))
    counted = jnp.maximum(jnp.sum(valid).astype(F32) * width, 1.0)
    gain_rows = width // (n_dp * n_mp)
    place = (dp * n_mp + me) * gain_rows
    rms = jnp.sqrt(summed[2 * width:] / counted)
    shard = heads * HD
    return (
        stream.astype(BF),
        grad_tokens,
        lax.dynamic_slice_in_dim(summed[:width], place, gain_rows),
        grad_qkv[:, :shard],
        grad_qkv[:, shard:2 * shard],
        grad_qkv[:, 2 * shard:],
        grad_out_proj,
        lax.dynamic_slice_in_dim(summed[width:2 * width], place, gain_rows),
        grad_up,
        grad_down,
        rms[0],
        rms[1],
        rms[2],
    )


def solution(mesh):
    tokens_spec = P(("dp", "mp"), None)
    cols, rows = P(None, "mp"), P("mp", None)
    return jax.shard_map(
        on_device,
        mesh=mesh,
        in_specs=(tokens_spec, P("dp"), P(), P(), cols, cols, cols, rows, P(), cols, rows, tokens_spec),
        out_specs=(
            tokens_spec,
            tokens_spec,
            P(("dp", "mp")),
            P("dp", "mp"),
            P("dp", "mp"),
            P("dp", "mp"),
            P("mp", "dp"),
            P(("dp", "mp")),
            P("dp", "mp"),
            P("mp", "dp"),
            P(),
            P(),
            P(),
        ),
        check_vma=False,
    )
```

```python
import functools

import jax
import jax.numpy as jnp
from jax import lax
from jax.experimental import pallas as pl
from jax.experimental.pallas import tpu as pltpu
from jax.sharding import PartitionSpec as P

HD = 128
NEGATIVE = -1e30
LOG2E = 1.4426950408889634
EPSILON = 1e-05
BF = jnp.bfloat16
F32 = jnp.float32
MIB = 2**20


def dot_nn(a, b):
    return jnp.dot(a, b, preferred_element_type=F32)


def dot_tn(a, b):
    return lax.dot_general(a, b, (((0,), (0,)), ((), ())), preferred_element_type=F32)


def dot_nt(a, b):
    return lax.dot_general(a, b, (((1,), (1,)), ((), ())), preferred_element_type=F32)


def diagonal(blk):
    rows = lax.broadcasted_iota(jnp.int32, (blk, blk), 0)
    cols = lax.broadcasted_iota(jnp.int32, (blk, blk), 1)
    return cols < rows, cols == rows


def attend_head(blk, count, place, queries, keys, values, rk_ref, ck_ref, put_mixed, put_lse, ks, vs):
    c = HD ** -0.5 * LOG2E
    for a in range(count):
        ks[a * blk:(a + 1) * blk, :] = keys(place(a))
        vs[a * blk:(a + 1) * blk, :] = values(place(a))
    earlier, itself = diagonal(blk)
    for a in range(count):
        end = (a + 1) * blk
        low = end - blk
        s = dot_nt(queries(place(a)), ks[:end, :])
        ok = rk_ref[low:end, :] == ck_ref[:, :end]
        sd = jnp.where((ok[:, low:] & earlier) | itself, s[:, low:], NEGATIVE)
        m = jnp.max(sd, axis=1, keepdims=True)
        if a:
            so = jnp.where(ok[:, :low], s[:, :low], NEGATIVE)
            m = jnp.maximum(m, jnp.max(so, axis=1, keepdims=True))
        pd = jnp.exp2((sd - m) * c)
        total = jnp.sum(pd, axis=1, keepdims=True)
        o = dot_nn(pd.astype(BF), vs[low:end, :])
        if a:
            po = jnp.exp2((so - m) * c)
            total += jnp.sum(po, axis=1, keepdims=True)
            o += dot_nn(po.astype(BF), vs[:low, :])
        put_mixed(place(a), (o / total).astype(BF))
        put_lse(a, m * c + jnp.log2(total))


def attn_fwd_body(blk, count, order_ref, q_ref, k_ref, v_ref, rk_ref, ck_ref, mix_ref, lse_ref, ks, vs):
    def place(a):
        return pl.multiple_of(order_ref[a] * blk, blk)

    def put_mixed(at, value):
        mix_ref[pl.ds(at, blk), :] = value

    def put_lse(a, value):
        lse_ref[0, a * blk:(a + 1) * blk, :] = value

    attend_head(
        blk, count, place, lambda at: q_ref[pl.ds(at, blk), :], lambda at: k_ref[pl.ds(at, blk), :],
        lambda at: v_ref[pl.ds(at, blk), :], rk_ref, ck_ref, put_mixed, put_lse, ks, vs,
    )


def attn_fwd(qkv, order, rowkey, colkey, heads, blk):
    seq = qkv.shape[0]
    part = lambda off: pl.BlockSpec((seq, HD), lambda h, o: (0, off * heads + h))
    return pl.pallas_call(
        functools.partial(attn_fwd_body, blk, seq // blk), name="attn_fwd",
        grid_spec=pltpu.PrefetchScalarGridSpec(
            num_scalar_prefetch=1, grid=(heads,),
            in_specs=[part(0), part(1), part(2), pl.BlockSpec((seq, 1), lambda h, o: (0, 0)),
                      pl.BlockSpec((1, seq), lambda h, o: (0, 0))],
            out_specs=[part(0), pl.BlockSpec((1, seq, 1), lambda h, o: (h, 0, 0))],
            scratch_shapes=[pltpu.VMEM((seq, HD), BF)] * 2),
        out_shape=[jax.ShapeDtypeStruct((seq, heads * HD), BF), jax.ShapeDtypeStruct((heads, seq, 1), F32)],
        compiler_params=pltpu.CompilerParams(vmem_limit_bytes=48 * MIB),
        cost_estimate=pl.CostEstimate(
            flops=2 * seq * seq * HD * heads, bytes_accessed=8 * seq * HD * heads, transcendentals=seq * seq * heads // 2),
    )(order, qkv, qkv, qkv, rowkey, colkey)


def unattend_head(blk, count, place, queries, keys, values, grads, mixes, lses, rk_ref, ck_ref, put_q, put_k, put_v, ks, vs, dks, dvs,
                  between=None):
    scale = HD ** -0.5
    c = scale * LOG2E
    for a in range(count):
        ks[a * blk:(a + 1) * blk, :] = keys(place(a))
        vs[a * blk:(a + 1) * blk, :] = values(place(a))
    earlier, itself = diagonal(blk)

    def add(ref, lo, hi, value, fresh):
        if fresh:
            ref[lo:hi, :] = value
        else:
            ref[lo:hi, :] += value

    for a in reversed(range(count)):
        end = (a + 1) * blk
        low = end - blk
        fresh = a == count - 1
        at = place(a)
        q, do = queries(at), grads(at)
        delta = jnp.sum(do.astype(F32) * mixes(at).astype(F32), axis=1, keepdims=True)
        p = jnp.exp2(dot_nt(q, ks[:end, :]) * c - lses(a))
        dp = dot_nt(do, vs[:end, :])
        ok = rk_ref[low:end, :] == ck_ref[:, :end]
        pd = jnp.where((ok[:, low:] & earlier) | itself, p[:, low:], 0.0)
        dsd = (pd * (dp[:, low:] - delta)).astype(BF)
        dq = dot_nn(dsd, ks[low:end, :])
        add(dks, low, end, dot_tn(dsd, q), fresh)
        add(dvs, low, end, dot_tn(pd.astype(BF), do), fresh)
        if a:
            po = jnp.where(ok[:, :low], p[:, :low], 0.0)
            dso = (po * (dp[:, :low] - delta)).astype(BF)
            dq += dot_nn(dso, ks[:low, :])
            add(dks, 0, low, dot_tn(dso, q), fresh)
            add(dvs, 0, low, dot_tn(po.astype(BF), do), fresh)
        put_q(at, (dq * scale).astype(BF))
        if between is not None:
            between(a)
    for a in range(count):
        put_k(place(a), (dks[a * blk:(a + 1) * blk, :] * scale).astype(BF))
        put_v(place(a), dvs[a * blk:(a + 1) * blk, :].astype(BF))


def attn_bwd_body(blk, count, order_ref, q_ref, k_ref, v_ref, do_ref, mix_ref, lse_ref, rk_ref, ck_ref, dq_ref, dk_ref, dv_ref,
                  ks, vs, dks, dvs):
    def place(a):
        return pl.multiple_of(order_ref[a] * blk, blk)

    def load(ref):
        return lambda at: ref[pl.ds(at, blk), :]

    def save(ref):
        def put(at, value):
            ref[pl.ds(at, blk), :] = value
        return put

    unattend_head(
        blk, count, place, load(q_ref), load(k_ref), load(v_ref), load(do_ref), load(mix_ref),
        lambda a: lse_ref[0, a * blk:(a + 1) * blk, :], rk_ref, ck_ref, save(dq_ref), save(dk_ref), save(dv_ref), ks, vs, dks, dvs,
    )


def attn_bwd(qkv, do, mixed, lse, order, rowkey, colkey, heads, blk):
    seq = qkv.shape[0]
    part = lambda off: pl.BlockSpec((seq, HD), lambda h, o: (0, off * heads + h))
    return pl.pallas_call(
        functools.partial(attn_bwd_body, blk, seq // blk), name="attn_bwd",
        grid_spec=pltpu.PrefetchScalarGridSpec(
            num_scalar_prefetch=1, grid=(heads,),
            in_specs=[part(0), part(1), part(2), part(0), part(0), pl.BlockSpec((1, seq, 1), lambda h, o: (h, 0, 0)),
                      pl.BlockSpec((seq, 1), lambda h, o: (0, 0)), pl.BlockSpec((1, seq), lambda h, o: (0, 0))],
            out_specs=[part(0), part(0), part(0)],
            scratch_shapes=[pltpu.VMEM((seq, HD), BF)] * 2 + [pltpu.VMEM((seq, HD), F32)] * 2),
        out_shape=[jax.ShapeDtypeStruct((seq, heads * HD), BF)] * 3,
        compiler_params=pltpu.CompilerParams(vmem_limit_bytes=56 * MIB),
        cost_estimate=pl.CostEstimate(
            flops=5 * seq * seq * HD * heads, bytes_accessed=16 * seq * HD * heads, transcendentals=seq * seq * heads // 2),
    )(order, qkv, qkv, qkv, do, mixed, lse, rowkey, colkey)


def row_scale(values):
    return lax.rsqrt(jnp.mean(values * values, axis=-1, keepdims=True) + EPSILON)


def norm_rows(values, norm_gain):
    return values * row_scale(values) * norm_gain


def norm_back(values, norm_gain, grad_norm):
    scale = row_scale(values)
    normal = values * scale
    grad_hat = grad_norm * norm_gain
    inner = jnp.mean(grad_hat * normal, axis=-1, keepdims=True)
    return scale * (grad_hat - normal * inner)


def gelu_fn(values):
    return jax.nn.gelu(values, approximate=True)


MESH = pl.DeviceIdType.MESH
HBM_SPACE = pl.ANY
VMEM_SPACE = pltpu.VMEM


def neighbours():
    dp, me = lax.axis_index("dp"), lax.axis_index("mp")
    core, along_x, along_y = me % 2, (me // 2) % 2, me // 4
    by_x, by_y = me + 2 - 4 * along_x, me + 4 - 8 * along_y
    first = (1 - core) * by_y + core * by_x
    second = (1 - core) * by_x + core * by_y
    return core, (dp, me + 1 - 2 * core), (dp, first), (dp, second)


def greet(*others):
    barrier = pltpu.get_barrier_semaphore()
    for other in others:
        pl.semaphore_signal(barrier, inc=1, device_id=other, device_id_type=MESH)
    pl.semaphore_wait(barrier, len(others))


class Gather:
    COPIES = 11

    def __init__(self, buf, sends, recvs, sib, first, second):
        rows = buf.shape[1]
        low, high, whole = pl.ds(0, rows // 2), pl.ds(rows // 2, rows // 2), pl.ds(0, rows)

        def copy(i, source, target, part, device):
            return pltpu.make_async_remote_copy(
                src_ref=buf.at[source, part], dst_ref=buf.at[target, part],
                send_sem=sends.at[i], recv_sem=recvs.at[i], device_id=device, device_id_type=MESH,
            )

        self.copies = [
            copy(0, 0, 4, high, first), copy(1, 0, 4, low, first),
            copy(2, 0, 2, low, second), copy(3, 0, 2, high, second),
            copy(4, 0, 1, whole, sib),
            copy(5, 2, 6, low, first), copy(6, 4, 6, high, second),
            copy(7, 4, 3, whole, sib), copy(8, 2, 5, whole, sib),
            copy(9, 6, 7, low, sib), copy(10, 6, 7, high, sib),
        ]

    def start(self):
        for i in (0, 2, 1, 3, 4):
            self.copies[i].start()

    def pair(self):
        self.copies[4].wait_recv()

    def forward(self):
        for arrived, onward in ((2, 5), (0, 6)):
            self.copies[arrived].wait_recv()
            self.copies[onward].start()
        for arrived, onward in ((1, 7), (3, 8)):
            self.copies[arrived].wait_recv()
            self.copies[onward].start()

    def middle(self):
        self.copies[7].wait_recv()
        self.copies[8].wait_recv()

    def finish(self):
        for arrived, onward in ((5, 9), (6, 10)):
            self.copies[arrived].wait_recv()
            self.copies[onward].start()
        self.copies[9].wait_recv()
        self.copies[10].wait_recv()

    def drain(self):
        for one in self.copies:
            one.wait_send()


def norm_store(rows_ref, gain_ref, store, step=32):
    def some(i, carry):
        part = pl.ds(pl.multiple_of(i * step, step), step)
        store(part, norm_rows(rows_ref[part, :].astype(F32), gain_ref[...]).astype(BF))
        return carry

    lax.fori_loop(0, rows_ref.shape[0] // step, some, 0)


def project_body(tok_hbm, gain_ref, wq_hbm, wk_hbm, wv_hbm, qkv_hbm, normed_hbm, tok_ref, w_ref, qkv_ref, buf, sends, recvs, locals_):
    core, sib, first, second = neighbours()
    rows = tok_ref.shape[0]
    width = wq_hbm.shape[1]
    fetch = [pltpu.make_async_copy(tok_hbm, tok_ref, locals_.at[16])]
    for k, w_hbm in enumerate((wq_hbm, wk_hbm, wv_hbm)):
        fetch.append(pltpu.make_async_copy(w_hbm, w_ref.at[:, pl.ds(k * width, width)], locals_.at[17 + k]))
    for one in fetch:
        one.start()
    greet(sib, first, second)
    fetch[0].wait()

    def keep(part, value):
        buf[0, part, :] = value

    norm_store(tok_ref, gain_ref, keep)
    ring = Gather(buf, sends, recvs, sib, first, second)
    ring.start()
    for one in fetch[1:]:
        one.wait()

    def moved(s):
        at = pl.ds(pl.multiple_of(s * rows, rows), rows)
        return (
            pltpu.make_async_copy(buf.at[s], normed_hbm.at[at], locals_.at[s]),
            pltpu.make_async_copy(qkv_ref.at[at], qkv_hbm.at[at], locals_.at[8 + s]),
        )

    def slot(s, carry):
        at = pl.ds(pl.multiple_of(s * rows, rows), rows)
        normed_out, qkv_out = moved(s)
        normed_out.start()
        qkv_ref[at, :] = dot_nn(buf[s], w_ref[...]).astype(BF)
        qkv_out.start()
        return carry

    ring.pair()
    lax.fori_loop(0, 2, slot, 0)
    ring.forward()
    ring.middle()
    lax.fori_loop(2, 6, slot, 0)
    ring.finish()
    lax.fori_loop(6, 8, slot, 0)
    for s in range(8):
        for one in moved(s):
            one.wait()
    ring.drain()


def project(tokens, gain, w_query, w_key, w_value):
    rows, width = tokens.shape
    cols = w_query.shape[1]
    hbm = pl.BlockSpec(memory_space=HBM_SPACE)
    return pl.pallas_call(
        project_body, name="gather_project",
        in_specs=[hbm, pl.BlockSpec(memory_space=VMEM_SPACE), hbm, hbm, hbm],
        out_specs=[hbm, hbm],
        out_shape=[jax.ShapeDtypeStruct((8 * rows, 3 * cols), BF), jax.ShapeDtypeStruct((8 * rows, width), BF)],
        scratch_shapes=[
            pltpu.VMEM((rows, width), BF), pltpu.VMEM((width, 3 * cols), BF), pltpu.VMEM((8 * rows, 3 * cols), BF),
            pltpu.VMEM((8, rows, width), BF), pltpu.SemaphoreType.DMA((11,)), pltpu.SemaphoreType.DMA((11,)),
            pltpu.SemaphoreType.DMA((20,)),
        ],
        compiler_params=pltpu.CompilerParams(collective_id=1, has_side_effects=True, vmem_limit_bytes=58 * 2**20),
        cost_estimate=pl.CostEstimate(flops=2 * 8 * rows * width * 3 * cols, bytes_accessed=60 * 2**20, transcendentals=0),
    )(tokens, gain[None, :], w_query, w_key, w_value)

class Scatter:
    def __init__(self, product, own_ref, bufs, sems, core, sib, first, second):
        self.product, self.own_ref, self.core = product, own_ref, core
        self.away_ref, self.r0, self.s1, self.r1, self.s2, self.r2, self.s3, self.r3 = bufs
        self.chunks, _, self.rows, self.step = self.away_ref.shape
        self.half = self.chunks * self.step
        sends, recvs = sems

        def copy(source, target, j, k, device):
            return pltpu.make_async_remote_copy(
                src_ref=source.at[j], dst_ref=target.at[j], send_sem=sends.at[j, k], recv_sem=recvs.at[j, k],
                device_id=device, device_id_type=MESH,
            )

        self.copies = [
            [copy(self.away_ref, self.r0, j, 0, sib), copy(self.s1, self.r1, j, 1, first),
             copy(self.s2, self.r2, j, 2, second), copy(self.s3, self.r3, j, 3, sib)]
            for j in range(self.chunks)
        ]

    def column(self, j, core):
        return pl.multiple_of(core * self.half + j * self.step, self.step)

    def away(self, j):
        col = self.column(j, 1 - self.core)

        def some(p, carry):
            self.away_ref[j, p] = self.product(p, col).astype(BF)
            return carry

        lax.fori_loop(0, 8, some, 0)
        self.copies[j][0].start()

    def kept(self, j, p):
        came = 4 * ((p // 2) % 2) + 2 * (p // 4) + 1 - p % 2
        return self.product(p, self.column(j, self.core)) + self.r0[j, came].astype(F32)

    def one(self, j):
        self.copies[j][0].wait_recv()

        def some(p, carry):
            self.s1[j, p - 4] = self.kept(j, p).astype(BF)
            return carry

        lax.fori_loop(4, 8, some, 0)
        self.copies[j][1].start()

    def two(self, j):
        self.copies[j][1].wait_recv()

        def some(p, carry):
            self.s2[j, p - 2] = (self.kept(j, p) + self.r1[j, p].astype(F32)).astype(BF)
            return carry

        lax.fori_loop(2, 4, some, 0)
        self.copies[j][2].start()

    def three(self, j):
        self.copies[j][2].wait_recv()

        def last(p):
            return self.kept(j, p) + self.r1[j, p].astype(F32) + self.r2[j, p].astype(F32)

        self.s3[j] = last(1).astype(BF)
        self.copies[j][3].start()
        self.own_ref[:, pl.ds(self.column(j, self.core), self.step)] = last(0)

    def four(self, j):
        self.copies[j][3].wait_recv()
        self.own_ref[:, pl.ds(self.column(j, 1 - self.core), self.step)] = self.r3[j].astype(F32)

    def each(self, stage):
        for j in range(self.chunks):
            stage(j)

    def drain(self):
        for copies in self.copies:
            for one in copies:
                one.wait_send()


def scatter_scratch(rows, width, chunks):
    step = width // 2 // chunks
    sizes = [(8, rows, step)] * 2 + [(4, rows, step)] * 2 + [(2, rows, step)] * 2 + [(rows, step)] * 2
    return [pltpu.VMEM((chunks,) + size, BF) for size in sizes] + [pltpu.SemaphoreType.DMA((chunks, 4))] * 2


def gather_scratch(rows, width):
    return [pltpu.VMEM((8, rows, width), BF), pltpu.SemaphoreType.DMA((11,)), pltpu.SemaphoreType.DMA((11,))]


def rows_loop(rows, step, body):
    def some(i, carry):
        body(pl.ds(pl.multiple_of(i * step, step), step))
        return carry

    lax.fori_loop(0, rows // step, some, 0)


def block_place(a, rows):
    me = lax.axis_index("mp")
    core = me % 2
    by_c = (a % 2 + core) % 2
    by_x = (a // 2 + me // 2) % 2
    by_y = (a // 4 + me // 4) % 2
    position = 4 * (by_y + core * (by_x - by_y)) + 2 * (by_x + core * (by_y - by_x)) + by_c
    return pl.multiple_of(position * rows, rows)


def forward_body(
    heads, qkv_hbm, grad_hbm, tok_hbm, w_out_hbm, w_up_hbm, gain_ref, rk_ref, ck_ref,
    mixed_hbm, lse_ref, attn_hbm, normed_hbm, hidden_hbm, rows_hbm,
    qkv, tok, w_out, w_up, mixed, own, hidden, ks, vs, loads, stores,
    nbuf, nsend, nrecv, gbuf, gsend, grecv, *scatter,
):
    core, sib, first, second = neighbours()
    rows, width = tok.shape
    local = pltpu.make_async_copy
    fetch = [
        local(grad_hbm, gbuf.at[0], loads.at[0]), local(qkv_hbm, qkv, loads.at[1]), local(w_out_hbm, w_out, loads.at[2]),
        local(tok_hbm, tok, loads.at[3]), local(w_up_hbm, w_up, loads.at[4]),
    ]
    for one in fetch:
        one.start()
    greet(sib, first, second)
    fetch[0].wait()
    grads = Gather(gbuf, gsend, grecv, sib, first, second)
    grads.start()
    fetch[1].wait()

    def head(h, carry):
        def part(k):
            return lambda at: qkv[pl.ds(at, rows), pl.ds(pl.multiple_of((k * heads + h) * HD, HD), HD)]

        def put_mixed(at, value):
            mixed[pl.ds(at, rows), pl.ds(pl.multiple_of(h * HD, HD), HD)] = value

        def put_lse(a, value):
            lse_ref[h, a * rows:(a + 1) * rows, :] = value

        attend_head(rows, 8, lambda a: block_place(a, rows), part(0), part(1), part(2), rk_ref, ck_ref, put_mixed, put_lse, ks, vs)
        return carry

    lax.fori_loop(0, heads, head, 0)
    mixed_out = local(mixed, mixed_hbm, stores.at[0])
    mixed_out.start()

    def product(p, col):
        return dot_nn(mixed[pl.ds(pl.multiple_of(p * rows, rows), rows), :], w_out[:, pl.ds(col, net.step)])

    fetch[2].wait()
    net = Scatter(product, own, scatter[:8], scatter[8:], core, sib, first, second)
    for stage in (net.away, net.one, net.two, net.three, net.four):
        net.each(stage)
    attn_out = local(own, attn_hbm, stores.at[1])
    attn_out.start()

    fetch[3].wait()

    def norm(part):
        residual = tok[part, :].astype(F32) + own[part, :]
        nbuf[0, part, :] = norm_rows(residual, gain_ref[...]).astype(BF)

    rows_loop(rows, 32, norm)
    ring = Gather(nbuf, nsend, nrecv, sib, first, second)
    ring.start()
    fetch[4].wait()
    cols = hidden.shape[1]
    tile = min(512, cols)

    def moved(s):
        at = pl.ds(pl.multiple_of(s * rows, rows), rows)
        return (
            local(nbuf.at[s], normed_hbm.at[at], stores.at[2 + s]),
            local(hidden.at[at], hidden_hbm.at[at], stores.at[10 + s]),
        )

    def slot(s, carry):
        at = pl.ds(pl.multiple_of(s * rows, rows), rows)
        normed_out, hidden_out = moved(s)
        normed_out.start()

        def some(t, inner):
            col = pl.ds(pl.multiple_of(t * tile, tile), tile)
            hidden[at, col] = gelu_fn(dot_nn(nbuf[s], w_up[:, col])).astype(BF)
            return inner

        lax.fori_loop(0, cols // tile, some, 0)
        hidden_out.start()
        return carry

    ring.pair()
    lax.fori_loop(0, 2, slot, 0)
    ring.forward()
    grads.pair()
    grads.forward()
    ring.middle()
    lax.fori_loop(2, 6, slot, 0)
    ring.finish()
    lax.fori_loop(6, 8, slot, 0)
    grads.middle()
    grads.finish()
    copies = [local(gbuf.at[s], rows_hbm.at[pl.ds(s * rows, rows)], stores.at[18 + s]) for s in range(8)]
    for one in copies:
        one.start()
    for s in range(8):
        copies.extend(moved(s))
    for one in copies + [mixed_out, attn_out]:
        one.wait()
    ring.drain()
    grads.drain()
    net.drain()


def forward(qkv, grad_out, tokens, w_out, w_up, gain, row_key, col_key, heads):
    rows, width = tokens.shape
    seq, hidden = 8 * rows, w_up.shape[1]
    hbm, vmem = pl.BlockSpec(memory_space=HBM_SPACE), pl.BlockSpec(memory_space=VMEM_SPACE)
    shape = jax.ShapeDtypeStruct
    return pl.pallas_call(
        functools.partial(forward_body, heads), name="forward_layer",
        in_specs=[hbm] * 5 + [vmem] * 3,
        out_specs=[hbm, vmem, hbm, hbm, hbm, hbm],
        out_shape=[
            shape((seq, heads * HD), BF), shape((heads, seq, 1), F32), shape((rows, width), F32), shape((seq, width), BF),
            shape((seq, hidden), BF), shape((seq, width), BF),
        ],
        scratch_shapes=[
            pltpu.VMEM((seq, 3 * heads * HD), BF), pltpu.VMEM((rows, width), BF), pltpu.VMEM((heads * HD, width), BF),
            pltpu.VMEM((width, hidden), BF), pltpu.VMEM((seq, heads * HD), BF), pltpu.VMEM((rows, width), F32),
            pltpu.VMEM((seq, hidden), BF), pltpu.VMEM((seq, HD), BF), pltpu.VMEM((seq, HD), BF),
            pltpu.SemaphoreType.DMA((5,)), pltpu.SemaphoreType.DMA((26,)),
        ] + gather_scratch(rows, width) * 2 + scatter_scratch(rows, width, 2),
        compiler_params=pltpu.CompilerParams(collective_id=2, has_side_effects=True, vmem_limit_bytes=62 * MIB),
        cost_estimate=pl.CostEstimate(flops=40 * 10**9, bytes_accessed=250 * MIB, transcendentals=0),
    )(qkv, grad_out, tokens, w_out, w_up, gain[None, :], row_key, col_key)

def gelu_slope(x):
    c = 0.7978845608028654
    square = x * x
    t = jnp.tanh(c * (x + 0.044715 * (x * square)))
    return 0.5 * (1.0 + t) + 0.5 * x * (1.0 - t * t) * (c * (1.0 + 3 * 0.044715 * square))


def row_sums(product):
    ones = jnp.ones((8, product.shape[1]), F32)
    return lax.dot_general(
        ones, product, (((1,), (1,)), ((), ())), preferred_element_type=F32, precision=lax.Precision.HIGHEST
    )[0:1]


def middle_body(
    hidden_hbm, w_down_hbm, w_up_hbm, normed_hbm, grads_hbm,
    mlp_hbm, dnorm_hbm, up_hbm, gain_ref,
    hidden, w_down, w_up, pre, normed, grads, tiles, ups, mlp, dnorm, loads, stores, *scatter,
):
    core, sib, first, second = neighbours()
    rows, width = mlp.shape
    inner = hidden.shape[1]
    local = pltpu.make_async_copy
    fetch = [
        local(source, target, loads.at[i])
        for i, (source, target) in enumerate(((hidden_hbm, hidden), (w_down_hbm, w_down), (w_up_hbm, w_up)))
    ]

    def at(p):
        return pl.ds(pl.multiple_of(p * rows, rows), rows)

    def block(s):
        return (
            local(normed_hbm.at[at(s)], normed.at[s % 2], loads.at[3 + s % 2]),
            local(grads_hbm.at[at(s)], grads.at[s % 2], loads.at[5 + s % 2]),
        )

    for one in fetch:
        one.start()
    for one in block(0):
        one.start()
    greet(sib, first, second)

    def down(p, col):
        return dot_nn(hidden[at(p), :], w_down[:, pl.ds(col, net.step)])

    def up_back(p, col):
        return dot_nt(pre[at(p), :], w_up[pl.ds(col, net.step), :])

    net = Scatter(down, mlp, scatter[:8], scatter[8:10], core, sib, first, second)
    back = Scatter(up_back, dnorm, scatter[10:18], scatter[18:], core, sib, first, second)
    fetch[0].wait()
    fetch[1].wait()
    net.each(net.away)
    net.each(net.one)
    fetch[2].wait()
    part = min(512, inner)

    def slopes(s, carry):
        for one in block(s):
            one.wait()

        @pl.when(s < 7)
        def _():
            for one in block(s + 1):
                one.start()

        def some(t, more):
            col = pl.ds(pl.multiple_of(t * part, part), part)
            slope = gelu_slope(dot_nn(normed[s % 2], w_up[:, col]))
            pre[at(s), col] = (slope * dot_nt(grads[s % 2], w_down[col, :])).astype(BF)
            return more

        lax.fori_loop(0, inner // part, some, 0)
        return carry

    lax.fori_loop(0, 8, slopes, 0)
    tile = tiles.shape[2]

    def load_tile(t):
        return local(normed_hbm.at[:, pl.ds(pl.multiple_of(t * tile, tile), tile)], tiles.at[t % 2], loads.at[7 + t % 2])

    def save_tile(t):
        return local(ups.at[t % 2], up_hbm.at[pl.ds(pl.multiple_of(t * tile, tile), tile)], stores.at[2 + t % 2])

    load_tile(0).start()
    net.each(net.two)
    back.each(back.away)
    back.each(back.one)
    net.each(net.three)

    def weight(t, carry):
        load_tile(t).wait()

        @pl.when(t < width // tile - 1)
        def _():
            load_tile(t + 1).start()

        @pl.when(t >= 2)
        def _():
            save_tile(t - 2).wait()

        value = dot_tn(tiles[t % 2], pre[...])
        ups[t % 2] = value.astype(BF)
        save_tile(t).start()
        gain_ref[:, pl.ds(pl.multiple_of(t * tile, tile), tile)] = row_sums(
            value * w_up[pl.ds(pl.multiple_of(t * tile, tile), tile), :].astype(F32)
        )
        return carry

    lax.fori_loop(0, width // tile, weight, 0)
    net.each(net.four)
    outs = [local(mlp, mlp_hbm, stores.at[0])]
    outs[0].start()
    for name in ("two", "three", "four"):
        back.each(getattr(back, name))
    outs.append(local(dnorm, dnorm_hbm, stores.at[1]))
    outs[1].start()
    for one in outs:
        one.wait()
    save_tile(width // tile - 2).wait()
    save_tile(width // tile - 1).wait()
    net.drain()
    back.drain()


def middle(hidden, w_down, w_up, normed, grads):
    seq, inner = hidden.shape
    width = w_down.shape[1]
    rows = seq // 8
    tile = 256
    hbm, vmem = pl.BlockSpec(memory_space=HBM_SPACE), pl.BlockSpec(memory_space=VMEM_SPACE)
    shape = jax.ShapeDtypeStruct
    return pl.pallas_call(
        middle_body, name="middle_layer",
        in_specs=[hbm] * 5,
        out_specs=[hbm] * 3 + [vmem],
        out_shape=[shape((rows, width), F32), shape((rows, width), F32), shape((width, inner), BF), shape((1, width), F32)],
        scratch_shapes=[
            pltpu.VMEM((seq, inner), BF), pltpu.VMEM((inner, width), BF), pltpu.VMEM((width, inner), BF),
            pltpu.VMEM((seq, inner), BF), pltpu.VMEM((2, rows, width), BF), pltpu.VMEM((2, rows, width), BF),
            pltpu.VMEM((2, seq, tile), BF), pltpu.VMEM((2, tile, inner), BF), pltpu.VMEM((rows, width), F32),
            pltpu.VMEM((rows, width), F32), pltpu.SemaphoreType.DMA((9,)), pltpu.SemaphoreType.DMA((4,)),
        ] + scatter_scratch(rows, width, 2) * 2,
        compiler_params=pltpu.CompilerParams(collective_id=5, has_side_effects=True, vmem_limit_bytes=63 * MIB),
        cost_estimate=pl.CostEstimate(flops=45 * 10**9, bytes_accessed=200 * MIB, transcendentals=0),
    )(hidden, w_down, w_up, normed, grads)


def turn_body(
    heads, dnorm_hbm, attn_hbm, tok_hbm, grad_hbm, w_out_hbm, qkv_hbm, mixed_hbm, gain_ref, lse_ref, rk_ref, ck_ref,
    branch_hbm, dqkv_hbm, residual_hbm,
    own, attn, tok, grad, w_out, qkv, mixed, dmixed, dqkv, ks, vs, dks, dvs, loads, stores, bbuf, bsend, brecv,
):
    core, sib, first, second = neighbours()
    rows, width = tok.shape
    local = pltpu.make_async_copy
    fetch = [
        local(source, target, loads.at[i])
        for i, (source, target) in enumerate((
            (dnorm_hbm, own), (attn_hbm, attn), (tok_hbm, tok), (grad_hbm, grad), (w_out_hbm, w_out), (qkv_hbm, qkv),
            (mixed_hbm, mixed),
        ))
    ]
    for one in fetch:
        one.start()
    greet(sib, first, second)
    for one in fetch[:4]:
        one.wait()

    def norm(part):
        residual = tok[part, :].astype(F32) + attn[part, :]
        total = grad[part, :].astype(F32) + norm_back(residual, gain_ref[...], own[part, :])
        own[part, :] = total
        bbuf[0, part, :] = total.astype(BF)

    rows_loop(rows, 32, norm)
    ring = Gather(bbuf, bsend, brecv, sib, first, second)
    ring.start()
    residual_out = local(own, residual_hbm, stores.at[0])
    residual_out.start()
    fetch[4].wait()

    def moved(s):
        return local(bbuf.at[s], branch_hbm.at[pl.ds(pl.multiple_of(s * rows, rows), rows)], stores.at[2 + s])

    def slot(s, carry):
        moved(s).start()
        dmixed[pl.ds(pl.multiple_of(s * rows, rows), rows), :] = dot_nt(bbuf[s], w_out[...]).astype(BF)
        return carry

    ring.pair()
    lax.fori_loop(0, 2, slot, 0)
    ring.forward()
    ring.middle()
    lax.fori_loop(2, 6, slot, 0)
    ring.finish()
    lax.fori_loop(6, 8, slot, 0)
    fetch[5].wait()
    fetch[6].wait()

    def head(h, carry):
        def load(ref, k):
            return lambda at: ref[pl.ds(at, rows), pl.ds(pl.multiple_of((k * heads + h) * HD, HD), HD)]

        def save(k):
            def put(at, value):
                dqkv[pl.ds(at, rows), pl.ds(pl.multiple_of((k * heads + h) * HD, HD), HD)] = value
            return put

        unattend_head(
            rows, 8, lambda a: block_place(a, rows), load(qkv, 0), load(qkv, 1), load(qkv, 2), load(dmixed, 0), load(mixed, 0),
            lambda a: lse_ref[h, a * rows:(a + 1) * rows, :], rk_ref, ck_ref, save(0), save(1), save(2), ks, vs, dks, dvs,
        )
        return carry

    lax.fori_loop(0, heads, head, 0)
    dqkv_out = local(dqkv, dqkv_hbm, stores.at[1])
    dqkv_out.start()
    for s in range(8):
        moved(s).wait()
    residual_out.wait()
    dqkv_out.wait()
    ring.drain()


def turn(dnorm, attn_own, tokens, grad_out, w_out, qkv, mixed, gain, lse, row_key, col_key, heads):
    rows, width = tokens.shape
    seq = 8 * rows
    hbm, vmem = pl.BlockSpec(memory_space=HBM_SPACE), pl.BlockSpec(memory_space=VMEM_SPACE)
    shape = jax.ShapeDtypeStruct
    cols = heads * HD
    return pl.pallas_call(
        functools.partial(turn_body, heads), name="turn_layer",
        in_specs=[hbm] * 7 + [vmem] * 4,
        out_specs=[hbm] * 3,
        out_shape=[shape((seq, width), BF), shape((seq, 3 * cols), BF), shape((rows, width), F32)],
        scratch_shapes=[
            pltpu.VMEM((rows, width), F32), pltpu.VMEM((rows, width), F32), pltpu.VMEM((rows, width), BF),
            pltpu.VMEM((rows, width), BF), pltpu.VMEM((cols, width), BF), pltpu.VMEM((seq, 3 * cols), BF),
            pltpu.VMEM((seq, cols), BF), pltpu.VMEM((seq, cols), BF), pltpu.VMEM((seq, 3 * cols), BF),
            pltpu.VMEM((seq, HD), BF), pltpu.VMEM((seq, HD), BF), pltpu.VMEM((seq, HD), F32), pltpu.VMEM((seq, HD), F32),
            pltpu.SemaphoreType.DMA((7,)), pltpu.SemaphoreType.DMA((10,)),
        ] + gather_scratch(rows, width),
        compiler_params=pltpu.CompilerParams(collective_id=3, has_side_effects=True, vmem_limit_bytes=60 * MIB),
        cost_estimate=pl.CostEstimate(flops=45 * 10**9, bytes_accessed=200 * MIB, transcendentals=0),
    )(dnorm, attn_own, tokens, grad_out, w_out, qkv, mixed, gain[None, :], lse, row_key, col_key)


def weights_body(normed_ref, branch_ref, dqkv_ref, mixed_ref, wq_ref, wk_ref, wv_ref, out_ref, gain_ref):
    cols = wq_ref.shape[1]
    value = dot_tn(normed_ref[...], dqkv_ref[...])
    out_ref[:, :3 * cols] = value.astype(BF)
    out_ref[:, 3 * cols:] = dot_tn(branch_ref[...], mixed_ref[...]).astype(BF)
    gain_ref[...] = sum(
        row_sums(value[:, k * cols:(k + 1) * cols] * w_ref[...].astype(F32))
        for k, w_ref in enumerate((wq_ref, wk_ref, wv_ref))
    )


def weights(normed, branch, dqkv, mixed, w_query, w_key, w_value):
    seq, width = normed.shape
    cols = w_query.shape[1]
    tile = 256
    full = lambda c: pl.BlockSpec((seq, c), lambda t: (0, 0))
    strip = pl.BlockSpec((seq, tile), lambda t: (0, t))
    rows = pl.BlockSpec((tile, cols), lambda t: (t, 0))
    return pl.pallas_call(
        weights_body, name="weight_gradients", grid=(width // tile,),
        in_specs=[strip, strip, full(3 * cols), full(cols), rows, rows, rows],
        out_specs=[pl.BlockSpec((tile, 4 * cols), lambda t: (t, 0)), pl.BlockSpec((1, tile), lambda t: (0, t))],
        out_shape=[jax.ShapeDtypeStruct((width, 4 * cols), BF), jax.ShapeDtypeStruct((1, width), F32)],
        compiler_params=pltpu.CompilerParams(vmem_limit_bytes=48 * MIB),
        cost_estimate=pl.CostEstimate(flops=2 * seq * width * 4 * cols, bytes_accessed=30 * MIB, transcendentals=0),
    )(normed, branch, dqkv, mixed, w_query, w_key, w_value)


def finish_body(dqkv_hbm, wq_hbm, wk_hbm, wv_hbm, dnorm_hbm, dqkv, w_qkv, dnorm, loads, stores, *scatter):
    core, sib, first, second = neighbours()
    rows = dnorm.shape[0]
    cols = wq_hbm.shape[1]
    local = pltpu.make_async_copy
    pairs = [(dqkv_hbm, dqkv)]
    pairs += [(w, w_qkv.at[:, pl.ds(k * cols, cols)]) for k, w in enumerate((wq_hbm, wk_hbm, wv_hbm))]
    fetch = [local(source, target, loads.at[i]) for i, (source, target) in enumerate(pairs)]
    for one in fetch:
        one.start()
    greet(sib, first, second)

    def project_back(p, col):
        return dot_nt(dqkv[pl.ds(pl.multiple_of(p * rows, rows), rows), :], w_qkv[pl.ds(col, net.step), :])

    net = Scatter(project_back, dnorm, scatter[:8], scatter[8:], core, sib, first, second)
    for one in fetch:
        one.wait()
    for stage in (net.away, net.one, net.two, net.three, net.four):
        net.each(stage)
    out = local(dnorm, dnorm_hbm, stores.at[0])
    out.start()
    out.wait()
    net.drain()


def finish(dqkv, w_query, w_key, w_value):
    seq = dqkv.shape[0]
    width, cols = w_query.shape
    rows = seq // 8
    hbm = pl.BlockSpec(memory_space=HBM_SPACE)
    return pl.pallas_call(
        finish_body, name="last_scatter",
        in_specs=[hbm] * 4,
        out_specs=hbm,
        out_shape=jax.ShapeDtypeStruct((rows, width), F32),
        scratch_shapes=[
            pltpu.VMEM((seq, 3 * cols), BF), pltpu.VMEM((width, 3 * cols), BF), pltpu.VMEM((rows, width), F32),
            pltpu.SemaphoreType.DMA((4,)), pltpu.SemaphoreType.DMA((1,)),
        ] + scatter_scratch(rows, width, 2),
        compiler_params=pltpu.CompilerParams(collective_id=4, has_side_effects=True, vmem_limit_bytes=48 * MIB),
        cost_estimate=pl.CostEstimate(flops=20 * 10**9, bytes_accessed=100 * MIB, transcendentals=0),
    )(dqkv, w_query, w_key, w_value)


def after(value, *others):
    return lax.optimization_barrier((value,) + others)[0]


def over_mp(value):
    return lax.all_gather(value, "mp", axis=0, tiled=True)


def sum_mp(value):
    return lax.psum_scatter(value.astype(BF), "mp", scatter_dimension=0, tiled=True).astype(F32)


def sum_dp(value, axis):
    return lax.psum_scatter(value.astype(BF), "dp", scatter_dimension=axis, tiled=True).astype(F32)


def small_total(vector, n_dp):
    for axis, count in (("mp", 8), ("dp", n_dp)):
        bit = 1
        while bit < count:
            vector = vector + lax.ppermute(vector, axis, [(i, i ^ bit) for i in range(count)])
            bit *= 2
    return vector


def on_device(tokens, segment, valid, gain_attn, w_query, w_key, w_value, w_out, gain_mlp, w_up, w_down, grad_out):
    own_rows, width = tokens.shape
    seq_rows = segment.shape[0]
    heads = w_query.shape[1] // HD
    n_dp, n_mp = lax.axis_size("dp"), lax.axis_size("mp")
    dp, me = lax.axis_index("dp"), lax.axis_index("mp")
    cube = n_mp == 8 and n_dp & (n_dp - 1) == 0
    order = jnp.arange(seq_rows // own_rows, dtype=jnp.int32)
    valid_group = lax.dynamic_slice_in_dim(valid, dp * seq_rows, seq_rows)
    valid_own = lax.dynamic_slice_in_dim(valid_group, me * own_rows, own_rows)
    row_key = segment[:, None]
    col_key = jnp.where(valid_group > 0, segment, -1)[None, :]
    tokens32 = tokens.astype(F32)

    if cube:
        qkv, normed = project(tokens, gain_attn, w_query, w_key, w_value)
        mixed, lse, attn_own, normed_mlp, hidden, grad_rows = forward(
            qkv, grad_out, tokens, w_out, w_up, gain_mlp, row_key, col_key, heads
        )
    else:
        normed = over_mp(norm_rows(tokens32, gain_attn).astype(BF))
        qkv = jnp.concatenate([dot_nn(normed, w).astype(BF) for w in (w_query, w_key, w_value)], 1)
        mixed, lse = attn_fwd(qkv, order, row_key, col_key, heads, own_rows)
        grad_rows = over_mp(after(grad_out, qkv))
        attn_own = sum_mp(dot_nn(mixed, w_out))
        normed_mlp = over_mp(norm_rows(tokens32 + attn_own, gain_mlp).astype(BF))
        hidden = gelu_fn(dot_nn(normed_mlp, w_up)).astype(BF)
    residual = tokens32 + attn_own

    part_down = dot_tn(hidden, grad_rows).astype(BF)
    grad_down = sum_dp(part_down, 1)
    if cube:
        mlp_own, grad_normed, part_up, gain_mlp_part = middle(
            hidden, w_down, w_up, normed_mlp, after(grad_rows, part_down)
        )
        grad_normed, grad_down = lax.optimization_barrier((grad_normed, grad_down))
        gain_mlp_part = gain_mlp_part[0]
        grad_up = sum_dp(part_up, 0)
        grad_branch, grads_qkv, grad_residual = turn(
            grad_normed, attn_own, tokens, grad_out, w_out, qkv, mixed, gain_mlp, lse, row_key, col_key, heads
        )
        part_last, gain_attn_part = weights(normed, grad_branch, grads_qkv, mixed, w_query, w_key, w_value)
        gain_attn_part = gain_attn_part[0]
        part_last, grads_qkv, grad_up = lax.optimization_barrier((part_last, grads_qkv, grad_up))
        grad_last = sum_dp(part_last, 0)
        grad_qkv, grad_out_proj = grad_last[:, :3 * heads * HD], grad_last[:, 3 * heads * HD:].T
        grad_normed_attn = finish(grads_qkv, w_query, w_key, w_value)
    else:
        grad_hidden = dot_nt(grad_rows, w_down)
        grad_pre = (gelu_slope(dot_nn(normed_mlp, w_up)) * grad_hidden).astype(BF)
        part_up = dot_tn(normed_mlp, grad_pre)
        grad_up = sum_dp(part_up, 0)
        gain_mlp_part = jnp.sum(part_up * w_up.astype(F32), axis=1)
        grad_residual = grad_out.astype(F32) + norm_back(residual, gain_mlp, sum_mp(dot_nt(grad_pre, w_up)))
        grad_branch = over_mp(grad_residual.astype(BF))
        grad_mixed = dot_nt(grad_branch, w_out).astype(BF)
        grads_qkv = jnp.concatenate(attn_bwd(qkv, grad_mixed, mixed, lse, order, row_key, col_key, heads, own_rows), 1)
        grad_out_proj = sum_dp(dot_tn(mixed, grad_branch), 1)
        part_qkv = dot_tn(normed, grads_qkv)
        grad_qkv = sum_dp(part_qkv, 0)
        w_qkv = jnp.concatenate([w_query, w_key, w_value], 1)
        gain_attn_part = jnp.sum(part_qkv * w_qkv.astype(F32), axis=1)
        mlp_own = sum_mp(dot_nn(hidden, w_down))
        grad_normed_attn = sum_mp(dot_nt(grads_qkv, w_qkv))
    stream = residual + mlp_own
    mask_own = valid_own.astype(F32)[:, None]
    grad_tokens = (grad_residual + norm_back(tokens32, gain_attn, grad_normed_attn)).astype(BF)

    squares = jnp.stack([jnp.sum(mask_own * part * part) for part in (stream, attn_own, mlp_own)])
    small = jnp.concatenate([gain_attn_part / gain_attn, gain_mlp_part / gain_mlp, squares])
    summed = small_total(small, n_dp) if cube else lax.psum(small, ("dp", "mp"))
    counted = jnp.maximum(jnp.sum(valid).astype(F32) * width, 1.0)
    gain_rows = width // (n_dp * n_mp)
    place = (dp * n_mp + me) * gain_rows
    rms = jnp.sqrt(summed[2 * width:] / counted)
    shard = heads * HD
    return (
        stream.astype(BF),
        grad_tokens,
        lax.dynamic_slice_in_dim(summed[:width], place, gain_rows),
        grad_qkv[:, :shard],
        grad_qkv[:, shard:2 * shard],
        grad_qkv[:, 2 * shard:],
        grad_out_proj,
        lax.dynamic_slice_in_dim(summed[width:2 * width], place, gain_rows),
        grad_up,
        grad_down,
        rms[0],
        rms[1],
        rms[2],
    )


def solution(mesh):
    tokens_spec = P(("dp", "mp"), None)
    cols, rows = P(None, "mp"), P("mp", None)
    return jax.shard_map(
        on_device,
        mesh=mesh,
        in_specs=(tokens_spec, P("dp"), P(), P(), cols, cols, cols, rows, P(), cols, rows, tokens_spec),
        out_specs=(
            tokens_spec,
            tokens_spec,
            P(("dp", "mp")),
            P("dp", "mp"),
            P("dp", "mp"),
            P("dp", "mp"),
            P("mp", "dp"),
            P(("dp", "mp")),
            P("dp", "mp"),
            P("mp", "dp"),
            P(),
            P(),
            P(),
        ),
        check_vma=False,
    )
```

```python
import functools

import jax
import jax.numpy as jnp
from jax import lax
from jax.experimental import pallas as pl
from jax.experimental.pallas import tpu as pltpu
from jax.sharding import PartitionSpec as P

HD = 128
NEGATIVE = -1e30
LOG2E = 1.4426950408889634
EPSILON = 1e-05
BF = jnp.bfloat16
F32 = jnp.float32
MIB = 2**20


def dot_nn(a, b):
    return jnp.dot(a, b, preferred_element_type=F32)


def dot_tn(a, b):
    return lax.dot_general(a, b, (((0,), (0,)), ((), ())), preferred_element_type=F32)


def dot_nt(a, b):
    return lax.dot_general(a, b, (((1,), (1,)), ((), ())), preferred_element_type=F32)


def diagonal(blk):
    rows = lax.broadcasted_iota(jnp.int32, (blk, blk), 0)
    cols = lax.broadcasted_iota(jnp.int32, (blk, blk), 1)
    return cols < rows, cols == rows


def attend_head(blk, count, place, queries, keys, values, rk_ref, ck_ref, put_mixed, put_lse, ks, vs):
    c = HD ** -0.5 * LOG2E
    for a in range(count):
        ks[a * blk:(a + 1) * blk, :] = keys(place(a))
        vs[a * blk:(a + 1) * blk, :] = values(place(a))
    earlier, itself = diagonal(blk)
    for a in range(count):
        end = (a + 1) * blk
        low = end - blk
        s = dot_nt(queries(place(a)), ks[:end, :])
        ok = rk_ref[low:end, 0:1] == ck_ref[:, :end]
        sd = jnp.where((ok[:, low:] & earlier) | itself, s[:, low:], NEGATIVE)
        m = jnp.max(sd, axis=1, keepdims=True)
        if a:
            so = jnp.where(ok[:, :low], s[:, :low], NEGATIVE)
            m = jnp.maximum(m, jnp.max(so, axis=1, keepdims=True))
        pd = jnp.exp2((sd - m) * c)
        total = jnp.sum(pd, axis=1, keepdims=True)
        o = dot_nn(pd.astype(BF), vs[low:end, :])
        if a:
            po = jnp.exp2((so - m) * c)
            total += jnp.sum(po, axis=1, keepdims=True)
            o += dot_nn(po.astype(BF), vs[:low, :])
        put_mixed(place(a), (o / total).astype(BF))
        put_lse(a, m * c + jnp.log2(total))


def attn_fwd_body(blk, count, order_ref, q_ref, k_ref, v_ref, rk_ref, ck_ref, mix_ref, lse_ref, ks, vs):
    def place(a):
        return pl.multiple_of(order_ref[a] * blk, blk)

    def put_mixed(at, value):
        mix_ref[pl.ds(at, blk), :] = value

    def put_lse(a, value):
        lse_ref[0, a * blk:(a + 1) * blk, :] = value

    attend_head(
        blk, count, place, lambda at: q_ref[pl.ds(at, blk), :], lambda at: k_ref[pl.ds(at, blk), :],
        lambda at: v_ref[pl.ds(at, blk), :], rk_ref, ck_ref, put_mixed, put_lse, ks, vs,
    )


def attn_fwd(qkv, order, rowkey, colkey, heads, blk):
    seq = qkv.shape[0]
    part = lambda off: pl.BlockSpec((seq, HD), lambda h, o: (0, off * heads + h))
    return pl.pallas_call(
        functools.partial(attn_fwd_body, blk, seq // blk), name="attn_fwd",
        grid_spec=pltpu.PrefetchScalarGridSpec(
            num_scalar_prefetch=1, grid=(heads,),
            in_specs=[part(0), part(1), part(2), pl.BlockSpec((seq, 1), lambda h, o: (0, 0)),
                      pl.BlockSpec((1, seq), lambda h, o: (0, 0))],
            out_specs=[part(0), pl.BlockSpec((1, seq, 1), lambda h, o: (h, 0, 0))],
            scratch_shapes=[pltpu.VMEM((seq, HD), BF)] * 2),
        out_shape=[jax.ShapeDtypeStruct((seq, heads * HD), BF), jax.ShapeDtypeStruct((heads, seq, 1), F32)],
        compiler_params=pltpu.CompilerParams(vmem_limit_bytes=48 * MIB),
        cost_estimate=pl.CostEstimate(
            flops=2 * seq * seq * HD * heads, bytes_accessed=8 * seq * HD * heads, transcendentals=seq * seq * heads // 2),
    )(order, qkv, qkv, qkv, rowkey, colkey)


def unattend_head(blk, count, place, queries, keys, values, grads, mixes, lses, rk_ref, ck_ref, put_q, put_k, put_v, ks, vs, dks, dvs,
                  between=None):
    scale = HD ** -0.5
    c = scale * LOG2E
    for a in range(count):
        ks[a * blk:(a + 1) * blk, :] = keys(place(a))
        vs[a * blk:(a + 1) * blk, :] = values(place(a))
    earlier, itself = diagonal(blk)

    def add(ref, lo, hi, value, fresh):
        if fresh:
            ref[lo:hi, :] = value
        else:
            ref[lo:hi, :] += value

    for a in reversed(range(count)):
        end = (a + 1) * blk
        low = end - blk
        fresh = a == count - 1
        at = place(a)
        q, do = queries(at), grads(at)
        delta = jnp.sum(do.astype(F32) * mixes(at).astype(F32), axis=1, keepdims=True)
        p = jnp.exp2(dot_nt(q, ks[:end, :]) * c - lses(a))
        dp = dot_nt(do, vs[:end, :])
        ok = rk_ref[low:end, 0:1] == ck_ref[:, :end]
        pd = jnp.where((ok[:, low:] & earlier) | itself, p[:, low:], 0.0)
        dsd = (pd * (dp[:, low:] - delta)).astype(BF)
        dq = dot_nn(dsd, ks[low:end, :])
        add(dks, low, end, dot_tn(dsd, q), fresh)
        add(dvs, low, end, dot_tn(pd.astype(BF), do), fresh)
        if a:
            po = jnp.where(ok[:, :low], p[:, :low], 0.0)
            dso = (po * (dp[:, :low] - delta)).astype(BF)
            dq += dot_nn(dso, ks[:low, :])
            add(dks, 0, low, dot_tn(dso, q), fresh)
            add(dvs, 0, low, dot_tn(po.astype(BF), do), fresh)
        put_q(at, (dq * scale).astype(BF))
        if between is not None:
            between(a)
    for a in range(count):
        put_k(place(a), (dks[a * blk:(a + 1) * blk, :] * scale).astype(BF))
        put_v(place(a), dvs[a * blk:(a + 1) * blk, :].astype(BF))


def attn_bwd_body(blk, count, order_ref, q_ref, k_ref, v_ref, do_ref, mix_ref, lse_ref, rk_ref, ck_ref, dq_ref, dk_ref, dv_ref,
                  ks, vs, dks, dvs):
    def place(a):
        return pl.multiple_of(order_ref[a] * blk, blk)

    def load(ref):
        return lambda at: ref[pl.ds(at, blk), :]

    def save(ref):
        def put(at, value):
            ref[pl.ds(at, blk), :] = value
        return put

    unattend_head(
        blk, count, place, load(q_ref), load(k_ref), load(v_ref), load(do_ref), load(mix_ref),
        lambda a: lse_ref[0, a * blk:(a + 1) * blk, :], rk_ref, ck_ref, save(dq_ref), save(dk_ref), save(dv_ref), ks, vs, dks, dvs,
    )


def attn_bwd(qkv, do, mixed, lse, order, rowkey, colkey, heads, blk):
    seq = qkv.shape[0]
    part = lambda off: pl.BlockSpec((seq, HD), lambda h, o: (0, off * heads + h))
    return pl.pallas_call(
        functools.partial(attn_bwd_body, blk, seq // blk), name="attn_bwd",
        grid_spec=pltpu.PrefetchScalarGridSpec(
            num_scalar_prefetch=1, grid=(heads,),
            in_specs=[part(0), part(1), part(2), part(0), part(0), pl.BlockSpec((1, seq, 1), lambda h, o: (h, 0, 0)),
                      pl.BlockSpec((seq, 1), lambda h, o: (0, 0)), pl.BlockSpec((1, seq), lambda h, o: (0, 0))],
            out_specs=[part(0), part(0), part(0)],
            scratch_shapes=[pltpu.VMEM((seq, HD), BF)] * 2 + [pltpu.VMEM((seq, HD), F32)] * 2),
        out_shape=[jax.ShapeDtypeStruct((seq, heads * HD), BF)] * 3,
        compiler_params=pltpu.CompilerParams(vmem_limit_bytes=56 * MIB),
        cost_estimate=pl.CostEstimate(
            flops=5 * seq * seq * HD * heads, bytes_accessed=16 * seq * HD * heads, transcendentals=seq * seq * heads // 2),
    )(order, qkv, qkv, qkv, do, mixed, lse, rowkey, colkey)


def row_scale(values):
    return lax.rsqrt(jnp.mean(values * values, axis=-1, keepdims=True) + EPSILON)


def norm_rows(values, norm_gain):
    return values * row_scale(values) * norm_gain


def norm_back(values, norm_gain, grad_norm):
    scale = row_scale(values)
    normal = values * scale
    grad_hat = grad_norm * norm_gain
    inner = jnp.mean(grad_hat * normal, axis=-1, keepdims=True)
    return scale * (grad_hat - normal * inner)


def gelu_fn(values):
    return jax.nn.gelu(values, approximate=True)


MESH = pl.DeviceIdType.MESH
HBM_SPACE = pl.ANY
VMEM_SPACE = pltpu.VMEM


def neighbours():
    dp, me = lax.axis_index("dp"), lax.axis_index("mp")
    core, along_x, along_y = me % 2, (me // 2) % 2, me // 4
    by_x, by_y = me + 2 - 4 * along_x, me + 4 - 8 * along_y
    first = (1 - core) * by_y + core * by_x
    second = (1 - core) * by_x + core * by_y
    return core, (dp, me + 1 - 2 * core), (dp, first), (dp, second)


def greet(*others):
    barrier = pltpu.get_barrier_semaphore()
    for other in others:
        pl.semaphore_signal(barrier, inc=1, device_id=other, device_id_type=MESH)
    pl.semaphore_wait(barrier, len(others))


class Gather:
    COPIES = 11

    def __init__(self, buf, sends, recvs, sib, first, second):
        rows = buf.shape[1]
        low, high, whole = pl.ds(0, rows // 2), pl.ds(rows // 2, rows // 2), pl.ds(0, rows)

        def copy(i, source, target, part, device):
            return pltpu.make_async_remote_copy(
                src_ref=buf.at[source, part], dst_ref=buf.at[target, part],
                send_sem=sends.at[i], recv_sem=recvs.at[i], device_id=device, device_id_type=MESH,
            )

        self.copies = [
            copy(0, 0, 4, high, first), copy(1, 0, 4, low, first),
            copy(2, 0, 2, low, second), copy(3, 0, 2, high, second),
            copy(4, 0, 1, whole, sib),
            copy(5, 2, 6, low, first), copy(6, 4, 6, high, second),
            copy(7, 4, 3, whole, sib), copy(8, 2, 5, whole, sib),
            copy(9, 6, 7, low, sib), copy(10, 6, 7, high, sib),
        ]

    def start(self):
        for i in (0, 2, 1, 3, 4):
            self.copies[i].start()

    def pair(self):
        self.copies[4].wait_recv()

    def forward(self, both=True):
        for arrived, onward in ((2, 5), (0, 6)):
            self.copies[arrived].wait_recv()
            if both:
                self.copies[onward].start()
        for arrived, onward in ((1, 7), (3, 8)):
            self.copies[arrived].wait_recv()
            self.copies[onward].start()

    def onward(self):
        self.copies[5].start()
        self.copies[6].start()

    def middle(self):
        self.copies[7].wait_recv()
        self.copies[8].wait_recv()

    def finish(self):
        for arrived, onward in ((5, 9), (6, 10)):
            self.copies[arrived].wait_recv()
            self.copies[onward].start()
        self.copies[9].wait_recv()
        self.copies[10].wait_recv()

    def drain(self):
        for one in self.copies:
            one.wait_send()


def norm_store(rows_ref, gain_ref, store, step=32):
    def some(i, carry):
        part = pl.ds(pl.multiple_of(i * step, step), step)
        store(part, norm_rows(rows_ref[part, :].astype(F32), gain_ref[...]).astype(BF))
        return carry

    lax.fori_loop(0, rows_ref.shape[0] // step, some, 0)


def project_body(tok_hbm, gain_ref, wq_hbm, wk_hbm, wv_hbm, qkv_hbm, normed_hbm, tok_ref, w_ref, qkv_ref, buf, sends, recvs, locals_):
    core, sib, first, second = neighbours()
    rows = tok_ref.shape[0]
    width = wq_hbm.shape[1]
    fetch = [pltpu.make_async_copy(tok_hbm, tok_ref, locals_.at[16])]
    for k, w_hbm in enumerate((wq_hbm, wk_hbm, wv_hbm)):
        fetch.append(pltpu.make_async_copy(w_hbm, w_ref.at[:, pl.ds(k * width, width)], locals_.at[17 + k]))
    for one in fetch:
        one.start()
    greet(sib, first, second)
    fetch[0].wait()

    def keep(part, value):
        buf[0, part, :] = value

    norm_store(tok_ref, gain_ref, keep)
    ring = Gather(buf, sends, recvs, sib, first, second)
    ring.start()
    for one in fetch[1:]:
        one.wait()

    def moved(s):
        at = pl.ds(pl.multiple_of(s * rows, rows), rows)
        return (
            pltpu.make_async_copy(buf.at[s], normed_hbm.at[at], locals_.at[s]),
            pltpu.make_async_copy(qkv_ref.at[at], qkv_hbm.at[at], locals_.at[8 + s]),
        )

    def slot(s, carry):
        at = pl.ds(pl.multiple_of(s * rows, rows), rows)
        normed_out, qkv_out = moved(s)
        normed_out.start()
        qkv_ref[at, :] = dot_nn(buf[s], w_ref[...]).astype(BF)
        qkv_out.start()
        return carry

    ring.pair()
    lax.fori_loop(0, 2, slot, 0)
    ring.forward()
    ring.middle()
    lax.fori_loop(2, 6, slot, 0)
    ring.finish()
    lax.fori_loop(6, 8, slot, 0)
    for s in range(8):
        for one in moved(s):
            one.wait()
    ring.drain()


def project(tokens, gain, w_query, w_key, w_value):
    rows, width = tokens.shape
    cols = w_query.shape[1]
    hbm = pl.BlockSpec(memory_space=HBM_SPACE)
    return pl.pallas_call(
        project_body, name="gather_project",
        in_specs=[hbm, pl.BlockSpec(memory_space=VMEM_SPACE), hbm, hbm, hbm],
        out_specs=[hbm, hbm],
        out_shape=[jax.ShapeDtypeStruct((8 * rows, 3 * cols), BF), jax.ShapeDtypeStruct((8 * rows, width), BF)],
        scratch_shapes=[
            pltpu.VMEM((rows, width), BF), pltpu.VMEM((width, 3 * cols), BF), pltpu.VMEM((8 * rows, 3 * cols), BF),
            pltpu.VMEM((8, rows, width), BF), pltpu.SemaphoreType.DMA((11,)), pltpu.SemaphoreType.DMA((11,)),
            pltpu.SemaphoreType.DMA((20,)),
        ],
        compiler_params=pltpu.CompilerParams(collective_id=1, has_side_effects=True, vmem_limit_bytes=58 * 2**20),
        cost_estimate=pl.CostEstimate(flops=2 * 8 * rows * width * 3 * cols, bytes_accessed=60 * 2**20, transcendentals=0),
    )(tokens, gain[None, :], w_query, w_key, w_value)

class Scatter:
    def __init__(self, product, own_ref, bufs, sems, core, sib, first, second):
        self.product, self.own_ref, self.core = product, own_ref, core
        self.sent = 0
        self.away_ref, self.r0, self.s1, self.r1, self.s2, self.r2, self.s3, self.r3 = bufs
        self.chunks, _, self.rows, self.step = self.away_ref.shape
        self.half = self.chunks * self.step
        sends, recvs = sems

        def copy(source, target, j, k, device):
            return pltpu.make_async_remote_copy(
                src_ref=source.at[j], dst_ref=target.at[j], send_sem=sends.at[j, k], recv_sem=recvs.at[j, k],
                device_id=device, device_id_type=MESH,
            )

        self.copies = [
            [copy(self.away_ref, self.r0, j, 0, sib), copy(self.s1, self.r1, j, 1, first),
             copy(self.s2, self.r2, j, 2, second), copy(self.s3, self.r3, j, 3, sib)]
            for j in range(self.chunks)
        ]

    def column(self, j, core):
        return pl.multiple_of(core * self.half + j * self.step, self.step)

    def away(self, j):
        col = self.column(j, 1 - self.core)

        def some(p, carry):
            self.away_ref[j, p] = self.product(p, col).astype(BF)
            return carry

        lax.fori_loop(0, 8, some, 0)
        self.copies[j][0].start()

    def kept(self, j, p):
        came = 4 * ((p // 2) % 2) + 2 * (p // 4) + 1 - p % 2
        return self.product(p, self.column(j, self.core)) + self.r0[j, came].astype(F32)

    def one(self, j):
        self.copies[j][0].wait_recv()

        def some(p, carry):
            self.s1[j, p - 4] = self.kept(j, p).astype(BF)
            return carry

        lax.fori_loop(4, 8, some, 0)
        self.copies[j][1].start()

    def two(self, j):
        self.copies[j][1].wait_recv()

        def some(p, carry):
            self.s2[j, p - 2] = (self.kept(j, p) + self.r1[j, p].astype(F32)).astype(BF)
            return carry

        lax.fori_loop(2, 4, some, 0)
        self.copies[j][2].start()

    def three(self, j):
        self.copies[j][2].wait_recv()

        def last(p):
            return self.kept(j, p) + self.r1[j, p].astype(F32) + self.r2[j, p].astype(F32)

        self.s3[j] = last(1).astype(BF)
        self.copies[j][3].start()
        self.own_ref[:, pl.ds(self.column(j, self.core), self.step)] = last(0)

    def four(self, j):
        self.copies[j][3].wait_recv()
        self.own_ref[:, pl.ds(self.column(j, 1 - self.core), self.step)] = self.r3[j].astype(F32)

    def each(self, stage):
        for j in range(self.chunks):
            stage(j)

    def release(self, j):
        self.copies[j][0].wait_send()
        self.sent = 1

    def drain(self):
        for copies in self.copies:
            for one in copies[self.sent:]:
                one.wait_send()


def scatter_scratch(rows, width, chunks):
    step = width // 2 // chunks
    sizes = [(8, rows, step)] * 2 + [(4, rows, step)] * 2 + [(2, rows, step)] * 2 + [(rows, step)] * 2
    return [pltpu.VMEM((chunks,) + size, BF) for size in sizes] + [pltpu.SemaphoreType.DMA((chunks, 4))] * 2


def gather_scratch(rows, width):
    return [pltpu.VMEM((8, rows, width), BF), pltpu.SemaphoreType.DMA((11,)), pltpu.SemaphoreType.DMA((11,))]


def rows_loop(rows, step, body):
    def some(i, carry):
        body(pl.ds(pl.multiple_of(i * step, step), step))
        return carry

    lax.fori_loop(0, rows // step, some, 0)


def block_place(a, rows):
    me = lax.axis_index("mp")
    core = me % 2
    by_c = (a % 2 + core) % 2
    by_x = (a // 2 + me // 2) % 2
    by_y = (a // 4 + me // 4) % 2
    position = 4 * (by_y + core * (by_x - by_y)) + 2 * (by_x + core * (by_y - by_x)) + by_c
    return pl.multiple_of(position * rows, rows)


def gelu_pair(x):
    c = 0.7978845608028654
    square = x * x
    t = jnp.tanh(c * (x + 0.044715 * (x * square)))
    upper = 0.5 * (1.0 + t)
    return x * upper, upper + 0.5 * x * (1.0 - t * t) * (c + (3 * 0.044715 * c) * square)


def fill_keys(seg_ref, valid_ref, rk, ck):
    seq = seg_ref.shape[1]
    here = pl.ds(pl.multiple_of(lax.axis_index("dp") * seq, seq), seq)
    numbers = seg_ref[...].astype(F32)
    ck[...] = jnp.where(valid_ref[:, here] > 0, numbers, -1.0)
    step = 256
    for i in range(0, seq, step):
        rk[i:i + step, :] = jnp.transpose(jnp.broadcast_to(numbers[:, i:i + step], (128, step)))


def forward_body(
    heads, qkv_hbm, grad_hbm, tok_hbm, w_out_hbm, w_up_hbm, w_down_hbm, gain_ref, seg_ref, valid_ref,
    mixed_hbm, lse_ref, attn_hbm, normed_hbm, hidden_hbm, pre_hbm, rows_hbm,
    qkv, w_out, w_up, w_down, mixed, own, hidden, pre, rk_ref, ck_ref, ks, vs, loads, stores,
    nbuf, nsend, nrecv, gbuf, gsend, grecv, *scatter,
):
    core, sib, first, second = neighbours()
    rows, width = own.shape
    local = pltpu.make_async_copy
    fetch = [
        local(grad_hbm, gbuf.at[0], loads.at[0]), local(qkv_hbm, qkv, loads.at[1]), local(w_out_hbm, w_out, loads.at[2]),
        local(tok_hbm, nbuf.at[0], loads.at[3]), local(w_up_hbm, w_up, loads.at[4]),
        local(w_down_hbm, w_down, loads.at[5]),
    ]
    for one in fetch:
        one.start()
    greet(sib, first, second)
    fetch[0].wait()
    grads = Gather(gbuf, gsend, grecv, sib, first, second)
    grads.start()
    fill_keys(seg_ref, valid_ref, rk_ref, ck_ref)
    fetch[1].wait()

    def head(h, carry):
        def part(k):
            return lambda at: qkv[pl.ds(at, rows), pl.ds(pl.multiple_of((k * heads + h) * HD, HD), HD)]

        def put_mixed(at, value):
            mixed[pl.ds(at, rows), pl.ds(pl.multiple_of(h * HD, HD), HD)] = value

        def put_lse(a, value):
            lse_ref[h, a * rows:(a + 1) * rows, :] = value

        attend_head(rows, 8, lambda a: block_place(a, rows), part(0), part(1), part(2), rk_ref, ck_ref, put_mixed, put_lse, ks, vs)
        return carry

    lax.fori_loop(0, heads, head, 0)
    mixed_out = local(mixed, mixed_hbm, stores.at[0])
    mixed_out.start()

    def product(p, col):
        return dot_nn(mixed[pl.ds(pl.multiple_of(p * rows, rows), rows), :], w_out[:, pl.ds(col, net.step)])

    fetch[2].wait()
    net = Scatter(product, own, scatter[:8], scatter[8:], core, sib, first, second)
    net.each(net.away)
    net.each(net.one)
    grads.pair()
    fetch[5].wait()
    net.each(net.release)
    slopes = net.away_ref
    tile = net.step

    def back(s, carry):
        for t in range(net.chunks):
            slopes[t, s] = dot_nt(gbuf[s], w_down[t * tile:(t + 1) * tile, :]).astype(BF)
        return carry

    lax.fori_loop(0, 2, back, 0)
    grads.forward(False)
    grads.middle()
    lax.fori_loop(2, 6, back, 0)
    net.each(net.two)
    net.each(net.three)
    grads.onward()
    net.each(net.four)
    attn_out = local(own, attn_hbm, stores.at[1])
    attn_out.start()

    fetch[3].wait()

    def at(s):
        return pl.ds(pl.multiple_of(s * rows, rows), rows)

    def norm(part):
        residual = nbuf[0, part, :].astype(F32) + own[part, :]
        nbuf[0, part, :] = norm_rows(residual, gain_ref[...]).astype(BF)

    rows_loop(rows, 32, norm)
    ring = Gather(nbuf, nsend, nrecv, sib, first, second)
    ring.start()
    fetch[4].wait()
    rows_out = [local(gbuf.at[s], rows_hbm.at[pl.ds(s * rows, rows)], stores.at[6 + s]) for s in range(8)]
    for one in rows_out[:6]:
        one.start()
    def normed_copy(s):
        return local(nbuf.at[s], normed_hbm.at[at(s)], stores.at[14 + s])

    def moved(s):
        return (
            local(hidden.at[s % 2], hidden_hbm.at[at(s)], stores.at[2 + s % 2]),
            local(pre.at[s % 2], pre_hbm.at[at(s)], stores.at[4 + s % 2]),
        )

    def slot(s, carry):
        normed_copy(s).start()

        @pl.when(s >= 2)
        def _():
            for one in moved(s - 2):
                one.wait()

        def some(t, inner):
            col = pl.ds(pl.multiple_of(t * tile, tile), tile)
            value, slope = gelu_pair(dot_nn(nbuf[s], w_up[:, col]))
            hidden[s % 2, :, col] = value.astype(BF)
            pre[s % 2, :, col] = (slope * slopes[t, s].astype(F32)).astype(BF)
            return inner

        lax.fori_loop(0, net.chunks, some, 0)
        for one in moved(s):
            one.start()
        return carry

    ring.pair()
    lax.fori_loop(0, 2, slot, 0)
    grads.finish()
    lax.fori_loop(6, 8, back, 0)
    for one in rows_out[6:]:
        one.start()
    ring.forward()
    ring.middle()
    lax.fori_loop(2, 6, slot, 0)
    ring.finish()
    lax.fori_loop(6, 8, slot, 0)
    for s in range(8):
        normed_copy(s).wait()
    for one in [*moved(6), *moved(7), *rows_out, mixed_out, attn_out]:
        one.wait()
    ring.drain()
    grads.drain()
    net.drain()


def forward(qkv, grad_out, tokens, w_out, w_up, w_down, gain, segment, valid, heads):
    rows, width = tokens.shape
    seq, hidden = 8 * rows, w_up.shape[1]
    hbm, vmem = pl.BlockSpec(memory_space=HBM_SPACE), pl.BlockSpec(memory_space=VMEM_SPACE)
    shape = jax.ShapeDtypeStruct
    return pl.pallas_call(
        functools.partial(forward_body, heads), name="forward_layer",
        in_specs=[hbm] * 6 + [vmem] * 3,
        out_specs=[hbm, vmem, hbm, hbm, hbm, hbm, hbm],
        out_shape=[
            shape((seq, heads * HD), BF), shape((heads, seq, 1), F32), shape((rows, width), F32), shape((seq, width), BF),
            shape((seq, hidden), BF), shape((seq, hidden), BF), shape((seq, width), BF),
        ],
        scratch_shapes=[
            pltpu.VMEM((seq, 3 * heads * HD), BF), pltpu.VMEM((heads * HD, width), BF),
            pltpu.VMEM((width, hidden), BF), pltpu.VMEM((hidden, width), BF), pltpu.VMEM((seq, heads * HD), BF),
            pltpu.VMEM((rows, width), F32), pltpu.VMEM((2, rows, hidden), BF), pltpu.VMEM((2, rows, hidden), BF),
            pltpu.VMEM((seq, 128), F32), pltpu.VMEM((1, seq), F32),
            pltpu.VMEM((seq, HD), BF), pltpu.VMEM((seq, HD), BF),
            pltpu.SemaphoreType.DMA((6,)), pltpu.SemaphoreType.DMA((22,)),
        ] + gather_scratch(rows, width) * 2 + scatter_scratch(rows, width, 2),
        compiler_params=pltpu.CompilerParams(collective_id=2, has_side_effects=True, vmem_limit_bytes=62 * MIB),
        cost_estimate=pl.CostEstimate(flops=40 * 10**9, bytes_accessed=250 * MIB, transcendentals=0),
    )(qkv, grad_out, tokens, w_out, w_up, w_down, gain[None, :], segment[None, :], valid[None, :])

def row_sums(product):
    part = sum(product[:, i:i + 128] for i in range(0, product.shape[1], 128))
    return lax.dot_general(
        jnp.ones((8, 128), F32), part, (((1,), (1,)), ((), ())), preferred_element_type=F32, precision=lax.Precision.HIGHEST
    )[0:1]


def middle_body(
    pre_hbm, w_up_hbm, normed_hbm, dnorm_hbm, up_hbm, gain_ref, pre, w_up, tiles, ups, dnorm, loads, stores, *scatter
):
    core, sib, first, second = neighbours()
    rows, width = dnorm.shape
    local = pltpu.make_async_copy
    tile = tiles.shape[2]
    count = width // tile
    fetch = [local(pre_hbm, pre, loads.at[0]), local(w_up_hbm, w_up, loads.at[1])]

    def strip(t):
        return pl.ds(pl.multiple_of(t * tile, tile), tile)

    def load_tile(t):
        return local(normed_hbm.at[:, strip(t)], tiles.at[t % 2], loads.at[2 + t % 2])

    def save_tile(t):
        return local(ups.at[t % 2], up_hbm.at[strip(t)], stores.at[1 + t % 2])

    for one in fetch:
        one.start()
    load_tile(0).start()
    greet(sib, first, second)

    def up_back(p, col):
        return dot_nt(pre[pl.ds(pl.multiple_of(p * rows, rows), rows), :], w_up[pl.ds(col, net.step), :])

    net = Scatter(up_back, dnorm, scatter[:8], scatter[8:], core, sib, first, second)
    fetch[0].wait()
    fetch[1].wait()
    net.each(net.away)
    net.each(net.one)

    def weight(t, carry):
        load_tile(t).wait()

        @pl.when(t < count - 1)
        def _():
            load_tile(t + 1).start()

        @pl.when(t >= 2)
        def _():
            save_tile(t - 2).wait()

        value = dot_tn(tiles[t % 2], pre[...])
        ups[t % 2] = value.astype(BF)
        save_tile(t).start()
        gain_ref[:, strip(t)] = row_sums(value * w_up[strip(t), :].astype(F32))
        return carry

    half = count // 2
    lax.fori_loop(0, half, weight, 0)
    net.two(0)
    lax.fori_loop(half, count, weight, 0)
    net.two(1)
    net.each(net.three)
    net.each(net.four)
    out = local(dnorm, dnorm_hbm, stores.at[0])
    out.start()
    out.wait()
    save_tile(count - 2).wait()
    save_tile(count - 1).wait()
    net.drain()


def middle(pre, w_up, normed):
    seq, inner = pre.shape
    width = w_up.shape[0]
    rows = seq // 8
    tile = 256
    hbm, vmem = pl.BlockSpec(memory_space=HBM_SPACE), pl.BlockSpec(memory_space=VMEM_SPACE)
    shape = jax.ShapeDtypeStruct
    return pl.pallas_call(
        middle_body, name="middle_layer",
        in_specs=[hbm] * 3,
        out_specs=[hbm] * 2 + [vmem],
        out_shape=[shape((rows, width), F32), shape((width, inner), BF), shape((1, width), F32)],
        scratch_shapes=[
            pltpu.VMEM((seq, inner), BF), pltpu.VMEM((width, inner), BF),
            pltpu.VMEM((2, seq, tile), BF), pltpu.VMEM((2, tile, inner), BF), pltpu.VMEM((rows, width), F32),
            pltpu.SemaphoreType.DMA((4,)), pltpu.SemaphoreType.DMA((3,)),
        ] + scatter_scratch(rows, width, 2),
        compiler_params=pltpu.CompilerParams(collective_id=5, has_side_effects=True, vmem_limit_bytes=56 * MIB),
        cost_estimate=pl.CostEstimate(flops=45 * 10**9, bytes_accessed=200 * MIB, transcendentals=0),
    )(pre, w_up, normed)


def turn_body(
    heads, dnorm_hbm, attn_hbm, tok_hbm, grad_hbm, w_out_hbm, qkv_hbm, mixed_hbm, gain_ref, lse_ref, seg_ref, valid_ref,
    branch_hbm, dqkv_hbm, residual_hbm,
    own, attn, tok, grad, w_out, qkv, mixed, dmixed, dqkv, rk_ref, ck_ref, ks, vs, dks, dvs, loads, stores, bbuf, bsend, brecv,
):
    core, sib, first, second = neighbours()
    rows, width = tok.shape
    local = pltpu.make_async_copy
    fetch = [
        local(source, target, loads.at[i])
        for i, (source, target) in enumerate((
            (dnorm_hbm, own), (attn_hbm, attn), (tok_hbm, tok), (grad_hbm, grad), (w_out_hbm, w_out), (qkv_hbm, qkv),
            (mixed_hbm, mixed),
        ))
    ]
    for one in fetch:
        one.start()
    greet(sib, first, second)
    for one in fetch[:4]:
        one.wait()

    def norm(part):
        residual = tok[part, :].astype(F32) + attn[part, :]
        total = grad[part, :].astype(F32) + norm_back(residual, gain_ref[...], own[part, :])
        own[part, :] = total
        bbuf[0, part, :] = total.astype(BF)

    rows_loop(rows, 32, norm)
    ring = Gather(bbuf, bsend, brecv, sib, first, second)
    ring.start()
    residual_out = local(own, residual_hbm, stores.at[0])
    residual_out.start()
    fill_keys(seg_ref, valid_ref, rk_ref, ck_ref)
    fetch[4].wait()

    def moved(s):
        return local(bbuf.at[s], branch_hbm.at[pl.ds(pl.multiple_of(s * rows, rows), rows)], stores.at[2 + s])

    def slot(s, carry):
        moved(s).start()
        dmixed[pl.ds(pl.multiple_of(s * rows, rows), rows), :] = dot_nt(bbuf[s], w_out[...]).astype(BF)
        return carry

    ring.pair()
    lax.fori_loop(0, 2, slot, 0)
    ring.forward()
    ring.middle()
    lax.fori_loop(2, 6, slot, 0)
    ring.finish()
    lax.fori_loop(6, 8, slot, 0)
    fetch[5].wait()
    fetch[6].wait()

    def head(h, carry):
        def load(ref, k):
            return lambda at: ref[pl.ds(at, rows), pl.ds(pl.multiple_of((k * heads + h) * HD, HD), HD)]

        def save(k):
            def put(at, value):
                dqkv[pl.ds(at, rows), pl.ds(pl.multiple_of((k * heads + h) * HD, HD), HD)] = value
            return put

        unattend_head(
            rows, 8, lambda a: block_place(a, rows), load(qkv, 0), load(qkv, 1), load(qkv, 2), load(dmixed, 0), load(mixed, 0),
            lambda a: lse_ref[h, a * rows:(a + 1) * rows, :], rk_ref, ck_ref, save(0), save(1), save(2), ks, vs, dks, dvs,
        )
        return carry

    lax.fori_loop(0, heads, head, 0)
    dqkv_out = local(dqkv, dqkv_hbm, stores.at[1])
    dqkv_out.start()
    for s in range(8):
        moved(s).wait()
    residual_out.wait()
    dqkv_out.wait()
    ring.drain()


def turn(dnorm, attn_own, tokens, grad_out, w_out, qkv, mixed, gain, lse, segment, valid, heads):
    rows, width = tokens.shape
    seq = 8 * rows
    hbm, vmem = pl.BlockSpec(memory_space=HBM_SPACE), pl.BlockSpec(memory_space=VMEM_SPACE)
    shape = jax.ShapeDtypeStruct
    cols = heads * HD
    return pl.pallas_call(
        functools.partial(turn_body, heads), name="turn_layer",
        in_specs=[hbm] * 7 + [vmem] * 4,
        out_specs=[hbm] * 3,
        out_shape=[shape((seq, width), BF), shape((seq, 3 * cols), BF), shape((rows, width), F32)],
        scratch_shapes=[
            pltpu.VMEM((rows, width), F32), pltpu.VMEM((rows, width), F32), pltpu.VMEM((rows, width), BF),
            pltpu.VMEM((rows, width), BF), pltpu.VMEM((cols, width), BF), pltpu.VMEM((seq, 3 * cols), BF),
            pltpu.VMEM((seq, cols), BF), pltpu.VMEM((seq, cols), BF), pltpu.VMEM((seq, 3 * cols), BF),
            pltpu.VMEM((seq, 128), F32), pltpu.VMEM((1, seq), F32),
            pltpu.VMEM((seq, HD), BF), pltpu.VMEM((seq, HD), BF), pltpu.VMEM((seq, HD), F32), pltpu.VMEM((seq, HD), F32),
            pltpu.SemaphoreType.DMA((7,)), pltpu.SemaphoreType.DMA((10,)),
        ] + gather_scratch(rows, width),
        compiler_params=pltpu.CompilerParams(collective_id=3, has_side_effects=True, vmem_limit_bytes=60 * MIB),
        cost_estimate=pl.CostEstimate(flops=45 * 10**9, bytes_accessed=200 * MIB, transcendentals=0),
    )(dnorm, attn_own, tokens, grad_out, w_out, qkv, mixed, gain[None, :], lse, segment[None, :], valid[None, :])


def weights_body(normed_ref, branch_ref, dqkv_ref, mixed_ref, wq_ref, wk_ref, wv_ref, out_ref, gain_ref):
    cols = wq_ref.shape[1]
    value = dot_tn(normed_ref[...], dqkv_ref[...])
    out_ref[:, :3 * cols] = value.astype(BF)
    out_ref[:, 3 * cols:] = dot_tn(mixed_ref[...], branch_ref[...]).astype(BF)
    gain_ref[...] = sum(
        row_sums(value[:, k * cols:(k + 1) * cols] * w_ref[...].astype(F32))
        for k, w_ref in enumerate((wq_ref, wk_ref, wv_ref))
    )


def down_body(hidden_ref, grad_ref, out_ref):
    out_ref[...] = dot_tn(hidden_ref[...], grad_ref[...]).astype(BF)


def down_weights(hidden, grads):
    seq, inner = hidden.shape
    width = grads.shape[1]
    tile = 512
    return pl.pallas_call(
        down_body, name="down_weights", grid=(width // tile,),
        in_specs=[pl.BlockSpec((seq, inner), lambda t: (0, 0)), pl.BlockSpec((seq, tile), lambda t: (0, t))],
        out_specs=pl.BlockSpec((inner, tile), lambda t: (0, t)),
        out_shape=jax.ShapeDtypeStruct((inner, width), BF),
        compiler_params=pltpu.CompilerParams(vmem_limit_bytes=63 * MIB),
        cost_estimate=pl.CostEstimate(flops=2 * seq * width * inner, bytes_accessed=16 * MIB, transcendentals=0),
    )(hidden, grads)


def weights(normed, branch, dqkv, mixed, w_query, w_key, w_value):
    seq, width = normed.shape
    cols = w_query.shape[1]
    tile = cols
    full = lambda c: pl.BlockSpec((seq, c), lambda t: (0, 0))
    strip = pl.BlockSpec((seq, tile), lambda t: (0, t))
    rows = pl.BlockSpec((tile, cols), lambda t: (t, 0))
    return pl.pallas_call(
        weights_body, name="weight_gradients", grid=(width // tile,),
        in_specs=[strip, strip, full(3 * cols), full(cols), rows, rows, rows],
        out_specs=[pl.BlockSpec((tile, 4 * cols), lambda t: (t, 0)), pl.BlockSpec((1, tile), lambda t: (0, t))],
        out_shape=[jax.ShapeDtypeStruct((width, 4 * cols), BF), jax.ShapeDtypeStruct((1, width), F32)],
        compiler_params=pltpu.CompilerParams(vmem_limit_bytes=63 * MIB),
        cost_estimate=pl.CostEstimate(flops=2 * seq * width * 4 * cols, bytes_accessed=30 * MIB, transcendentals=0),
    )(normed, branch, dqkv, mixed, w_query, w_key, w_value)


class Total:
    def __init__(self, vec, got, sends, recvs, sib, first, second):
        self.vec, self.got = vec, got
        self.partners = [sib, first, second]
        self.copies = [
            pltpu.make_async_remote_copy(
                src_ref=vec, dst_ref=got.at[k], send_sem=sends.at[k], recv_sem=recvs.at[k], device_id=other, device_id_type=MESH,
            )
            for k, other in enumerate(self.partners)
        ]

    def start(self, k):
        self.copies[k].start()

    def add(self, k):
        self.copies[k].wait()
        self.vec[...] += self.got[k]
        if k + 1 < len(self.copies):
            self.copies[k + 1].start()


def finish_body(
    hidden_hbm, w_down_hbm, dqkv_hbm, wq_hbm, wk_hbm, wv_hbm, tok_hbm, attn_hbm, gres_hbm, gain_ref, part_attn_ref, part_mlp_ref,
    valid_ref, tokens_hbm, grads_hbm, total_ref,
    hidden, w_down, dqkv, w_qkv, tok, attn, gres, out, mlp, dnorm, vec, got, sends, recvs, loads, stores, *scatter,
):
    core, sib, first, second = neighbours()
    rows, width = mlp.shape
    cols = wq_hbm.shape[1]
    local = pltpu.make_async_copy
    pairs = [(hidden_hbm, hidden), (w_down_hbm, w_down), (dqkv_hbm, dqkv)]
    pairs += [(w, w_qkv.at[:, pl.ds(k * cols, cols)]) for k, w in enumerate((wq_hbm, wk_hbm, wv_hbm))]
    pairs += [(tok_hbm, tok), (attn_hbm, attn), (gres_hbm, gres)]
    fetch = [local(source, target, loads.at[i]) for i, (source, target) in enumerate(pairs)]
    for one in fetch:
        one.start()
    total = Total(vec, got, sends, recvs, sib, first, second)
    greet(*total.partners)

    def at(p):
        return pl.ds(pl.multiple_of(p * rows, rows), rows)

    def down(p, col):
        return dot_nn(hidden[at(p), :], w_down[:, pl.ds(col, late.step)])

    def project_back(p, col):
        return dot_nt(dqkv[at(p), :], w_qkv[pl.ds(col, net.step), :])

    late = Scatter(down, mlp, scatter[:8], scatter[8:10], core, sib, first, second)
    net = Scatter(project_back, dnorm, scatter[10:18], scatter[18:], core, sib, first, second)
    fetch[0].wait()
    fetch[1].wait()
    late.each(late.away)
    late.each(late.one)
    for one in fetch[2:]:
        one.wait()
    net.each(net.away)
    net.each(net.one)
    for stage in (late.two, late.three, late.four):
        late.each(stage)

    own = pl.ds(pl.multiple_of((lax.axis_index("dp") * 8 + lax.axis_index("mp")) * rows, rows), rows)
    mask = jnp.transpose(jnp.broadcast_to(valid_ref[:, own].astype(F32), (128, rows)))
    vec[...] = jnp.zeros_like(vec)
    vec[0:1, :] = part_attn_ref[...]
    vec[1:2, :] = part_mlp_ref[...]
    step = 64
    for i in range(0, rows, step):
        part = slice(i, i + step)
        attn_part, mlp_part = attn[part, :], mlp[part, :]
        stream = tok[part, :].astype(F32) + attn_part + mlp_part
        out[0, part, :] = stream.astype(BF)
        for k, value in enumerate((stream, attn_part, mlp_part)):
            vec[2 + k:3 + k, :] += jnp.sum(mask[part, 0:1] * value * value, axis=0, keepdims=True)
    tokens_out = local(out.at[0], tokens_hbm, stores.at[0])
    tokens_out.start()
    total.start(0)
    net.each(net.two)
    total.add(0)
    net.each(net.three)
    total.add(1)
    net.each(net.four)

    def last(part):
        back = norm_back(tok[part, :].astype(F32), gain_ref[...], dnorm[part, :])
        out[1, part, :] = (gres[part, :] + back).astype(BF)

    rows_loop(rows, 32, last)
    grads_out = local(out.at[1], grads_hbm, stores.at[1])
    grads_out.start()
    total.add(2)
    total_ref[...] = vec[...]
    tokens_out.wait()
    grads_out.wait()
    net.drain()
    late.drain()


def finish(hidden, w_down, dqkv, w_query, w_key, w_value, tokens, attn_own, grad_residual, gain, part_attn, part_mlp, valid):
    seq, inner = hidden.shape
    rows, width = tokens.shape
    cols = w_query.shape[1]
    stages = 3
    hbm, vmem = pl.BlockSpec(memory_space=HBM_SPACE), pl.BlockSpec(memory_space=VMEM_SPACE)
    shape = jax.ShapeDtypeStruct
    return pl.pallas_call(
        finish_body, name="last_scatters",
        in_specs=[hbm] * 9 + [vmem] * 4,
        out_specs=[hbm] * 2 + [vmem],
        out_shape=[shape((rows, width), BF), shape((rows, width), BF), shape((8, width), F32)],
        scratch_shapes=[
            pltpu.VMEM((seq, inner), BF), pltpu.VMEM((inner, width), BF), pltpu.VMEM((seq, 3 * cols), BF),
            pltpu.VMEM((width, 3 * cols), BF), pltpu.VMEM((rows, width), BF), pltpu.VMEM((rows, width), F32),
            pltpu.VMEM((rows, width), F32), pltpu.VMEM((2, rows, width), BF), pltpu.VMEM((rows, width), F32),
            pltpu.VMEM((rows, width), F32), pltpu.VMEM((8, width), F32), pltpu.VMEM((stages, 8, width), F32),
            pltpu.SemaphoreType.DMA((stages,)), pltpu.SemaphoreType.DMA((stages,)),
            pltpu.SemaphoreType.DMA((9,)), pltpu.SemaphoreType.DMA((2,)),
        ] + scatter_scratch(rows, width, 2) * 2,
        compiler_params=pltpu.CompilerParams(collective_id=4, has_side_effects=True, vmem_limit_bytes=63 * MIB),
        cost_estimate=pl.CostEstimate(flops=30 * 10**9, bytes_accessed=200 * MIB, transcendentals=0),
    )(hidden, w_down, dqkv, w_query, w_key, w_value, tokens, attn_own, grad_residual, gain[None, :], part_attn, part_mlp,
      valid[None, :])


def after(value, *others):
    return lax.optimization_barrier((value,) + others)[0]


def over_mp(value):
    return lax.all_gather(value, "mp", axis=0, tiled=True)


def sum_mp(value):
    return lax.psum_scatter(value.astype(BF), "mp", scatter_dimension=0, tiled=True).astype(F32)


def sum_dp(value, axis):
    return lax.psum_scatter(value.astype(BF), "dp", scatter_dimension=axis, tiled=True)


def on_device(tokens, segment, valid, gain_attn, w_query, w_key, w_value, w_out, gain_mlp, w_up, w_down, grad_out):
    own_rows, width = tokens.shape
    seq_rows = segment.shape[0]
    heads = w_query.shape[1] // HD
    n_dp, n_mp = lax.axis_size("dp"), lax.axis_size("mp")
    dp, me = lax.axis_index("dp"), lax.axis_index("mp")
    cube = n_mp == 8 and n_dp & (n_dp - 1) == 0
    order = jnp.arange(seq_rows // own_rows, dtype=jnp.int32)
    valid_group = lax.dynamic_slice_in_dim(valid, dp * seq_rows, seq_rows)
    valid_own = lax.dynamic_slice_in_dim(valid_group, me * own_rows, own_rows)
    tokens32 = tokens.astype(F32)

    if cube:
        qkv, normed = project(tokens, gain_attn, w_query, w_key, w_value)
        mixed, lse, attn_own, normed_mlp, hidden, grad_pre, grad_rows = forward(
            qkv, grad_out, tokens, w_out, w_up, w_down, gain_mlp, segment, valid, heads
        )
    else:
        row_key = segment[:, None]
        col_key = jnp.where(valid_group > 0, segment, -1)[None, :]
        normed = over_mp(norm_rows(tokens32, gain_attn).astype(BF))
        qkv = jnp.concatenate([dot_nn(normed, w).astype(BF) for w in (w_query, w_key, w_value)], 1)
        mixed, lse = attn_fwd(qkv, order, row_key, col_key, heads, own_rows)
        grad_rows = over_mp(after(grad_out, qkv))
        attn_own = sum_mp(dot_nn(mixed, w_out))
        normed_mlp = over_mp(norm_rows(tokens32 + attn_own, gain_mlp).astype(BF))
        hidden = gelu_fn(dot_nn(normed_mlp, w_up)).astype(BF)
    residual = tokens32 + attn_own

    if cube:
        part_down = down_weights(hidden, grad_rows)
        sum_down = sum_dp(part_down, 1)
        grad_normed, part_up, gain_mlp_part = middle(after(grad_pre, part_down), w_up, normed_mlp)
        sum_up = sum_dp(part_up, 0)
        grad_branch, grads_qkv, grad_residual = turn(
            grad_normed, attn_own, tokens, grad_out, w_out, qkv, mixed, gain_mlp, lse, segment, valid, heads
        )
        grads_qkv, sum_down = lax.optimization_barrier((grads_qkv, sum_down))
        part_last, gain_attn_part = weights(normed, grad_branch, grads_qkv, mixed, w_query, w_key, w_value)
        grad_down = after(sum_down, part_last).astype(F32)
        grads_qkv = after(grads_qkv, part_last, grad_down)
        grad_last = sum_dp(part_last, 0)
        cols = heads * HD
        grad_qkv = grad_last[:, :3 * cols].astype(F32)
        grad_out_proj = jnp.concatenate(
            [grad_last[i:i + cols, 3 * cols:] for i in range(0, grad_last.shape[0], cols)], 1
        ).astype(F32)
        out_tokens, grad_tokens, summed = finish(
            hidden, w_down, grads_qkv, w_query, w_key, w_value, tokens, attn_own, grad_residual, gain_attn,
            gain_attn_part, gain_mlp_part, valid
        )
        grad_up = after(sum_up, out_tokens).astype(F32)
        bit = 1
        while bit < n_dp:
            if bit == 2:
                summed, grad_up = lax.optimization_barrier((summed, grad_up))
            summed = summed + lax.ppermute(summed, "dp", [(i, i ^ bit) for i in range(n_dp)])
            bit *= 2
    else:
        grad_down = sum_dp(dot_tn(hidden, grad_rows), 1).astype(F32)
        grad_pre = (gelu_pair(dot_nn(normed_mlp, w_up))[1] * dot_nt(grad_rows, w_down)).astype(BF)
        part_up = dot_tn(normed_mlp, grad_pre)
        grad_up = sum_dp(part_up, 0).astype(F32)
        gain_mlp_part = jnp.sum(part_up * w_up.astype(F32), axis=1)
        grad_residual = grad_out.astype(F32) + norm_back(residual, gain_mlp, sum_mp(dot_nt(grad_pre, w_up)))
        grad_branch = over_mp(grad_residual.astype(BF))
        grad_mixed = dot_nt(grad_branch, w_out).astype(BF)
        grads_qkv = jnp.concatenate(attn_bwd(qkv, grad_mixed, mixed, lse, order, row_key, col_key, heads, own_rows), 1)
        grad_out_proj = sum_dp(dot_tn(mixed, grad_branch), 1).astype(F32)
        part_qkv = dot_tn(normed, grads_qkv)
        grad_qkv = sum_dp(part_qkv, 0).astype(F32)
        w_qkv = jnp.concatenate([w_query, w_key, w_value], 1)
        gain_attn_part = jnp.sum(part_qkv * w_qkv.astype(F32), axis=1)
        mlp_own = sum_mp(dot_nn(hidden, w_down))
        grad_normed_attn = sum_mp(dot_nt(grads_qkv, w_qkv))
        stream = residual + mlp_own
        out_tokens = stream.astype(BF)
        grad_tokens = (grad_residual + norm_back(tokens32, gain_attn, grad_normed_attn)).astype(BF)
        mask_own = valid_own.astype(F32)[:, None]
        squares = [jnp.sum(mask_own * part * part, axis=0) for part in (stream, attn_own, mlp_own)]
        summed = lax.psum(jnp.stack([gain_attn_part, gain_mlp_part, *squares]), ("dp", "mp"))
    counted = jnp.maximum(jnp.sum(valid).astype(F32) * width, 1.0)
    gain_rows = width // (n_dp * n_mp)
    place = (dp * n_mp + me) * gain_rows
    rms = jnp.sqrt(jnp.sum(summed[2:5], axis=1) / counted)
    gains = [
        lax.dynamic_slice_in_dim(summed[k], place, gain_rows) / lax.dynamic_slice_in_dim(gain, place, gain_rows)
        for k, gain in enumerate((gain_attn, gain_mlp))
    ]
    shard = heads * HD
    return (
        out_tokens,
        grad_tokens,
        gains[0],
        grad_qkv[:, :shard],
        grad_qkv[:, shard:2 * shard],
        grad_qkv[:, 2 * shard:],
        grad_out_proj,
        gains[1],
        grad_up,
        grad_down,
        rms[0],
        rms[1],
        rms[2],
    )


def solution(mesh):
    tokens_spec = P(("dp", "mp"), None)
    cols, rows = P(None, "mp"), P("mp", None)
    return jax.shard_map(
        on_device,
        mesh=mesh,
        in_specs=(tokens_spec, P("dp"), P(), P(), cols, cols, cols, rows, P(), cols, rows, tokens_spec),
        out_specs=(
            tokens_spec,
            tokens_spec,
            P(("dp", "mp")),
            P("dp", "mp"),
            P("dp", "mp"),
            P("dp", "mp"),
            P("mp", "dp"),
            P(("dp", "mp")),
            P("dp", "mp"),
            P("mp", "dp"),
            P(),
            P(),
            P(),
        ),
        check_vma=False,
    )
```

```python
import functools

import jax
import jax.numpy as jnp
from jax import lax
from jax.experimental import pallas as pl
from jax.experimental.pallas import tpu as pltpu
from jax.sharding import PartitionSpec as P

HD = 128
NEGATIVE = -1e30
LOG2E = 1.4426950408889634
EPSILON = 1e-05
BF = jnp.bfloat16
F32 = jnp.float32
MIB = 2**20


def dot_nn(a, b):
    return jnp.dot(a, b, preferred_element_type=F32)


def dot_tn(a, b):
    return lax.dot_general(a, b, (((0,), (0,)), ((), ())), preferred_element_type=F32)


def dot_nt(a, b):
    return lax.dot_general(a, b, (((1,), (1,)), ((), ())), preferred_element_type=F32)


def diagonal(blk):
    rows = lax.broadcasted_iota(jnp.int32, (blk, blk), 0)
    cols = lax.broadcasted_iota(jnp.int32, (blk, blk), 1)
    return cols < rows, cols == rows


def attend_head(blk, count, place, queries, keys, values, rk_ref, ck_ref, put_mixed, put_lse, ks, vs):
    c = HD ** -0.5 * LOG2E
    for a in range(count):
        ks[a * blk:(a + 1) * blk, :] = keys(place(a))
        vs[a * blk:(a + 1) * blk, :] = values(place(a))
    earlier, itself = diagonal(blk)
    for a in range(count):
        end = (a + 1) * blk
        low = end - blk
        s = dot_nt(queries(place(a)), ks[:end, :])
        ok = rk_ref[low:end, 0:1] == ck_ref[:, :end]
        sd = jnp.where((ok[:, low:] & earlier) | itself, s[:, low:], NEGATIVE)
        m = jnp.max(sd, axis=1, keepdims=True)
        if a:
            so = jnp.where(ok[:, :low], s[:, :low], NEGATIVE)
            m = jnp.maximum(m, jnp.max(so, axis=1, keepdims=True))
        pd = jnp.exp2((sd - m) * c)
        total = jnp.sum(pd, axis=1, keepdims=True)
        o = dot_nn(pd.astype(BF), vs[low:end, :])
        if a:
            po = jnp.exp2((so - m) * c)
            total += jnp.sum(po, axis=1, keepdims=True)
            o += dot_nn(po.astype(BF), vs[:low, :])
        put_mixed(place(a), (o / total).astype(BF))
        put_lse(a, m * c + jnp.log2(total))


def attn_fwd_body(blk, count, order_ref, q_ref, k_ref, v_ref, rk_ref, ck_ref, mix_ref, lse_ref, ks, vs):
    def place(a):
        return pl.multiple_of(order_ref[a] * blk, blk)

    def put_mixed(at, value):
        mix_ref[pl.ds(at, blk), :] = value

    def put_lse(a, value):
        lse_ref[0, a * blk:(a + 1) * blk, :] = value

    attend_head(
        blk, count, place, lambda at: q_ref[pl.ds(at, blk), :], lambda at: k_ref[pl.ds(at, blk), :],
        lambda at: v_ref[pl.ds(at, blk), :], rk_ref, ck_ref, put_mixed, put_lse, ks, vs,
    )


def attn_fwd(qkv, order, rowkey, colkey, heads, blk):
    seq = qkv.shape[0]
    part = lambda off: pl.BlockSpec((seq, HD), lambda h, o: (0, off * heads + h))
    return pl.pallas_call(
        functools.partial(attn_fwd_body, blk, seq // blk), name="attn_fwd",
        grid_spec=pltpu.PrefetchScalarGridSpec(
            num_scalar_prefetch=1, grid=(heads,),
            in_specs=[part(0), part(1), part(2), pl.BlockSpec((seq, 1), lambda h, o: (0, 0)),
                      pl.BlockSpec((1, seq), lambda h, o: (0, 0))],
            out_specs=[part(0), pl.BlockSpec((1, seq, 1), lambda h, o: (h, 0, 0))],
            scratch_shapes=[pltpu.VMEM((seq, HD), BF)] * 2),
        out_shape=[jax.ShapeDtypeStruct((seq, heads * HD), BF), jax.ShapeDtypeStruct((heads, seq, 1), F32)],
        compiler_params=pltpu.CompilerParams(vmem_limit_bytes=48 * MIB),
        cost_estimate=pl.CostEstimate(
            flops=2 * seq * seq * HD * heads, bytes_accessed=8 * seq * HD * heads, transcendentals=seq * seq * heads // 2),
    )(order, qkv, qkv, qkv, rowkey, colkey)


def unattend_head(blk, count, place, queries, keys, values, grads, mixes, lses, rk_ref, ck_ref, put_q, put_k, put_v, ks, vs, dks, dvs,
                  between=None):
    scale = HD ** -0.5
    c = scale * LOG2E
    for a in range(count):
        ks[a * blk:(a + 1) * blk, :] = keys(place(a))
        vs[a * blk:(a + 1) * blk, :] = values(place(a))
    earlier, itself = diagonal(blk)

    def add(ref, lo, hi, value, fresh):
        if fresh:
            ref[lo:hi, :] = value
        else:
            ref[lo:hi, :] += value

    for a in reversed(range(count)):
        end = (a + 1) * blk
        low = end - blk
        fresh = a == count - 1
        at = place(a)
        q, do = queries(at), grads(at)
        delta = jnp.sum(do.astype(F32) * mixes(at).astype(F32), axis=1, keepdims=True)
        p = jnp.exp2(dot_nt(q, ks[:end, :]) * c - lses(a))
        dp = dot_nt(do, vs[:end, :])
        ok = rk_ref[low:end, 0:1] == ck_ref[:, :end]
        pd = jnp.where((ok[:, low:] & earlier) | itself, p[:, low:], 0.0)
        dsd = (pd * (dp[:, low:] - delta)).astype(BF)
        dq = dot_nn(dsd, ks[low:end, :])
        add(dks, low, end, dot_tn(dsd, q), fresh)
        add(dvs, low, end, dot_tn(pd.astype(BF), do), fresh)
        if a:
            po = jnp.where(ok[:, :low], p[:, :low], 0.0)
            dso = (po * (dp[:, :low] - delta)).astype(BF)
            dq += dot_nn(dso, ks[:low, :])
            add(dks, 0, low, dot_tn(dso, q), fresh)
            add(dvs, 0, low, dot_tn(po.astype(BF), do), fresh)
        put_q(at, (dq * scale).astype(BF))
        if between is not None:
            between(a)
    for a in range(count):
        put_k(place(a), (dks[a * blk:(a + 1) * blk, :] * scale).astype(BF))
        put_v(place(a), dvs[a * blk:(a + 1) * blk, :].astype(BF))


def attn_bwd_body(blk, count, order_ref, q_ref, k_ref, v_ref, do_ref, mix_ref, lse_ref, rk_ref, ck_ref, dq_ref, dk_ref, dv_ref,
                  ks, vs, dks, dvs):
    def place(a):
        return pl.multiple_of(order_ref[a] * blk, blk)

    def load(ref):
        return lambda at: ref[pl.ds(at, blk), :]

    def save(ref):
        def put(at, value):
            ref[pl.ds(at, blk), :] = value
        return put

    unattend_head(
        blk, count, place, load(q_ref), load(k_ref), load(v_ref), load(do_ref), load(mix_ref),
        lambda a: lse_ref[0, a * blk:(a + 1) * blk, :], rk_ref, ck_ref, save(dq_ref), save(dk_ref), save(dv_ref), ks, vs, dks, dvs,
    )


def attn_bwd(qkv, do, mixed, lse, order, rowkey, colkey, heads, blk):
    seq = qkv.shape[0]
    part = lambda off: pl.BlockSpec((seq, HD), lambda h, o: (0, off * heads + h))
    return pl.pallas_call(
        functools.partial(attn_bwd_body, blk, seq // blk), name="attn_bwd",
        grid_spec=pltpu.PrefetchScalarGridSpec(
            num_scalar_prefetch=1, grid=(heads,),
            in_specs=[part(0), part(1), part(2), part(0), part(0), pl.BlockSpec((1, seq, 1), lambda h, o: (h, 0, 0)),
                      pl.BlockSpec((seq, 1), lambda h, o: (0, 0)), pl.BlockSpec((1, seq), lambda h, o: (0, 0))],
            out_specs=[part(0), part(0), part(0)],
            scratch_shapes=[pltpu.VMEM((seq, HD), BF)] * 2 + [pltpu.VMEM((seq, HD), F32)] * 2),
        out_shape=[jax.ShapeDtypeStruct((seq, heads * HD), BF)] * 3,
        compiler_params=pltpu.CompilerParams(vmem_limit_bytes=56 * MIB),
        cost_estimate=pl.CostEstimate(
            flops=5 * seq * seq * HD * heads, bytes_accessed=16 * seq * HD * heads, transcendentals=seq * seq * heads // 2),
    )(order, qkv, qkv, qkv, do, mixed, lse, rowkey, colkey)


def row_scale(values):
    return lax.rsqrt(jnp.mean(values * values, axis=-1, keepdims=True) + EPSILON)


def norm_rows(values, norm_gain):
    return values * row_scale(values) * norm_gain


def norm_back(values, norm_gain, grad_norm):
    scale = row_scale(values)
    normal = values * scale
    grad_hat = grad_norm * norm_gain
    inner = jnp.mean(grad_hat * normal, axis=-1, keepdims=True)
    return scale * (grad_hat - normal * inner)


def gelu_fn(values):
    return jax.nn.gelu(values, approximate=True)


MESH = pl.DeviceIdType.MESH
HBM_SPACE = pl.ANY
VMEM_SPACE = pltpu.VMEM


def neighbours():
    dp, me = lax.axis_index("dp"), lax.axis_index("mp")
    core, along_x, along_y = me % 2, (me // 2) % 2, me // 4
    by_x, by_y = me + 2 - 4 * along_x, me + 4 - 8 * along_y
    first = (1 - core) * by_y + core * by_x
    second = (1 - core) * by_x + core * by_y
    return core, (dp, me + 1 - 2 * core), (dp, first), (dp, second)


def greet(*others):
    barrier = pltpu.get_barrier_semaphore()
    for other in others:
        pl.semaphore_signal(barrier, inc=1, device_id=other, device_id_type=MESH)
    pl.semaphore_wait(barrier, len(others))


class Gather:
    COPIES = 11

    def __init__(self, buf, sends, recvs, sib, first, second):
        rows = buf.shape[1]
        low, high, whole = pl.ds(0, rows // 2), pl.ds(rows // 2, rows // 2), pl.ds(0, rows)

        def copy(i, source, target, part, device):
            return pltpu.make_async_remote_copy(
                src_ref=buf.at[source, part], dst_ref=buf.at[target, part],
                send_sem=sends.at[i], recv_sem=recvs.at[i], device_id=device, device_id_type=MESH,
            )

        self.copies = [
            copy(0, 0, 4, high, first), copy(1, 0, 4, low, first),
            copy(2, 0, 2, low, second), copy(3, 0, 2, high, second),
            copy(4, 0, 1, whole, sib),
            copy(5, 2, 6, low, first), copy(6, 4, 6, high, second),
            copy(7, 4, 3, whole, sib), copy(8, 2, 5, whole, sib),
            copy(9, 6, 7, low, sib), copy(10, 6, 7, high, sib),
        ]

    def start(self):
        for i in (0, 2, 1, 3, 4):
            self.copies[i].start()

    def pair(self):
        self.copies[4].wait_recv()

    def forward(self, both=True):
        for arrived, onward in ((2, 5), (0, 6)):
            self.copies[arrived].wait_recv()
            if both:
                self.copies[onward].start()
        for arrived, onward in ((1, 7), (3, 8)):
            self.copies[arrived].wait_recv()
            self.copies[onward].start()

    def onward(self):
        self.copies[5].start()
        self.copies[6].start()

    def middle(self):
        self.copies[7].wait_recv()
        self.copies[8].wait_recv()

    def finish(self):
        for arrived, onward in ((5, 9), (6, 10)):
            self.copies[arrived].wait_recv()
            self.copies[onward].start()
        self.copies[9].wait_recv()
        self.copies[10].wait_recv()

    def drain(self):
        for one in self.copies:
            one.wait_send()

class Scatter:
    def __init__(self, product, own_ref, bufs, sems, core, sib, first, second):
        self.product, self.own_ref, self.core = product, own_ref, core
        self.sent = 0
        self.away_ref, self.r0, self.s1, self.r1, self.s2, self.r2, self.s3, self.r3 = bufs
        self.chunks, _, self.rows, self.step = self.away_ref.shape
        self.half = self.chunks * self.step
        sends, recvs = sems

        def copy(source, target, j, k, device):
            return pltpu.make_async_remote_copy(
                src_ref=source.at[j], dst_ref=target.at[j], send_sem=sends.at[j, k], recv_sem=recvs.at[j, k],
                device_id=device, device_id_type=MESH,
            )

        self.copies = [
            [copy(self.away_ref, self.r0, j, 0, sib), copy(self.s1, self.r1, j, 1, first),
             copy(self.s2, self.r2, j, 2, second), copy(self.s3, self.r3, j, 3, sib)]
            for j in range(self.chunks)
        ]

    def column(self, j, core):
        return pl.multiple_of(core * self.half + j * self.step, self.step)

    def away(self, j):
        col = self.column(j, 1 - self.core)

        def some(p, carry):
            self.away_ref[j, p] = self.product(p, col).astype(BF)
            return carry

        lax.fori_loop(0, 8, some, 0)
        self.copies[j][0].start()

    def kept(self, j, p):
        came = 4 * ((p // 2) % 2) + 2 * (p // 4) + 1 - p % 2
        return self.product(p, self.column(j, self.core)) + self.r0[j, came].astype(F32)

    def one(self, j, go=True):
        self.copies[j][0].wait_recv()

        def some(p, carry):
            self.s1[j, p - 4] = self.kept(j, p).astype(BF)
            return carry

        lax.fori_loop(4, 8, some, 0)
        if go:
            self.go(j)

    def go(self, j):
        self.copies[j][1].start()

    def two(self, j):
        self.copies[j][1].wait_recv()

        def some(p, carry):
            self.s2[j, p - 2] = (self.kept(j, p) + self.r1[j, p].astype(F32)).astype(BF)
            return carry

        lax.fori_loop(2, 4, some, 0)
        self.copies[j][2].start()

    def three(self, j):
        self.copies[j][2].wait_recv()

        def last(p):
            return self.kept(j, p) + self.r1[j, p].astype(F32) + self.r2[j, p].astype(F32)

        self.s3[j] = last(1).astype(BF)
        self.copies[j][3].start()
        self.own_ref[:, pl.ds(self.column(j, self.core), self.step)] = last(0)

    def four(self, j):
        self.copies[j][3].wait_recv()
        self.own_ref[:, pl.ds(self.column(j, 1 - self.core), self.step)] = self.r3[j].astype(F32)

    def each(self, stage):
        for j in range(self.chunks):
            stage(j)

    def release(self, j):
        self.copies[j][0].wait_send()
        self.sent = 1

    def drain(self):
        for copies in self.copies:
            for one in copies[self.sent:]:
                one.wait_send()


def scatter_scratch(rows, width, chunks):
    step = width // 2 // chunks
    sizes = [(8, rows, step)] * 2 + [(4, rows, step)] * 2 + [(2, rows, step)] * 2 + [(rows, step)] * 2
    return [pltpu.VMEM((chunks,) + size, BF) for size in sizes] + [pltpu.SemaphoreType.DMA((chunks, 4))] * 2


def gather_scratch(rows, width):
    return [pltpu.VMEM((8, rows, width), BF), pltpu.SemaphoreType.DMA((11,)), pltpu.SemaphoreType.DMA((11,))]


def rows_loop(rows, step, body):
    def some(i, carry):
        body(pl.ds(pl.multiple_of(i * step, step), step))
        return carry

    lax.fori_loop(0, rows // step, some, 0)


def block_place(a, rows):
    me = lax.axis_index("mp")
    core = me % 2
    by_c = (a % 2 + core) % 2
    by_x = (a // 2 + me // 2) % 2
    by_y = (a // 4 + me // 4) % 2
    position = 4 * (by_y + core * (by_x - by_y)) + 2 * (by_x + core * (by_y - by_x)) + by_c
    return pl.multiple_of(position * rows, rows)


def gelu_pair(x):
    c = 0.7978845608028654
    square = x * x
    t = jnp.tanh(c * (x + 0.044715 * (x * square)))
    upper = 0.5 * (1.0 + t)
    return x * upper, upper + 0.5 * x * (1.0 - t * t) * (c + (3 * 0.044715 * c) * square)


def fill_keys(seg_ref, valid_ref, rk, ck):
    seq = seg_ref.shape[1]
    here = pl.ds(pl.multiple_of(lax.axis_index("dp") * seq, seq), seq)
    numbers = seg_ref[...].astype(F32)
    ck[...] = jnp.where(valid_ref[:, here] > 0, numbers, -1.0)
    step = 256
    for i in range(0, seq, step):
        rk[i:i + step, :] = jnp.transpose(jnp.broadcast_to(numbers[:, i:i + step], (128, step)))


def forward_body(
    heads, tok_hbm, grad_hbm, wq_hbm, wk_hbm, wv_hbm, w_out_hbm, w_up_hbm, w_down_hbm, gain_attn_ref, gain_ref, seg_ref, valid_ref,
    qkv_hbm, first_hbm, mixed_hbm, lse_ref, attn_hbm, normed_hbm, hidden_hbm, pre_hbm, rows_hbm,
    qkv, w_out, w_up, w_down, mixed, own, hidden, pre, rk_ref, ck_ref, ks, vs, loads, stores,
    asend, arecv, nbuf, nsend, nrecv, gbuf, gsend, grecv, *scatter,
):
    core, sib, first, second = neighbours()
    rows, width = own.shape
    local = pltpu.make_async_copy
    cols = wq_hbm.shape[1]
    fetch = [
        local(grad_hbm, gbuf.at[0], loads.at[0]), local(tok_hbm, nbuf.at[0], loads.at[1]), local(w_out_hbm, w_out, loads.at[2]),
        local(tok_hbm, nbuf.at[0], loads.at[3]), local(w_up_hbm, w_up, loads.at[4]), local(w_down_hbm, w_down, loads.at[5]),
    ]
    projections = [
        local(w, w_up.at[:, pl.ds(k * cols, cols)], loads.at[6 + k]) for k, w in enumerate((wq_hbm, wk_hbm, wv_hbm))
    ]
    for one in [fetch[1], *projections, fetch[0], fetch[2], fetch[5]]:
        one.start()
    greet(sib, first, second)
    fetch[1].wait()

    def at(s):
        return pl.ds(pl.multiple_of(s * rows, rows), rows)

    def norm_first(part):
        nbuf[0, part, :] = norm_rows(nbuf[0, part, :].astype(F32), gain_attn_ref[...]).astype(BF)

    rows_loop(rows, 32, norm_first)
    opening = Gather(nbuf, asend, arecv, sib, first, second)
    opening.start()
    fill_keys(seg_ref, valid_ref, rk_ref, ck_ref)
    for one in projections:
        one.wait()

    def first_copy(s):
        return local(nbuf.at[s], first_hbm.at[at(s)], stores.at[14 + s])

    def projected(s, carry):
        first_copy(s).start()
        qkv[at(s), :] = dot_nn(nbuf[s], w_up[:, :3 * cols]).astype(BF)
        return carry

    opening.pair()
    lax.fori_loop(0, 2, projected, 0)
    opening.forward()
    opening.middle()
    lax.fori_loop(2, 6, projected, 0)
    opening.finish()
    fetch[0].wait()
    grads = Gather(gbuf, gsend, grecv, sib, first, second)
    grads.start()
    lax.fori_loop(6, 8, projected, 0)
    fetch[4].start()
    qkv_out = local(qkv, qkv_hbm, stores.at[22])
    qkv_out.start()

    def head(h, carry):
        def part(k):
            return lambda at: qkv[pl.ds(at, rows), pl.ds(pl.multiple_of((k * heads + h) * HD, HD), HD)]

        def put_mixed(at, value):
            mixed[pl.ds(at, rows), pl.ds(pl.multiple_of(h * HD, HD), HD)] = value

        def put_lse(a, value):
            lse_ref[h, a * rows:(a + 1) * rows, :] = value

        attend_head(rows, 8, lambda a: block_place(a, rows), part(0), part(1), part(2), rk_ref, ck_ref, put_mixed, put_lse, ks, vs)
        return carry

    lax.fori_loop(0, heads, head, 0)
    mixed_out = local(mixed, mixed_hbm, stores.at[0])
    mixed_out.start()

    def product(p, col):
        return dot_nn(mixed[pl.ds(pl.multiple_of(p * rows, rows), rows), :], w_out[:, pl.ds(col, net.step)])

    fetch[2].wait()
    net = Scatter(product, own, scatter[:8], scatter[8:], core, sib, first, second)
    net.each(net.away)
    for s in range(8):
        first_copy(s).wait()
    opening.drain()
    fetch[3].start()
    net.each(net.one)
    grads.pair()
    fetch[5].wait()
    net.each(net.release)
    slopes = net.away_ref
    tile = net.step

    def back(s, carry):
        for t in range(net.chunks):
            slopes[t, s] = dot_nt(gbuf[s], w_down[t * tile:(t + 1) * tile, :]).astype(BF)
        return carry

    lax.fori_loop(0, 2, back, 0)
    grads.forward(False)
    grads.middle()
    lax.fori_loop(2, 6, back, 0)
    net.each(net.two)
    net.each(net.three)
    grads.onward()
    net.each(net.four)
    attn_out = local(own, attn_hbm, stores.at[1])
    attn_out.start()

    fetch[3].wait()

    def norm(part):
        residual = nbuf[0, part, :].astype(F32) + own[part, :]
        nbuf[0, part, :] = norm_rows(residual, gain_ref[...]).astype(BF)

    rows_loop(rows, 32, norm)
    ring = Gather(nbuf, nsend, nrecv, sib, first, second)
    ring.start()
    fetch[4].wait()
    rows_out = [local(gbuf.at[s], rows_hbm.at[pl.ds(s * rows, rows)], stores.at[6 + s]) for s in range(8)]
    for one in rows_out[:6]:
        one.start()
    def normed_copy(s):
        return local(nbuf.at[s], normed_hbm.at[at(s)], stores.at[14 + s])

    def moved(s):
        return (
            local(hidden.at[s % 2], hidden_hbm.at[at(s)], stores.at[2 + s % 2]),
            local(pre.at[s % 2], pre_hbm.at[at(s)], stores.at[4 + s % 2]),
        )

    def slot(s, carry):
        normed_copy(s).start()

        @pl.when(s >= 2)
        def _():
            for one in moved(s - 2):
                one.wait()

        def some(t, inner):
            col = pl.ds(pl.multiple_of(t * tile, tile), tile)
            value, slope = gelu_pair(dot_nn(nbuf[s], w_up[:, col]))
            hidden[s % 2, :, col] = value.astype(BF)
            pre[s % 2, :, col] = (slope * slopes[t, s].astype(F32)).astype(BF)
            return inner

        lax.fori_loop(0, net.chunks, some, 0)
        for one in moved(s):
            one.start()
        return carry

    ring.pair()
    lax.fori_loop(0, 2, slot, 0)
    grads.finish()
    lax.fori_loop(6, 8, back, 0)
    for one in rows_out[6:]:
        one.start()
    ring.forward()
    ring.middle()
    lax.fori_loop(2, 6, slot, 0)
    ring.finish()
    lax.fori_loop(6, 8, slot, 0)
    for s in range(8):
        normed_copy(s).wait()
    for one in [*moved(6), *moved(7), *rows_out, mixed_out, attn_out, qkv_out]:
        one.wait()
    ring.drain()
    grads.drain()
    net.drain()


def forward(tokens, grad_out, w_query, w_key, w_value, w_out, w_up, w_down, gain_attn, gain_mlp, segment, valid, heads):
    rows, width = tokens.shape
    seq, hidden = 8 * rows, w_up.shape[1]
    hbm, vmem = pl.BlockSpec(memory_space=HBM_SPACE), pl.BlockSpec(memory_space=VMEM_SPACE)
    shape = jax.ShapeDtypeStruct
    return pl.pallas_call(
        functools.partial(forward_body, heads), name="forward_layer",
        in_specs=[hbm] * 8 + [vmem] * 4,
        out_specs=[hbm, hbm, hbm, vmem, hbm, hbm, hbm, hbm, hbm],
        out_shape=[
            shape((seq, 3 * heads * HD), BF), shape((seq, width), BF),
            shape((seq, heads * HD), BF), shape((heads, seq, 1), F32), shape((rows, width), F32), shape((seq, width), BF),
            shape((seq, hidden), BF), shape((seq, hidden), BF), shape((seq, width), BF),
        ],
        scratch_shapes=[
            pltpu.VMEM((seq, 3 * heads * HD), BF), pltpu.VMEM((heads * HD, width), BF),
            pltpu.VMEM((width, hidden), BF), pltpu.VMEM((hidden, width), BF), pltpu.VMEM((seq, heads * HD), BF),
            pltpu.VMEM((rows, width), F32), pltpu.VMEM((2, rows, hidden), BF), pltpu.VMEM((2, rows, hidden), BF),
            pltpu.VMEM((seq, 128), F32), pltpu.VMEM((1, seq), F32),
            pltpu.VMEM((seq, HD), BF), pltpu.VMEM((seq, HD), BF),
            pltpu.SemaphoreType.DMA((9,)), pltpu.SemaphoreType.DMA((23,)),
            pltpu.SemaphoreType.DMA((11,)), pltpu.SemaphoreType.DMA((11,)),
        ] + gather_scratch(rows, width) * 2 + scatter_scratch(rows, width, 2),
        compiler_params=pltpu.CompilerParams(collective_id=2, has_side_effects=True, vmem_limit_bytes=63 * MIB),
        cost_estimate=pl.CostEstimate(flops=40 * 10**9, bytes_accessed=250 * MIB, transcendentals=0),
    )(tokens, grad_out, w_query, w_key, w_value, w_out, w_up, w_down, gain_attn[None, :], gain_mlp[None, :], segment[None, :],
      valid[None, :])

def row_sums(product):
    part = sum(product[:, i:i + 128] for i in range(0, product.shape[1], 128))
    return lax.dot_general(
        jnp.ones((8, 128), F32), part, (((1,), (1,)), ((), ())), preferred_element_type=F32, precision=lax.Precision.HIGHEST
    )[0:1]


def middle_body(
    pre_hbm, w_up_hbm, normed_hbm, dnorm_hbm, up_hbm, gain_ref, pre, w_up, tiles, ups, dnorm, loads, stores, *scatter
):
    core, sib, first, second = neighbours()
    rows, width = dnorm.shape
    local = pltpu.make_async_copy
    tile = tiles.shape[2]
    count = width // tile
    fetch = [local(pre_hbm, pre, loads.at[0]), local(w_up_hbm, w_up, loads.at[1])]

    def strip(t):
        return pl.ds(pl.multiple_of(t * tile, tile), tile)

    def load_tile(t):
        return local(normed_hbm.at[:, strip(t)], tiles.at[t % 2], loads.at[2 + t % 2])

    def save_tile(t):
        return local(ups.at[t % 2], up_hbm.at[strip(t)], stores.at[1 + t % 2])

    for one in fetch:
        one.start()
    load_tile(0).start()
    greet(sib, first, second)

    def up_back(p, col):
        return dot_nt(pre[pl.ds(pl.multiple_of(p * rows, rows), rows), :], w_up[pl.ds(col, net.step), :])

    net = Scatter(up_back, dnorm, scatter[:8], scatter[8:], core, sib, first, second)
    fetch[0].wait()
    fetch[1].wait()
    net.each(net.away)
    net.each(net.one)

    def weight(t, carry):
        load_tile(t).wait()

        @pl.when(t < count - 1)
        def _():
            load_tile(t + 1).start()

        @pl.when(t >= 2)
        def _():
            save_tile(t - 2).wait()

        value = dot_tn(tiles[t % 2], pre[...])
        ups[t % 2] = value.astype(BF)
        save_tile(t).start()
        gain_ref[:, strip(t)] = row_sums(value * w_up[strip(t), :].astype(F32))
        return carry

    half = count // 2
    lax.fori_loop(0, half, weight, 0)
    net.two(0)
    lax.fori_loop(half, count, weight, 0)
    net.two(1)
    net.each(net.three)
    net.each(net.four)
    out = local(dnorm, dnorm_hbm, stores.at[0])
    out.start()
    out.wait()
    save_tile(count - 2).wait()
    save_tile(count - 1).wait()
    net.drain()


def middle(pre, w_up, normed):
    seq, inner = pre.shape
    width = w_up.shape[0]
    rows = seq // 8
    tile = 256
    hbm, vmem = pl.BlockSpec(memory_space=HBM_SPACE), pl.BlockSpec(memory_space=VMEM_SPACE)
    shape = jax.ShapeDtypeStruct
    return pl.pallas_call(
        middle_body, name="middle_layer",
        in_specs=[hbm] * 3,
        out_specs=[hbm] * 2 + [vmem],
        out_shape=[shape((rows, width), F32), shape((width, inner), BF), shape((1, width), F32)],
        scratch_shapes=[
            pltpu.VMEM((seq, inner), BF), pltpu.VMEM((width, inner), BF),
            pltpu.VMEM((2, seq, tile), BF), pltpu.VMEM((2, tile, inner), BF), pltpu.VMEM((rows, width), F32),
            pltpu.SemaphoreType.DMA((4,)), pltpu.SemaphoreType.DMA((3,)),
        ] + scatter_scratch(rows, width, 2),
        compiler_params=pltpu.CompilerParams(collective_id=5, has_side_effects=True, vmem_limit_bytes=56 * MIB),
        cost_estimate=pl.CostEstimate(flops=45 * 10**9, bytes_accessed=200 * MIB, transcendentals=0),
    )(pre, w_up, normed)


def turn_body(
    heads, dnorm_hbm, attn_hbm, tok_hbm, grad_hbm, w_out_hbm, qkv_hbm, mixed_hbm, hidden_hbm, w_down_hbm,
    gain_ref, lse_ref, seg_ref, valid_ref,
    branch_hbm, dqkv_hbm, residual_hbm, mlp_hbm,
    own, attn, tok, grad, w_out, qkv, mixed, hidden, w_down, dmixed, dqkv, rk_ref, ck_ref, ks, vs, dks, dvs, loads, stores,
    bbuf, bsend, brecv, *scatter,
):
    core, sib, first, second = neighbours()
    rows, width = tok.shape
    local = pltpu.make_async_copy
    fetch = [
        local(source, target, loads.at[i])
        for i, (source, target) in enumerate((
            (dnorm_hbm, own), (attn_hbm, attn), (tok_hbm, tok), (grad_hbm, grad), (w_out_hbm, w_out), (qkv_hbm, qkv),
            (mixed_hbm, mixed), (hidden_hbm, hidden), (w_down_hbm, w_down),
        ))
    ]
    for one in fetch:
        one.start()
    greet(sib, first, second)
    for one in fetch[:4]:
        one.wait()

    def norm(part):
        residual = tok[part, :].astype(F32) + attn[part, :]
        total = grad[part, :].astype(F32) + norm_back(residual, gain_ref[...], own[part, :])
        own[part, :] = total
        bbuf[0, part, :] = total.astype(BF)

    rows_loop(rows, 32, norm)
    ring = Gather(bbuf, bsend, brecv, sib, first, second)
    ring.start()
    residual_out = local(own, residual_hbm, stores.at[0])
    residual_out.start()
    fill_keys(seg_ref, valid_ref, rk_ref, ck_ref)
    fetch[4].wait()

    def moved(s):
        return local(bbuf.at[s], branch_hbm.at[pl.ds(pl.multiple_of(s * rows, rows), rows)], stores.at[2 + s])

    def slot(s, carry):
        moved(s).start()
        dmixed[pl.ds(pl.multiple_of(s * rows, rows), rows), :] = dot_nt(bbuf[s], w_out[...]).astype(BF)
        return carry

    def down(p, col):
        return dot_nn(hidden[pl.ds(pl.multiple_of(p * rows, rows), rows), :], w_down[:, pl.ds(col, net.step)])

    net = Scatter(down, attn, scatter[:8], scatter[8:], core, sib, first, second)
    ring.pair()
    lax.fori_loop(0, 2, slot, 0)
    fetch[7].wait()
    fetch[8].wait()
    net.each(net.away)
    ring.forward()
    ring.middle()
    lax.fori_loop(2, 6, slot, 0)
    net.one(0, False)
    ring.finish()
    net.go(0)
    lax.fori_loop(6, 8, slot, 0)
    fetch[5].wait()
    fetch[6].wait()

    def head(h, carry):
        def load(ref, k):
            return lambda at: ref[pl.ds(at, rows), pl.ds(pl.multiple_of((k * heads + h) * HD, HD), HD)]

        def save(k):
            def put(at, value):
                dqkv[pl.ds(at, rows), pl.ds(pl.multiple_of((k * heads + h) * HD, HD), HD)] = value
            return put

        unattend_head(
            rows, 8, lambda a: block_place(a, rows), load(qkv, 0), load(qkv, 1), load(qkv, 2), load(dmixed, 0), load(mixed, 0),
            lambda a: lse_ref[h, a * rows:(a + 1) * rows, :], rk_ref, ck_ref, save(0), save(1), save(2), ks, vs, dks, dvs,
        )

        @pl.when(h == 0)
        def _():
            net.one(1)
            net.two(0)

        return carry

    lax.fori_loop(0, heads, head, 0)
    dqkv_out = local(dqkv, dqkv_hbm, stores.at[1])
    dqkv_out.start()
    net.two(1)
    net.each(net.three)
    net.each(net.four)
    mlp_out = local(attn, mlp_hbm, stores.at[10])
    mlp_out.start()
    for s in range(8):
        moved(s).wait()
    for one in (residual_out, dqkv_out, mlp_out):
        one.wait()
    ring.drain()
    net.drain()


def turn(dnorm, attn_own, tokens, grad_out, w_out, qkv, mixed, hidden, w_down, gain, lse, segment, valid, heads):
    rows, width = tokens.shape
    seq = 8 * rows
    hbm, vmem = pl.BlockSpec(memory_space=HBM_SPACE), pl.BlockSpec(memory_space=VMEM_SPACE)
    shape = jax.ShapeDtypeStruct
    cols = heads * HD
    return pl.pallas_call(
        functools.partial(turn_body, heads), name="turn_layer",
        in_specs=[hbm] * 9 + [vmem] * 4,
        out_specs=[hbm] * 4,
        out_shape=[shape((seq, width), BF), shape((seq, 3 * cols), BF), shape((rows, width), F32), shape((rows, width), F32)],
        scratch_shapes=[
            pltpu.VMEM((rows, width), F32), pltpu.VMEM((rows, width), F32), pltpu.VMEM((rows, width), BF),
            pltpu.VMEM((rows, width), BF), pltpu.VMEM((cols, width), BF), pltpu.VMEM((seq, 3 * cols), BF),
            pltpu.VMEM((seq, cols), BF), pltpu.VMEM(hidden.shape, BF), pltpu.VMEM(w_down.shape, BF),
            pltpu.VMEM((seq, cols), BF), pltpu.VMEM((seq, 3 * cols), BF), pltpu.VMEM((seq, 128), F32), pltpu.VMEM((1, seq), F32),
            pltpu.VMEM((seq, HD), BF), pltpu.VMEM((seq, HD), BF), pltpu.VMEM((seq, HD), F32), pltpu.VMEM((seq, HD), F32),
            pltpu.SemaphoreType.DMA((9,)), pltpu.SemaphoreType.DMA((11,)),
        ] + gather_scratch(rows, width) + scatter_scratch(rows, width, 2),
        compiler_params=pltpu.CompilerParams(collective_id=3, has_side_effects=True, vmem_limit_bytes=63 * MIB),
        cost_estimate=pl.CostEstimate(flops=45 * 10**9, bytes_accessed=200 * MIB, transcendentals=0),
    )(dnorm, attn_own, tokens, grad_out, w_out, qkv, mixed, hidden, w_down, gain[None, :], lse, segment[None, :], valid[None, :])


def down_body(hidden_ref, grad_ref, out_ref):
    out_ref[...] = dot_tn(hidden_ref[...], grad_ref[...]).astype(BF)


def down_weights(hidden, grads):
    seq, inner = hidden.shape
    width = grads.shape[1]
    tile = 512
    return pl.pallas_call(
        down_body, name="down_weights", grid=(width // tile,),
        in_specs=[pl.BlockSpec((seq, inner), lambda t: (0, 0)), pl.BlockSpec((seq, tile), lambda t: (0, t))],
        out_specs=pl.BlockSpec((inner, tile), lambda t: (0, t)),
        out_shape=jax.ShapeDtypeStruct((inner, width), BF),
        compiler_params=pltpu.CompilerParams(vmem_limit_bytes=63 * MIB),
        cost_estimate=pl.CostEstimate(flops=2 * seq * width * inner, bytes_accessed=16 * MIB, transcendentals=0),
    )(hidden, grads)


def weights_body(normed_ref, branch_ref, dqkv_ref, mixed_ref, out_ref):
    cols = mixed_ref.shape[1]
    out_ref[:, :3 * cols] = dot_tn(normed_ref[...], dqkv_ref[...]).astype(BF)
    out_ref[:, 3 * cols:] = dot_tn(mixed_ref[...], branch_ref[...]).astype(BF)


def weights(normed, branch, dqkv, mixed):
    seq, width = normed.shape
    cols = mixed.shape[1]
    tile = cols
    full = lambda c: pl.BlockSpec((seq, c), lambda t: (0, 0))
    strip = pl.BlockSpec((seq, tile), lambda t: (0, t))
    return pl.pallas_call(
        weights_body, name="weight_gradients", grid=(width // tile,),
        in_specs=[strip, strip, full(3 * cols), full(cols)],
        out_specs=pl.BlockSpec((tile, 4 * cols), lambda t: (t, 0)),
        out_shape=jax.ShapeDtypeStruct((width, 4 * cols), BF),
        compiler_params=pltpu.CompilerParams(vmem_limit_bytes=63 * MIB),
        cost_estimate=pl.CostEstimate(flops=2 * seq * width * 4 * cols, bytes_accessed=30 * MIB, transcendentals=0),
    )(normed, branch, dqkv, mixed)


def unpack_body(sum_ref, q_ref, k_ref, v_ref, out_ref):
    cols = q_ref.shape[1]
    for k, ref in enumerate((q_ref, k_ref, v_ref)):
        ref[...] = sum_ref[:, k * cols:(k + 1) * cols].astype(F32)
    for i in range(sum_ref.shape[0] // cols):
        out_ref[:, i * cols:(i + 1) * cols] = sum_ref[i * cols:(i + 1) * cols, 3 * cols:].astype(F32)


def unpack(summed, cols):
    rows = summed.shape[0]
    vmem = pl.BlockSpec(memory_space=VMEM_SPACE)
    shapes = [jax.ShapeDtypeStruct((rows, cols), F32)] * 3 + [jax.ShapeDtypeStruct((cols, rows), F32)]
    return pl.pallas_call(unpack_body, name="unpack", in_specs=[vmem], out_specs=[vmem] * 4, out_shape=shapes)(summed)


class Total:
    def __init__(self, vec, got, sends, recvs, sib, first, second):
        self.vec, self.got = vec, got
        self.partners = [sib, first, second]
        self.copies = [
            pltpu.make_async_remote_copy(
                src_ref=vec, dst_ref=got.at[k], send_sem=sends.at[k], recv_sem=recvs.at[k], device_id=other, device_id_type=MESH,
            )
            for k, other in enumerate(self.partners)
        ]

    def start(self, k):
        self.copies[k].start()

    def add(self, k):
        self.copies[k].wait()
        self.vec[...] += self.got[k]
        if k + 1 < len(self.copies):
            self.copies[k + 1].start()


def finish_body(
    dqkv_hbm, wq_hbm, wk_hbm, wv_hbm, tok_hbm, attn_hbm, gres_hbm, mlp_hbm, part_hbm, gain_ref, part_mlp_ref,
    valid_ref, tokens_hbm, grads_hbm, total_ref,
    dqkv, w_qkv, part_ref, tok, attn, gres, out, mlp, dnorm, vec, got, sends, recvs, loads, stores, *scatter,
):
    core, sib, first, second = neighbours()
    rows, width = mlp.shape
    cols = wq_hbm.shape[1]
    local = pltpu.make_async_copy
    pairs = [(dqkv_hbm, dqkv)]
    pairs += [(w, w_qkv.at[:, pl.ds(k * cols, cols)]) for k, w in enumerate((wq_hbm, wk_hbm, wv_hbm))]
    pairs += [(tok_hbm, tok), (attn_hbm, attn), (gres_hbm, gres), (mlp_hbm, mlp), (part_hbm, part_ref)]
    fetch = [local(source, target, loads.at[i]) for i, (source, target) in enumerate(pairs)]
    for one in fetch:
        one.start()
    total = Total(vec, got, sends, recvs, sib, first, second)
    greet(*total.partners)

    def project_back(p, col):
        return dot_nt(dqkv[pl.ds(pl.multiple_of(p * rows, rows), rows), :], w_qkv[pl.ds(col, net.step), :])

    net = Scatter(project_back, dnorm, scatter[:8], scatter[8:], core, sib, first, second)
    for one in fetch[:4]:
        one.wait()
    net.each(net.away)
    net.each(net.one)
    for one in fetch[4:]:
        one.wait()
    own = pl.ds(pl.multiple_of((lax.axis_index("dp") * 8 + lax.axis_index("mp")) * rows, rows), rows)
    mask = jnp.transpose(jnp.broadcast_to(valid_ref[:, own].astype(F32), (128, rows)))
    vec[...] = jnp.zeros_like(vec)
    vec[1:2, :] = part_mlp_ref[...]
    step = 64
    for i in range(0, rows, step):
        part = slice(i, i + step)
        attn_part, mlp_part = attn[part, :], mlp[part, :]
        stream = tok[part, :].astype(F32) + attn_part + mlp_part
        out[0, part, :] = stream
        for k, value in enumerate((stream, attn_part, mlp_part)):
            vec[2 + k:3 + k, :] += jnp.sum(mask[part, 0:1] * value * value, axis=0, keepdims=True)
    for i in range(0, width, cols):
        tile = slice(i, i + cols)
        vec[0:1, tile] = row_sums(part_ref[tile, :3 * cols].astype(F32) * w_qkv[tile, :].astype(F32))
    tokens_out = local(out.at[0], tokens_hbm, stores.at[0])
    tokens_out.start()
    total.start(0)
    net.each(net.two)
    total.add(0)
    net.each(net.three)
    total.add(1)
    net.each(net.four)

    def last(part):
        back = norm_back(tok[part, :].astype(F32), gain_ref[...], dnorm[part, :])
        out[1, part, :] = gres[part, :] + back

    rows_loop(rows, 32, last)
    grads_out = local(out.at[1], grads_hbm, stores.at[1])
    grads_out.start()
    total.add(2)
    total_ref[...] = vec[...]
    tokens_out.wait()
    grads_out.wait()
    net.drain()


def finish(dqkv, w_query, w_key, w_value, tokens, attn_own, grad_residual, mlp_own, part_last, gain, part_mlp, valid):
    seq = dqkv.shape[0]
    rows, width = tokens.shape
    cols = w_query.shape[1]
    stages = 3
    hbm, vmem = pl.BlockSpec(memory_space=HBM_SPACE), pl.BlockSpec(memory_space=VMEM_SPACE)
    shape = jax.ShapeDtypeStruct
    return pl.pallas_call(
        finish_body, name="last_scatters",
        in_specs=[hbm] * 9 + [vmem] * 3,
        out_specs=[hbm] * 2 + [vmem],
        out_shape=[shape((rows, width), F32), shape((rows, width), F32), shape((8, width), F32)],
        scratch_shapes=[
            pltpu.VMEM((seq, 3 * cols), BF),
            pltpu.VMEM((width, 3 * cols), BF), pltpu.VMEM(part_last.shape, BF), pltpu.VMEM((rows, width), BF), pltpu.VMEM((rows, width), F32),
            pltpu.VMEM((rows, width), F32), pltpu.VMEM((2, rows, width), F32), pltpu.VMEM((rows, width), F32),
            pltpu.VMEM((rows, width), F32), pltpu.VMEM((8, width), F32), pltpu.VMEM((stages, 8, width), F32),
            pltpu.SemaphoreType.DMA((stages,)), pltpu.SemaphoreType.DMA((stages,)),
            pltpu.SemaphoreType.DMA((9,)), pltpu.SemaphoreType.DMA((2,)),
        ] + scatter_scratch(rows, width, 2),
        compiler_params=pltpu.CompilerParams(collective_id=4, has_side_effects=True, vmem_limit_bytes=63 * MIB),
        cost_estimate=pl.CostEstimate(flops=30 * 10**9, bytes_accessed=200 * MIB, transcendentals=0),
    )(dqkv, w_query, w_key, w_value, tokens, attn_own, grad_residual, mlp_own, part_last, gain[None, :], part_mlp,
      valid[None, :])


def after(value, *others):
    return lax.optimization_barrier((value,) + others)[0]


def over_mp(value):
    return lax.all_gather(value, "mp", axis=0, tiled=True)


def sum_mp(value):
    return lax.psum_scatter(value.astype(BF), "mp", scatter_dimension=0, tiled=True).astype(F32)


def sum_dp(value, axis):
    return lax.psum_scatter(value.astype(BF), "dp", scatter_dimension=axis, tiled=True)


def on_device(tokens, segment, valid, gain_attn, w_query, w_key, w_value, w_out, gain_mlp, w_up, w_down, grad_out):
    own_rows, width = tokens.shape
    seq_rows = segment.shape[0]
    heads = w_query.shape[1] // HD
    n_dp, n_mp = lax.axis_size("dp"), lax.axis_size("mp")
    dp, me = lax.axis_index("dp"), lax.axis_index("mp")
    cube = n_mp == 8 and n_dp in (1, 2, 4) and width == 8 * heads * HD
    order = jnp.arange(seq_rows // own_rows, dtype=jnp.int32)
    valid_group = lax.dynamic_slice_in_dim(valid, dp * seq_rows, seq_rows)
    valid_own = lax.dynamic_slice_in_dim(valid_group, me * own_rows, own_rows)
    tokens32 = tokens.astype(F32)

    if cube:
        qkv, normed, mixed, lse, attn_own, normed_mlp, hidden, grad_pre, grad_rows = forward(
            tokens, grad_out, w_query, w_key, w_value, w_out, w_up, w_down, gain_attn, gain_mlp, segment, valid, heads
        )
    else:
        row_key = segment[:, None]
        col_key = jnp.where(valid_group > 0, segment, -1)[None, :]
        normed = over_mp(norm_rows(tokens32, gain_attn).astype(BF))
        qkv = jnp.concatenate([dot_nn(normed, w).astype(BF) for w in (w_query, w_key, w_value)], 1)
        mixed, lse = attn_fwd(qkv, order, row_key, col_key, heads, own_rows)
        grad_rows = over_mp(after(grad_out, qkv))
        attn_own = sum_mp(dot_nn(mixed, w_out))
        normed_mlp = over_mp(norm_rows(tokens32 + attn_own, gain_mlp).astype(BF))
        hidden = gelu_fn(dot_nn(normed_mlp, w_up)).astype(BF)
    residual = tokens32 + attn_own

    if cube:
        part_down = down_weights(hidden, grad_rows)
        sum_down = sum_dp(part_down, 1)
        grad_normed, part_up, gain_mlp_part = middle(after(grad_pre, part_down), w_up, normed_mlp)
        sum_up = sum_dp(part_up, 0)
        grad_branch, grads_qkv, grad_residual, mlp_own = turn(
            grad_normed, attn_own, tokens, grad_out, w_out, qkv, mixed, hidden, w_down, gain_mlp, lse, segment, valid, heads
        )
        grads_qkv, sum_down = lax.optimization_barrier((grads_qkv, sum_down))
        part_last = weights(normed, grad_branch, grads_qkv, mixed)
        grad_last = sum_dp(part_last, 0)
        grad_down = after(sum_down, part_last).astype(F32)
        grads_qkv = after(grads_qkv, part_last, grad_down)
        stream, grad_tokens, summed = finish(
            grads_qkv, w_query, w_key, w_value, tokens, attn_own, grad_residual, mlp_own, part_last, gain_attn, gain_mlp_part, valid
        )
        near, far, both = [
            lax.ppermute(summed, "dp", [(i, i ^ bit) for i in range(n_dp)]) if bit < n_dp else jnp.zeros_like(summed)
            for bit in (1, 2, 3)
        ]
        grad_up = after(sum_up, stream).astype(F32)
        out_tokens, grad_tokens = stream.astype(BF), grad_tokens.astype(BF)
        summed = (summed + near) + (far + both)
    else:
        grad_down = sum_dp(dot_tn(hidden, grad_rows), 1).astype(F32)
        grad_pre = (gelu_pair(dot_nn(normed_mlp, w_up))[1] * dot_nt(grad_rows, w_down)).astype(BF)
        part_up = dot_tn(normed_mlp, grad_pre)
        grad_up = sum_dp(part_up, 0).astype(F32)
        gain_mlp_part = jnp.sum(part_up * w_up.astype(F32), axis=1)
        grad_residual = grad_out.astype(F32) + norm_back(residual, gain_mlp, sum_mp(dot_nt(grad_pre, w_up)))
        grad_branch = over_mp(grad_residual.astype(BF))
        grad_mixed = dot_nt(grad_branch, w_out).astype(BF)
        grads_qkv = jnp.concatenate(attn_bwd(qkv, grad_mixed, mixed, lse, order, row_key, col_key, heads, own_rows), 1)
        grad_out_proj = sum_dp(dot_tn(mixed, grad_branch), 1).astype(F32)
        part_qkv = dot_tn(normed, grads_qkv)
        grad_qkv = jnp.split(sum_dp(part_qkv, 0).astype(F32), 3, axis=1)
        w_qkv = jnp.concatenate([w_query, w_key, w_value], 1)
        gain_attn_part = jnp.sum(part_qkv * w_qkv.astype(F32), axis=1)
        mlp_own = sum_mp(dot_nn(hidden, w_down))
        grad_normed_attn = sum_mp(dot_nt(grads_qkv, w_qkv))
        stream = residual + mlp_own
        out_tokens = stream.astype(BF)
        grad_tokens = (grad_residual + norm_back(tokens32, gain_attn, grad_normed_attn)).astype(BF)
        mask_own = valid_own.astype(F32)[:, None]
        squares = [jnp.sum(mask_own * part * part, axis=0) for part in (stream, attn_own, mlp_own)]
        summed = lax.psum(jnp.stack([gain_attn_part, gain_mlp_part, *squares]), ("dp", "mp"))
    counted = jnp.maximum(jnp.sum(valid).astype(F32) * width, 1.0)
    gain_rows = width // (n_dp * n_mp)
    place = (dp * n_mp + me) * gain_rows
    rms = jnp.sqrt(jnp.sum(summed[2:5], axis=1) / counted)
    gains = [
        lax.dynamic_slice_in_dim(summed[k], place, gain_rows) / lax.dynamic_slice_in_dim(gain, place, gain_rows)
        for k, gain in enumerate((gain_attn, gain_mlp))
    ]
    if cube:
        grad_last, *_ = lax.optimization_barrier((grad_last, grad_up, out_tokens, grad_tokens, rms, gains))
        *grad_qkv, grad_out_proj = unpack(grad_last, heads * HD)
    return (
        out_tokens,
        grad_tokens,
        gains[0],
        *grad_qkv,
        grad_out_proj,
        gains[1],
        grad_up,
        grad_down,
        rms[0],
        rms[1],
        rms[2],
    )


def solution(mesh):
    tokens_spec = P(("dp", "mp"), None)
    cols, rows = P(None, "mp"), P("mp", None)
    return jax.shard_map(
        on_device,
        mesh=mesh,
        in_specs=(tokens_spec, P("dp"), P(), P(), cols, cols, cols, rows, P(), cols, rows, tokens_spec),
        out_specs=(
            tokens_spec,
            tokens_spec,
            P(("dp", "mp")),
            P("dp", "mp"),
            P("dp", "mp"),
            P("dp", "mp"),
            P("mp", "dp"),
            P(("dp", "mp")),
            P("dp", "mp"),
            P("mp", "dp"),
            P(),
            P(),
            P(),
        ),
        check_vma=False,
    )
```

```python
import functools

import jax
import jax.numpy as jnp
from jax import lax
from jax.experimental import pallas as pl
from jax.experimental.pallas import tpu as pltpu
from jax.sharding import PartitionSpec as P

HD = 128
NEGATIVE = -1e30
LOG2E = 1.4426950408889634
EPSILON = 1e-05
BF = jnp.bfloat16
F32 = jnp.float32
MIB = 2**20


def dot_nn(a, b):
    return jnp.dot(a, b, preferred_element_type=F32)


def dot_tn(a, b):
    return lax.dot_general(a, b, (((0,), (0,)), ((), ())), preferred_element_type=F32)


def dot_nt(a, b):
    return lax.dot_general(a, b, (((1,), (1,)), ((), ())), preferred_element_type=F32)


def diagonal(blk):
    rows = lax.broadcasted_iota(jnp.int32, (blk, blk), 0)
    cols = lax.broadcasted_iota(jnp.int32, (blk, blk), 1)
    return cols < rows, cols == rows


def attend_head(blk, count, place, queries, keys, values, rk_ref, ck_ref, put_mixed, put_lse, ks, vs):
    c = HD ** -0.5 * LOG2E
    for a in range(count):
        ks[a * blk:(a + 1) * blk, :] = keys(place(a))
        vs[a * blk:(a + 1) * blk, :] = values(place(a))
    earlier, itself = diagonal(blk)
    for a in range(count):
        end = (a + 1) * blk
        low = end - blk
        s = dot_nt(queries(place(a)), ks[:end, :])
        ok = rk_ref[low:end, 0:1] == ck_ref[:, :end]
        sd = jnp.where((ok[:, low:] & earlier) | itself, s[:, low:], NEGATIVE)
        m = jnp.max(sd, axis=1, keepdims=True)
        if a:
            so = jnp.where(ok[:, :low], s[:, :low], NEGATIVE)
            m = jnp.maximum(m, jnp.max(so, axis=1, keepdims=True))
        pd = jnp.exp2((sd - m) * c)
        total = jnp.sum(pd, axis=1, keepdims=True)
        o = dot_nn(pd.astype(BF), vs[low:end, :])
        if a:
            po = jnp.exp2((so - m) * c)
            total += jnp.sum(po, axis=1, keepdims=True)
            o += dot_nn(po.astype(BF), vs[:low, :])
        put_mixed(place(a), (o / total).astype(BF))
        put_lse(a, m * c + jnp.log2(total))


def attn_fwd_body(blk, count, order_ref, q_ref, k_ref, v_ref, rk_ref, ck_ref, mix_ref, lse_ref, ks, vs):
    def place(a):
        return pl.multiple_of(order_ref[a] * blk, blk)

    def put_mixed(at, value):
        mix_ref[pl.ds(at, blk), :] = value

    def put_lse(a, value):
        lse_ref[0, a * blk:(a + 1) * blk, :] = value

    attend_head(
        blk, count, place, lambda at: q_ref[pl.ds(at, blk), :], lambda at: k_ref[pl.ds(at, blk), :],
        lambda at: v_ref[pl.ds(at, blk), :], rk_ref, ck_ref, put_mixed, put_lse, ks, vs,
    )


def attn_fwd(qkv, order, rowkey, colkey, heads, blk):
    seq = qkv.shape[0]
    part = lambda off: pl.BlockSpec((seq, HD), lambda h, o: (0, off * heads + h))
    return pl.pallas_call(
        functools.partial(attn_fwd_body, blk, seq // blk), name="attn_fwd",
        grid_spec=pltpu.PrefetchScalarGridSpec(
            num_scalar_prefetch=1, grid=(heads,),
            in_specs=[part(0), part(1), part(2), pl.BlockSpec((seq, 1), lambda h, o: (0, 0)),
                      pl.BlockSpec((1, seq), lambda h, o: (0, 0))],
            out_specs=[part(0), pl.BlockSpec((1, seq, 1), lambda h, o: (h, 0, 0))],
            scratch_shapes=[pltpu.VMEM((seq, HD), BF)] * 2),
        out_shape=[jax.ShapeDtypeStruct((seq, heads * HD), BF), jax.ShapeDtypeStruct((heads, seq, 1), F32)],
        compiler_params=pltpu.CompilerParams(vmem_limit_bytes=48 * MIB),
        cost_estimate=pl.CostEstimate(
            flops=2 * seq * seq * HD * heads, bytes_accessed=8 * seq * HD * heads, transcendentals=seq * seq * heads // 2),
    )(order, qkv, qkv, qkv, rowkey, colkey)


def unattend_head(blk, count, place, queries, keys, values, grads, mixes, lses, rk_ref, ck_ref, put_q, put_k, put_v, ks, vs, dks, dvs,
                  between=None):
    scale = HD ** -0.5
    c = scale * LOG2E
    for a in range(count):
        ks[a * blk:(a + 1) * blk, :] = keys(place(a))
        vs[a * blk:(a + 1) * blk, :] = values(place(a))
    earlier, itself = diagonal(blk)

    def add(ref, lo, hi, value, fresh):
        if fresh:
            ref[lo:hi, :] = value
        else:
            ref[lo:hi, :] += value

    for a in reversed(range(count)):
        end = (a + 1) * blk
        low = end - blk
        fresh = a == count - 1
        at = place(a)
        q, do = queries(at), grads(at)
        delta = jnp.sum(do.astype(F32) * mixes(at).astype(F32), axis=1, keepdims=True)
        p = jnp.exp2(dot_nt(q, ks[:end, :]) * c - lses(a))
        dp = dot_nt(do, vs[:end, :])
        ok = rk_ref[low:end, 0:1] == ck_ref[:, :end]
        pd = jnp.where((ok[:, low:] & earlier) | itself, p[:, low:], 0.0)
        dsd = (pd * (dp[:, low:] - delta)).astype(BF)
        dq = dot_nn(dsd, ks[low:end, :])
        add(dks, low, end, dot_tn(dsd, q), fresh)
        add(dvs, low, end, dot_tn(pd.astype(BF), do), fresh)
        if a:
            po = jnp.where(ok[:, :low], p[:, :low], 0.0)
            dso = (po * (dp[:, :low] - delta)).astype(BF)
            dq += dot_nn(dso, ks[:low, :])
            add(dks, 0, low, dot_tn(dso, q), fresh)
            add(dvs, 0, low, dot_tn(po.astype(BF), do), fresh)
        put_q(at, (dq * scale).astype(BF))
        if between is not None:
            between(a)
    for a in range(count):
        put_k(place(a), (dks[a * blk:(a + 1) * blk, :] * scale).astype(BF))
        put_v(place(a), dvs[a * blk:(a + 1) * blk, :].astype(BF))


def attn_bwd_body(blk, count, order_ref, q_ref, k_ref, v_ref, do_ref, mix_ref, lse_ref, rk_ref, ck_ref, dq_ref, dk_ref, dv_ref,
                  ks, vs, dks, dvs):
    def place(a):
        return pl.multiple_of(order_ref[a] * blk, blk)

    def load(ref):
        return lambda at: ref[pl.ds(at, blk), :]

    def save(ref):
        def put(at, value):
            ref[pl.ds(at, blk), :] = value
        return put

    unattend_head(
        blk, count, place, load(q_ref), load(k_ref), load(v_ref), load(do_ref), load(mix_ref),
        lambda a: lse_ref[0, a * blk:(a + 1) * blk, :], rk_ref, ck_ref, save(dq_ref), save(dk_ref), save(dv_ref), ks, vs, dks, dvs,
    )


def attn_bwd(qkv, do, mixed, lse, order, rowkey, colkey, heads, blk):
    seq = qkv.shape[0]
    part = lambda off: pl.BlockSpec((seq, HD), lambda h, o: (0, off * heads + h))
    return pl.pallas_call(
        functools.partial(attn_bwd_body, blk, seq // blk), name="attn_bwd",
        grid_spec=pltpu.PrefetchScalarGridSpec(
            num_scalar_prefetch=1, grid=(heads,),
            in_specs=[part(0), part(1), part(2), part(0), part(0), pl.BlockSpec((1, seq, 1), lambda h, o: (h, 0, 0)),
                      pl.BlockSpec((seq, 1), lambda h, o: (0, 0)), pl.BlockSpec((1, seq), lambda h, o: (0, 0))],
            out_specs=[part(0), part(0), part(0)],
            scratch_shapes=[pltpu.VMEM((seq, HD), BF)] * 2 + [pltpu.VMEM((seq, HD), F32)] * 2),
        out_shape=[jax.ShapeDtypeStruct((seq, heads * HD), BF)] * 3,
        compiler_params=pltpu.CompilerParams(vmem_limit_bytes=56 * MIB),
        cost_estimate=pl.CostEstimate(
            flops=5 * seq * seq * HD * heads, bytes_accessed=16 * seq * HD * heads, transcendentals=seq * seq * heads // 2),
    )(order, qkv, qkv, qkv, do, mixed, lse, rowkey, colkey)


def row_scale(values):
    return lax.rsqrt(jnp.mean(values * values, axis=-1, keepdims=True) + EPSILON)


def norm_rows(values, norm_gain):
    return values * row_scale(values) * norm_gain


def norm_back(values, norm_gain, grad_norm):
    scale = row_scale(values)
    normal = values * scale
    grad_hat = grad_norm * norm_gain
    inner = jnp.mean(grad_hat * normal, axis=-1, keepdims=True)
    return scale * (grad_hat - normal * inner)


def gelu_fn(values):
    return jax.nn.gelu(values, approximate=True)


MESH = pl.DeviceIdType.MESH
HBM_SPACE = pl.ANY
VMEM_SPACE = pltpu.VMEM


def neighbours():
    dp, me = lax.axis_index("dp"), lax.axis_index("mp")
    core, along_x, along_y = me % 2, (me // 2) % 2, me // 4
    by_x, by_y = me + 2 - 4 * along_x, me + 4 - 8 * along_y
    first = (1 - core) * by_y + core * by_x
    second = (1 - core) * by_x + core * by_y
    return core, (dp, me + 1 - 2 * core), (dp, first), (dp, second)


def greet(*others):
    barrier = pltpu.get_barrier_semaphore()
    for other in others:
        pl.semaphore_signal(barrier, inc=1, device_id=other, device_id_type=MESH)
    pl.semaphore_wait(barrier, len(others))


class Gather:
    COPIES = 11

    def __init__(self, buf, sends, recvs, sib, first, second):
        rows = buf.shape[1]
        low, high, whole = pl.ds(0, rows // 2), pl.ds(rows // 2, rows // 2), pl.ds(0, rows)

        def copy(i, source, target, part, device):
            return pltpu.make_async_remote_copy(
                src_ref=buf.at[source, part], dst_ref=buf.at[target, part],
                send_sem=sends.at[i], recv_sem=recvs.at[i], device_id=device, device_id_type=MESH,
            )

        self.copies = [
            copy(0, 0, 4, high, first), copy(1, 0, 4, low, first),
            copy(2, 0, 2, low, second), copy(3, 0, 2, high, second),
            copy(4, 0, 1, whole, sib),
            copy(5, 2, 6, low, first), copy(6, 4, 6, high, second),
            copy(7, 4, 3, whole, sib), copy(8, 2, 5, whole, sib),
            copy(9, 6, 7, low, sib), copy(10, 6, 7, high, sib),
        ]

    def start(self):
        for i in (0, 2, 1, 3, 4):
            self.copies[i].start()

    def pair(self):
        self.copies[4].wait_recv()

    def forward(self, both=True):
        for arrived, onward in ((2, 5), (0, 6)):
            self.copies[arrived].wait_recv()
            if both:
                self.copies[onward].start()
        for arrived, onward in ((1, 7), (3, 8)):
            self.copies[arrived].wait_recv()
            self.copies[onward].start()

    def onward(self):
        self.copies[5].start()
        self.copies[6].start()

    def middle(self):
        self.copies[7].wait_recv()
        self.copies[8].wait_recv()

    def finish(self):
        for arrived, onward in ((5, 9), (6, 10)):
            self.copies[arrived].wait_recv()
            self.copies[onward].start()
        self.copies[9].wait_recv()
        self.copies[10].wait_recv()

    def drain(self):
        for one in self.copies:
            one.wait_send()

class Scatter:
    def __init__(self, product, own_ref, bufs, sems, core, sib, first, second):
        self.product, self.own_ref, self.core = product, own_ref, core
        self.sent = 0
        self.away_ref, self.r0, self.s1, self.r1, self.s2, self.r2, self.s3, self.r3 = bufs
        self.chunks, _, self.rows, self.step = self.away_ref.shape
        self.half = self.chunks * self.step
        sends, recvs = sems

        def copy(source, target, j, k, device):
            return pltpu.make_async_remote_copy(
                src_ref=source.at[j], dst_ref=target.at[j], send_sem=sends.at[j, k], recv_sem=recvs.at[j, k],
                device_id=device, device_id_type=MESH,
            )

        self.copies = [
            [copy(self.away_ref, self.r0, j, 0, sib), copy(self.s1, self.r1, j, 1, first),
             copy(self.s2, self.r2, j, 2, second), copy(self.s3, self.r3, j, 3, sib)]
            for j in range(self.chunks)
        ]

    def column(self, j, core):
        return pl.multiple_of(core * self.half + j * self.step, self.step)

    def away(self, j):
        col = self.column(j, 1 - self.core)

        def some(p, carry):
            self.away_ref[j, p] = self.product(p, col).astype(BF)
            return carry

        lax.fori_loop(0, 8, some, 0)
        self.copies[j][0].start()

    def kept(self, j, p):
        came = 4 * ((p // 2) % 2) + 2 * (p // 4) + 1 - p % 2
        return self.product(p, self.column(j, self.core)) + self.r0[j, came].astype(F32)

    def one(self, j):
        self.copies[j][0].wait_recv()

        def some(p, carry):
            self.s1[j, p - 4] = self.kept(j, p).astype(BF)
            return carry

        lax.fori_loop(4, 8, some, 0)
        self.copies[j][1].start()

    def two(self, j):
        self.copies[j][1].wait_recv()

        def some(p, carry):
            self.s2[j, p - 2] = (self.kept(j, p) + self.r1[j, p].astype(F32)).astype(BF)
            return carry

        lax.fori_loop(2, 4, some, 0)
        self.copies[j][2].start()

    def three(self, j):
        self.copies[j][2].wait_recv()

        def last(p):
            return self.kept(j, p) + self.r1[j, p].astype(F32) + self.r2[j, p].astype(F32)

        self.s3[j] = last(1).astype(BF)
        self.copies[j][3].start()
        self.own_ref[:, pl.ds(self.column(j, self.core), self.step)] = last(0)

    def four(self, j):
        self.copies[j][3].wait_recv()
        self.own_ref[:, pl.ds(self.column(j, 1 - self.core), self.step)] = self.r3[j].astype(F32)

    def each(self, stage):
        for j in range(self.chunks):
            stage(j)

    def release(self, j):
        self.copies[j][0].wait_send()
        self.sent = 1

    def drain(self):
        for copies in self.copies:
            for one in copies[self.sent:]:
                one.wait_send()


def scatter_scratch(rows, width, chunks):
    step = width // 2 // chunks
    sizes = [(8, rows, step)] * 2 + [(4, rows, step)] * 2 + [(2, rows, step)] * 2 + [(rows, step)] * 2
    return [pltpu.VMEM((chunks,) + size, BF) for size in sizes] + [pltpu.SemaphoreType.DMA((chunks, 4))] * 2


def gather_scratch(rows, width):
    return [pltpu.VMEM((8, rows, width), BF), pltpu.SemaphoreType.DMA((11,)), pltpu.SemaphoreType.DMA((11,))]


def rows_loop(rows, step, body):
    def some(i, carry):
        body(pl.ds(pl.multiple_of(i * step, step), step))
        return carry

    lax.fori_loop(0, rows // step, some, 0)


def block_place(a, rows):
    me = lax.axis_index("mp")
    core = me % 2
    by_c = (a % 2 + core) % 2
    by_x = (a // 2 + me // 2) % 2
    by_y = (a // 4 + me // 4) % 2
    position = 4 * (by_y + core * (by_x - by_y)) + 2 * (by_x + core * (by_y - by_x)) + by_c
    return pl.multiple_of(position * rows, rows)


def gelu_pair(x):
    c = 0.7978845608028654
    square = x * x
    t = jnp.tanh(c * (x + 0.044715 * (x * square)))
    upper = 0.5 * (1.0 + t)
    return x * upper, upper + 0.5 * x * (1.0 - t * t) * (c + (3 * 0.044715 * c) * square)


def fill_keys(seg_ref, valid_ref, rk, ck):
    seq = seg_ref.shape[1]
    here = pl.ds(pl.multiple_of(lax.axis_index("dp") * seq, seq), seq)
    numbers = seg_ref[...].astype(F32)
    ck[...] = jnp.where(valid_ref[:, here] > 0, numbers, -1.0)
    step = 256
    for i in range(0, seq, step):
        rk[i:i + step, :] = jnp.transpose(jnp.broadcast_to(numbers[:, i:i + step], (128, step)))


def forward_body(
    heads, tok_hbm, grad_hbm, wq_hbm, wk_hbm, wv_hbm, w_out_hbm, w_up_hbm, w_down_hbm, gain_attn_ref, gain_ref, seg_ref, valid_ref,
    qkv_hbm, first_hbm, mixed_hbm, lse_ref, attn_hbm, normed_hbm, hidden_hbm, pre_hbm, rows_hbm,
    qkv, w_out, w_up, w_down, mixed, own, hidden, pre, rk_ref, ck_ref, ks, vs, loads, stores,
    asend, arecv, nbuf, nsend, nrecv, gbuf, gsend, grecv, *scatter,
):
    core, sib, first, second = neighbours()
    rows, width = own.shape
    local = pltpu.make_async_copy
    cols = wq_hbm.shape[1]
    fetch = [
        local(grad_hbm, gbuf.at[0], loads.at[0]), local(tok_hbm, nbuf.at[0], loads.at[1]), local(w_out_hbm, w_out, loads.at[2]),
        local(tok_hbm, nbuf.at[0], loads.at[3]), local(w_up_hbm, w_up, loads.at[4]), local(w_down_hbm, w_down, loads.at[5]),
    ]
    projections = [
        local(w, w_up.at[:, pl.ds(k * cols, cols)], loads.at[6 + k]) for k, w in enumerate((wq_hbm, wk_hbm, wv_hbm))
    ]
    for one in [fetch[1], *projections, fetch[0], fetch[2], fetch[5]]:
        one.start()
    greet(sib, first, second)
    fetch[1].wait()

    def at(s):
        return pl.ds(pl.multiple_of(s * rows, rows), rows)

    def norm_first(part):
        nbuf[0, part, :] = norm_rows(nbuf[0, part, :].astype(F32), gain_attn_ref[...]).astype(BF)

    rows_loop(rows, 32, norm_first)
    opening = Gather(nbuf, asend, arecv, sib, first, second)
    opening.start()
    fill_keys(seg_ref, valid_ref, rk_ref, ck_ref)
    for one in projections:
        one.wait()

    def first_copy(s):
        return local(nbuf.at[s], first_hbm.at[at(s)], stores.at[14 + s])

    def projected(s, carry):
        first_copy(s).start()
        qkv[at(s), :] = dot_nn(nbuf[s], w_up[:, :3 * cols]).astype(BF)
        return carry

    opening.pair()
    lax.fori_loop(0, 2, projected, 0)
    opening.forward()
    opening.middle()
    lax.fori_loop(2, 6, projected, 0)
    opening.finish()
    fetch[0].wait()
    grads = Gather(gbuf, gsend, grecv, sib, first, second)
    grads.start()
    lax.fori_loop(6, 8, projected, 0)
    fetch[4].start()
    qkv_out = local(qkv, qkv_hbm, stores.at[22])
    qkv_out.start()

    def head(h, carry):
        def part(k):
            return lambda at: qkv[pl.ds(at, rows), pl.ds(pl.multiple_of((k * heads + h) * HD, HD), HD)]

        def put_mixed(at, value):
            mixed[pl.ds(at, rows), pl.ds(pl.multiple_of(h * HD, HD), HD)] = value

        def put_lse(a, value):
            lse_ref[h, a * rows:(a + 1) * rows, :] = value

        attend_head(rows, 8, lambda a: block_place(a, rows), part(0), part(1), part(2), rk_ref, ck_ref, put_mixed, put_lse, ks, vs)
        return carry

    lax.fori_loop(0, heads, head, 0)
    mixed_out = local(mixed, mixed_hbm, stores.at[0])
    mixed_out.start()

    def product(p, col):
        return dot_nn(mixed[pl.ds(pl.multiple_of(p * rows, rows), rows), :], w_out[:, pl.ds(col, net.step)])

    fetch[2].wait()
    net = Scatter(product, own, scatter[:8], scatter[8:], core, sib, first, second)
    net.each(net.away)
    for s in range(8):
        first_copy(s).wait()
    opening.drain()
    fetch[3].start()
    net.each(net.one)
    grads.pair()
    fetch[5].wait()
    net.each(net.release)
    slopes = net.away_ref
    tile = net.step

    def back(s, carry):
        for t in range(net.chunks):
            slopes[t, s] = dot_nt(gbuf[s], w_down[t * tile:(t + 1) * tile, :]).astype(BF)
        return carry

    lax.fori_loop(0, 2, back, 0)
    grads.forward(False)
    grads.middle()
    lax.fori_loop(2, 6, back, 0)
    net.each(net.two)
    grads.onward()
    net.each(net.three)
    net.each(net.four)
    attn_out = local(own, attn_hbm, stores.at[1])
    attn_out.start()

    fetch[3].wait()

    def norm(part):
        residual = nbuf[0, part, :].astype(F32) + own[part, :]
        nbuf[0, part, :] = norm_rows(residual, gain_ref[...]).astype(BF)

    rows_loop(rows, 32, norm)
    ring = Gather(nbuf, nsend, nrecv, sib, first, second)
    ring.start()
    fetch[4].wait()
    rows_out = [local(gbuf.at[s], rows_hbm.at[pl.ds(s * rows, rows)], stores.at[6 + s]) for s in range(8)]
    for one in rows_out[:6]:
        one.start()
    def normed_copy(s):
        return local(nbuf.at[s], normed_hbm.at[at(s)], stores.at[14 + s])

    def moved(s):
        return (
            local(hidden.at[s % 2], hidden_hbm.at[at(s)], stores.at[2 + s % 2]),
            local(pre.at[s % 2], pre_hbm.at[at(s)], stores.at[4 + s % 2]),
        )

    def slot(s, carry):
        normed_copy(s).start()

        @pl.when(s >= 2)
        def _():
            for one in moved(s - 2):
                one.wait()

        small = tile // 2
        for t in range(net.chunks):
            for i in range(0, tile, small):
                col = slice(t * tile + i, t * tile + i + small)
                value, slope = gelu_pair(dot_nn(nbuf[s], w_up[:, col]))
                hidden[s % 2, :, col] = value.astype(BF)
                pre[s % 2, :, col] = (slope * slopes[t, s, :, i:i + small].astype(F32)).astype(BF)

        for one in moved(s):
            one.start()
        return carry

    ring.pair()
    lax.fori_loop(0, 2, slot, 0)
    grads.finish()
    lax.fori_loop(6, 8, back, 0)
    for one in rows_out[6:]:
        one.start()
    ring.forward()
    ring.middle()
    lax.fori_loop(2, 6, slot, 0)
    ring.finish()
    lax.fori_loop(6, 8, slot, 0)
    for s in range(8):
        normed_copy(s).wait()
    for one in [*moved(6), *moved(7), *rows_out, mixed_out, attn_out, qkv_out]:
        one.wait()
    ring.drain()
    grads.drain()
    net.drain()


def forward(tokens, grad_out, w_query, w_key, w_value, w_out, w_up, w_down, gain_attn, gain_mlp, segment, valid, heads):
    rows, width = tokens.shape
    seq, hidden = 8 * rows, w_up.shape[1]
    hbm, vmem = pl.BlockSpec(memory_space=HBM_SPACE), pl.BlockSpec(memory_space=VMEM_SPACE)
    shape = jax.ShapeDtypeStruct
    return pl.pallas_call(
        functools.partial(forward_body, heads), name="forward_layer",
        in_specs=[hbm] * 8 + [vmem] * 4,
        out_specs=[hbm, hbm, hbm, vmem, hbm, hbm, hbm, hbm, hbm],
        out_shape=[
            shape((seq, 3 * heads * HD), BF), shape((seq, width), BF),
            shape((seq, heads * HD), BF), shape((heads, seq, 1), F32), shape((rows, width), F32), shape((seq, width), BF),
            shape((seq, hidden), BF), shape((seq, hidden), BF), shape((seq, width), BF),
        ],
        scratch_shapes=[
            pltpu.VMEM((seq, 3 * heads * HD), BF), pltpu.VMEM((heads * HD, width), BF),
            pltpu.VMEM((width, hidden), BF), pltpu.VMEM((hidden, width), BF), pltpu.VMEM((seq, heads * HD), BF),
            pltpu.VMEM((rows, width), F32), pltpu.VMEM((2, rows, hidden), BF), pltpu.VMEM((2, rows, hidden), BF),
            pltpu.VMEM((seq, 128), F32), pltpu.VMEM((1, seq), F32),
            pltpu.VMEM((seq, HD), BF), pltpu.VMEM((seq, HD), BF),
            pltpu.SemaphoreType.DMA((9,)), pltpu.SemaphoreType.DMA((23,)),
            pltpu.SemaphoreType.DMA((11,)), pltpu.SemaphoreType.DMA((11,)),
        ] + gather_scratch(rows, width) * 2 + scatter_scratch(rows, width, 2),
        compiler_params=pltpu.CompilerParams(collective_id=2, has_side_effects=True, vmem_limit_bytes=63 * MIB),
        cost_estimate=pl.CostEstimate(flops=40 * 10**9, bytes_accessed=250 * MIB, transcendentals=0),
    )(tokens, grad_out, w_query, w_key, w_value, w_out, w_up, w_down, gain_attn[None, :], gain_mlp[None, :], segment[None, :],
      valid[None, :])

def row_sums(product):
    part = sum(product[:, i:i + 128] for i in range(0, product.shape[1], 128))
    return lax.dot_general(
        jnp.ones((8, 128), F32), part, (((1,), (1,)), ((), ())), preferred_element_type=F32, precision=lax.Precision.HIGHEST
    )[0:1]


def middle_body(
    pre_hbm, w_up_hbm, normed_hbm, dnorm_hbm, up_hbm, gain_ref, pre, w_up, tiles, ups, dnorm, loads, stores, *scatter
):
    core, sib, first, second = neighbours()
    rows, width = dnorm.shape
    local = pltpu.make_async_copy
    tile = tiles.shape[2]
    count = width // tile
    fetch = [local(pre_hbm, pre, loads.at[0]), local(w_up_hbm, w_up, loads.at[1])]

    def strip(t):
        return pl.ds(pl.multiple_of(t * tile, tile), tile)

    def load_tile(t):
        return local(normed_hbm.at[:, strip(t)], tiles.at[t % 2], loads.at[2 + t % 2])

    def save_tile(t):
        return local(ups.at[t % 2], up_hbm.at[strip(t)], stores.at[1 + t % 2])

    for one in fetch:
        one.start()
    load_tile(0).start()
    greet(sib, first, second)

    def up_back(p, col):
        return dot_nt(pre[pl.ds(pl.multiple_of(p * rows, rows), rows), :], w_up[pl.ds(col, net.step), :])

    net = Scatter(up_back, dnorm, scatter[:8], scatter[8:], core, sib, first, second)
    fetch[0].wait()
    fetch[1].wait()
    net.each(net.away)
    net.each(net.one)

    def weight(t, carry):
        load_tile(t).wait()

        @pl.when(t < count - 1)
        def _():
            load_tile(t + 1).start()

        @pl.when(t >= 2)
        def _():
            save_tile(t - 2).wait()

        value = dot_tn(tiles[t % 2], pre[...])
        ups[t % 2] = value.astype(BF)
        save_tile(t).start()
        gain_ref[:, strip(t)] = row_sums(value * w_up[strip(t), :].astype(F32))
        return carry

    half = count // 2
    lax.fori_loop(0, half, weight, 0)
    net.two(0)
    lax.fori_loop(half, count, weight, 0)
    net.two(1)
    net.each(net.three)
    net.each(net.four)
    out = local(dnorm, dnorm_hbm, stores.at[0])
    out.start()
    out.wait()
    save_tile(count - 2).wait()
    save_tile(count - 1).wait()
    net.drain()


def middle(pre, w_up, normed):
    seq, inner = pre.shape
    width = w_up.shape[0]
    rows = seq // 8
    tile = 256
    hbm, vmem = pl.BlockSpec(memory_space=HBM_SPACE), pl.BlockSpec(memory_space=VMEM_SPACE)
    shape = jax.ShapeDtypeStruct
    return pl.pallas_call(
        middle_body, name="middle_layer",
        in_specs=[hbm] * 3,
        out_specs=[hbm] * 2 + [vmem],
        out_shape=[shape((rows, width), F32), shape((width, inner), BF), shape((1, width), F32)],
        scratch_shapes=[
            pltpu.VMEM((seq, inner), BF), pltpu.VMEM((width, inner), BF),
            pltpu.VMEM((2, seq, tile), BF), pltpu.VMEM((2, tile, inner), BF), pltpu.VMEM((rows, width), F32),
            pltpu.SemaphoreType.DMA((4,)), pltpu.SemaphoreType.DMA((3,)),
        ] + scatter_scratch(rows, width, 2),
        compiler_params=pltpu.CompilerParams(collective_id=5, has_side_effects=True, vmem_limit_bytes=56 * MIB),
        cost_estimate=pl.CostEstimate(flops=45 * 10**9, bytes_accessed=200 * MIB, transcendentals=0),
    )(pre, w_up, normed)


def turn_body(
    heads, dnorm_hbm, attn_hbm, tok_hbm, grad_hbm, w_out_hbm, qkv_hbm, mixed_hbm, hidden_hbm, w_down_hbm,
    gain_ref, lse_ref, seg_ref, valid_ref,
    branch_hbm, dqkv_hbm, residual_hbm, mlp_hbm,
    own, attn, tok, grad, w_out, qkv, mixed, hidden, w_down, dmixed, dqkv, rk_ref, ck_ref, ks, vs, dks, dvs, loads, stores,
    bbuf, bsend, brecv, *scatter,
):
    core, sib, first, second = neighbours()
    rows, width = tok.shape
    local = pltpu.make_async_copy
    fetch = [
        local(source, target, loads.at[i])
        for i, (source, target) in enumerate((
            (dnorm_hbm, own), (attn_hbm, attn), (tok_hbm, tok), (grad_hbm, grad), (w_out_hbm, w_out), (qkv_hbm, qkv),
            (mixed_hbm, mixed), (hidden_hbm, hidden), (w_down_hbm, w_down),
        ))
    ]
    for one in fetch:
        one.start()
    greet(sib, first, second)
    for one in fetch[:4]:
        one.wait()

    def norm(part):
        residual = tok[part, :].astype(F32) + attn[part, :]
        total = grad[part, :].astype(F32) + norm_back(residual, gain_ref[...], own[part, :])
        own[part, :] = total
        bbuf[0, part, :] = total.astype(BF)

    rows_loop(rows, 32, norm)
    ring = Gather(bbuf, bsend, brecv, sib, first, second)
    ring.start()
    residual_out = local(own, residual_hbm, stores.at[0])
    residual_out.start()
    fill_keys(seg_ref, valid_ref, rk_ref, ck_ref)
    fetch[4].wait()

    def moved(s):
        return local(bbuf.at[s], branch_hbm.at[pl.ds(pl.multiple_of(s * rows, rows), rows)], stores.at[2 + s])

    def slot(s, carry):
        moved(s).start()
        dmixed[pl.ds(pl.multiple_of(s * rows, rows), rows), :] = dot_nt(bbuf[s], w_out[...]).astype(BF)
        return carry

    def down(p, col):
        return dot_nn(hidden[pl.ds(pl.multiple_of(p * rows, rows), rows), :], w_down[:, pl.ds(col, net.step)])

    net = Scatter(down, attn, scatter[:8], scatter[8:], core, sib, first, second)
    ring.pair()
    lax.fori_loop(0, 2, slot, 0)
    fetch[7].wait()
    fetch[8].wait()
    net.each(net.away)
    ring.forward()
    ring.middle()
    lax.fori_loop(2, 6, slot, 0)
    net.each(net.one)
    ring.finish()
    lax.fori_loop(6, 8, slot, 0)
    fetch[5].wait()
    fetch[6].wait()

    def head(h, carry):
        def load(ref, k):
            return lambda at: ref[pl.ds(at, rows), pl.ds(pl.multiple_of((k * heads + h) * HD, HD), HD)]

        def save(k):
            def put(at, value):
                dqkv[pl.ds(at, rows), pl.ds(pl.multiple_of((k * heads + h) * HD, HD), HD)] = value
            return put

        unattend_head(
            rows, 8, lambda a: block_place(a, rows), load(qkv, 0), load(qkv, 1), load(qkv, 2), load(dmixed, 0), load(mixed, 0),
            lambda a: lse_ref[h, a * rows:(a + 1) * rows, :], rk_ref, ck_ref, save(0), save(1), save(2), ks, vs, dks, dvs,
        )

        return carry

    lax.fori_loop(0, heads, head, 0)
    dqkv_out = local(dqkv, dqkv_hbm, stores.at[1])
    dqkv_out.start()
    net.each(net.two)
    net.each(net.three)
    net.each(net.four)
    mlp_out = local(attn, mlp_hbm, stores.at[10])
    mlp_out.start()
    for s in range(8):
        moved(s).wait()
    for one in (residual_out, dqkv_out, mlp_out):
        one.wait()
    ring.drain()
    net.drain()


def turn(dnorm, attn_own, tokens, grad_out, w_out, qkv, mixed, hidden, w_down, gain, lse, segment, valid, heads):
    rows, width = tokens.shape
    seq = 8 * rows
    hbm, vmem = pl.BlockSpec(memory_space=HBM_SPACE), pl.BlockSpec(memory_space=VMEM_SPACE)
    shape = jax.ShapeDtypeStruct
    cols = heads * HD
    return pl.pallas_call(
        functools.partial(turn_body, heads), name="turn_layer",
        in_specs=[hbm] * 9 + [vmem] * 4,
        out_specs=[hbm] * 4,
        out_shape=[shape((seq, width), BF), shape((seq, 3 * cols), BF), shape((rows, width), F32), shape((rows, width), F32)],
        scratch_shapes=[
            pltpu.VMEM((rows, width), F32), pltpu.VMEM((rows, width), F32), pltpu.VMEM((rows, width), BF),
            pltpu.VMEM((rows, width), BF), pltpu.VMEM((cols, width), BF), pltpu.VMEM((seq, 3 * cols), BF),
            pltpu.VMEM((seq, cols), BF), pltpu.VMEM(hidden.shape, BF), pltpu.VMEM(w_down.shape, BF),
            pltpu.VMEM((seq, cols), BF), pltpu.VMEM((seq, 3 * cols), BF), pltpu.VMEM((seq, 128), F32), pltpu.VMEM((1, seq), F32),
            pltpu.VMEM((seq, HD), BF), pltpu.VMEM((seq, HD), BF), pltpu.VMEM((seq, HD), F32), pltpu.VMEM((seq, HD), F32),
            pltpu.SemaphoreType.DMA((9,)), pltpu.SemaphoreType.DMA((11,)),
        ] + gather_scratch(rows, width) + scatter_scratch(rows, width, 2),
        compiler_params=pltpu.CompilerParams(collective_id=3, has_side_effects=True, vmem_limit_bytes=63 * MIB),
        cost_estimate=pl.CostEstimate(flops=45 * 10**9, bytes_accessed=200 * MIB, transcendentals=0),
    )(dnorm, attn_own, tokens, grad_out, w_out, qkv, mixed, hidden, w_down, gain[None, :], lse, segment[None, :], valid[None, :])


def down_body(hidden_ref, grad_ref, out_ref):
    out_ref[...] = dot_tn(hidden_ref[...], grad_ref[...]).astype(BF)


def down_weights(hidden, grads):
    seq, inner = hidden.shape
    width = grads.shape[1]
    tile = 512
    return pl.pallas_call(
        down_body, name="down_weights", grid=(width // tile,),
        in_specs=[pl.BlockSpec((seq, inner), lambda t: (0, 0)), pl.BlockSpec((seq, tile), lambda t: (0, t))],
        out_specs=pl.BlockSpec((inner, tile), lambda t: (0, t)),
        out_shape=jax.ShapeDtypeStruct((inner, width), BF),
        compiler_params=pltpu.CompilerParams(vmem_limit_bytes=63 * MIB),
        cost_estimate=pl.CostEstimate(flops=2 * seq * width * inner, bytes_accessed=16 * MIB, transcendentals=0),
    )(hidden, grads)


def weights_body(normed_ref, branch_ref, dqkv_ref, mixed_ref, out_ref):
    cols = mixed_ref.shape[1]
    out_ref[:, :3 * cols] = dot_tn(normed_ref[...], dqkv_ref[...]).astype(BF)
    out_ref[:, 3 * cols:] = dot_tn(mixed_ref[...], branch_ref[...]).astype(BF)


def weights(normed, branch, dqkv, mixed):
    seq, width = normed.shape
    cols = mixed.shape[1]
    tile = cols
    full = lambda c: pl.BlockSpec((seq, c), lambda t: (0, 0))
    strip = pl.BlockSpec((seq, tile), lambda t: (0, t))
    return pl.pallas_call(
        weights_body, name="weight_gradients", grid=(width // tile,),
        in_specs=[strip, strip, full(3 * cols), full(cols)],
        out_specs=pl.BlockSpec((tile, 4 * cols), lambda t: (t, 0)),
        out_shape=jax.ShapeDtypeStruct((width, 4 * cols), BF),
        compiler_params=pltpu.CompilerParams(vmem_limit_bytes=63 * MIB),
        cost_estimate=pl.CostEstimate(flops=2 * seq * width * 4 * cols, bytes_accessed=30 * MIB, transcendentals=0),
    )(normed, branch, dqkv, mixed)


def unpack_body(sum_ref, q_ref, k_ref, v_ref, out_ref):
    cols = q_ref.shape[1]
    for k, ref in enumerate((q_ref, k_ref, v_ref)):
        ref[...] = sum_ref[:, k * cols:(k + 1) * cols].astype(F32)
    for i in range(sum_ref.shape[0] // cols):
        out_ref[:, i * cols:(i + 1) * cols] = sum_ref[i * cols:(i + 1) * cols, 3 * cols:].astype(F32)


def unpack(summed, cols):
    rows = summed.shape[0]
    vmem = pl.BlockSpec(memory_space=VMEM_SPACE)
    shapes = [jax.ShapeDtypeStruct((rows, cols), F32)] * 3 + [jax.ShapeDtypeStruct((cols, rows), F32)]
    return pl.pallas_call(unpack_body, name="unpack", in_specs=[vmem], out_specs=[vmem] * 4, out_shape=shapes)(summed)


class Total:
    def __init__(self, vec, got, sends, recvs, sib, first, second):
        self.vec, self.got = vec, got
        self.partners = [sib, first, second]
        self.copies = [
            pltpu.make_async_remote_copy(
                src_ref=vec, dst_ref=got.at[k], send_sem=sends.at[k], recv_sem=recvs.at[k], device_id=other, device_id_type=MESH,
            )
            for k, other in enumerate(self.partners)
        ]

    def start(self, k):
        self.copies[k].start()

    def add(self, k):
        self.copies[k].wait()
        self.vec[...] += self.got[k]
        if k + 1 < len(self.copies):
            self.copies[k + 1].start()


def finish_body(
    dqkv_hbm, wq_hbm, wk_hbm, wv_hbm, tok_hbm, attn_hbm, gres_hbm, mlp_hbm, part_hbm, gain_ref, part_mlp_ref,
    valid_ref, tokens_hbm, grads_hbm, total_ref,
    dqkv, w_qkv, part_ref, tok, attn, gres, out, mlp, dnorm, vec, got, sends, recvs, loads, stores, *scatter,
):
    core, sib, first, second = neighbours()
    rows, width = mlp.shape
    cols = wq_hbm.shape[1]
    local = pltpu.make_async_copy
    pairs = [(dqkv_hbm, dqkv)]
    pairs += [(w, w_qkv.at[:, pl.ds(k * cols, cols)]) for k, w in enumerate((wq_hbm, wk_hbm, wv_hbm))]
    pairs += [(tok_hbm, tok), (attn_hbm, attn), (gres_hbm, gres), (mlp_hbm, mlp), (part_hbm, part_ref)]
    fetch = [local(source, target, loads.at[i]) for i, (source, target) in enumerate(pairs)]
    for one in fetch:
        one.start()
    total = Total(vec, got, sends, recvs, sib, first, second)
    greet(*total.partners)

    def project_back(p, col):
        return dot_nt(dqkv[pl.ds(pl.multiple_of(p * rows, rows), rows), :], w_qkv[pl.ds(col, net.step), :])

    net = Scatter(project_back, dnorm, scatter[:8], scatter[8:], core, sib, first, second)
    for one in fetch[:4]:
        one.wait()
    net.each(net.away)
    net.each(net.one)
    for one in fetch[4:]:
        one.wait()
    own = pl.ds(pl.multiple_of((lax.axis_index("dp") * 8 + lax.axis_index("mp")) * rows, rows), rows)
    mask = jnp.transpose(jnp.broadcast_to(valid_ref[:, own].astype(F32), (128, rows)))
    vec[...] = jnp.zeros_like(vec)
    vec[1:2, :] = part_mlp_ref[...]
    step = 64
    for i in range(0, rows, step):
        part = slice(i, i + step)
        attn_part, mlp_part = attn[part, :], mlp[part, :]
        stream = tok[part, :].astype(F32) + attn_part + mlp_part
        out[0, part, :] = stream
        for k, value in enumerate((stream, attn_part, mlp_part)):
            vec[2 + k:3 + k, :] += jnp.sum(mask[part, 0:1] * value * value, axis=0, keepdims=True)
    for i in range(0, width, cols):
        tile = slice(i, i + cols)
        vec[0:1, tile] = row_sums(part_ref[tile, :3 * cols].astype(F32) * w_qkv[tile, :].astype(F32))
    tokens_out = local(out.at[0], tokens_hbm, stores.at[0])
    tokens_out.start()
    total.start(0)
    net.each(net.two)
    total.add(0)
    net.each(net.three)
    total.add(1)
    net.each(net.four)

    def last(part):
        back = norm_back(tok[part, :].astype(F32), gain_ref[...], dnorm[part, :])
        out[1, part, :] = gres[part, :] + back

    rows_loop(rows, 32, last)
    grads_out = local(out.at[1], grads_hbm, stores.at[1])
    grads_out.start()
    total.add(2)
    total_ref[...] = vec[...]
    tokens_out.wait()
    grads_out.wait()
    net.drain()


def finish(dqkv, w_query, w_key, w_value, tokens, attn_own, grad_residual, mlp_own, part_last, gain, part_mlp, valid):
    seq = dqkv.shape[0]
    rows, width = tokens.shape
    cols = w_query.shape[1]
    stages = 3
    hbm, vmem = pl.BlockSpec(memory_space=HBM_SPACE), pl.BlockSpec(memory_space=VMEM_SPACE)
    shape = jax.ShapeDtypeStruct
    return pl.pallas_call(
        finish_body, name="last_scatters",
        in_specs=[hbm] * 9 + [vmem] * 3,
        out_specs=[hbm] * 2 + [vmem],
        out_shape=[shape((rows, width), F32), shape((rows, width), F32), shape((8, width), F32)],
        scratch_shapes=[
            pltpu.VMEM((seq, 3 * cols), BF),
            pltpu.VMEM((width, 3 * cols), BF), pltpu.VMEM(part_last.shape, BF), pltpu.VMEM((rows, width), BF), pltpu.VMEM((rows, width), F32),
            pltpu.VMEM((rows, width), F32), pltpu.VMEM((2, rows, width), F32), pltpu.VMEM((rows, width), F32),
            pltpu.VMEM((rows, width), F32), pltpu.VMEM((8, width), F32), pltpu.VMEM((stages, 8, width), F32),
            pltpu.SemaphoreType.DMA((stages,)), pltpu.SemaphoreType.DMA((stages,)),
            pltpu.SemaphoreType.DMA((9,)), pltpu.SemaphoreType.DMA((2,)),
        ] + scatter_scratch(rows, width, 2),
        compiler_params=pltpu.CompilerParams(collective_id=4, has_side_effects=True, vmem_limit_bytes=63 * MIB),
        cost_estimate=pl.CostEstimate(flops=30 * 10**9, bytes_accessed=200 * MIB, transcendentals=0),
    )(dqkv, w_query, w_key, w_value, tokens, attn_own, grad_residual, mlp_own, part_last, gain[None, :], part_mlp,
      valid[None, :])


def after(value, *others):
    return lax.optimization_barrier((value,) + others)[0]


def over_mp(value):
    return lax.all_gather(value, "mp", axis=0, tiled=True)


def sum_mp(value):
    return lax.psum_scatter(value.astype(BF), "mp", scatter_dimension=0, tiled=True).astype(F32)


def sum_dp(value, axis):
    return lax.psum_scatter(value.astype(BF), "dp", scatter_dimension=axis, tiled=True)


def on_device(tokens, segment, valid, gain_attn, w_query, w_key, w_value, w_out, gain_mlp, w_up, w_down, grad_out):
    own_rows, width = tokens.shape
    seq_rows = segment.shape[0]
    heads = w_query.shape[1] // HD
    n_dp, n_mp = lax.axis_size("dp"), lax.axis_size("mp")
    dp, me = lax.axis_index("dp"), lax.axis_index("mp")
    cube = n_mp == 8 and n_dp in (1, 2, 4) and width == 8 * heads * HD
    order = jnp.arange(seq_rows // own_rows, dtype=jnp.int32)
    valid_group = lax.dynamic_slice_in_dim(valid, dp * seq_rows, seq_rows)
    valid_own = lax.dynamic_slice_in_dim(valid_group, me * own_rows, own_rows)
    tokens32 = tokens.astype(F32)

    if cube:
        qkv, normed, mixed, lse, attn_own, normed_mlp, hidden, grad_pre, grad_rows = forward(
            tokens, grad_out, w_query, w_key, w_value, w_out, w_up, w_down, gain_attn, gain_mlp, segment, valid, heads
        )
    else:
        row_key = segment[:, None]
        col_key = jnp.where(valid_group > 0, segment, -1)[None, :]
        normed = over_mp(norm_rows(tokens32, gain_attn).astype(BF))
        qkv = jnp.concatenate([dot_nn(normed, w).astype(BF) for w in (w_query, w_key, w_value)], 1)
        mixed, lse = attn_fwd(qkv, order, row_key, col_key, heads, own_rows)
        grad_rows = over_mp(after(grad_out, qkv))
        attn_own = sum_mp(dot_nn(mixed, w_out))
        normed_mlp = over_mp(norm_rows(tokens32 + attn_own, gain_mlp).astype(BF))
        hidden = gelu_fn(dot_nn(normed_mlp, w_up)).astype(BF)
    residual = tokens32 + attn_own

    if cube:
        part_down = down_weights(hidden, grad_rows)
        sum_down = sum_dp(part_down, 1)
        grad_normed, part_up, gain_mlp_part = middle(after(grad_pre, part_down), w_up, normed_mlp)
        sum_up = sum_dp(part_up, 0)
        grad_branch, grads_qkv, grad_residual, mlp_own = turn(
            grad_normed, attn_own, tokens, grad_out, w_out, qkv, mixed, hidden, w_down, gain_mlp, lse, segment, valid, heads
        )
        grads_qkv, sum_down = lax.optimization_barrier((grads_qkv, sum_down))
        part_last = weights(normed, grad_branch, grads_qkv, mixed)
        grad_last = sum_dp(part_last, 0)
        grad_down = after(sum_down, part_last).astype(F32)
        grads_qkv = after(grads_qkv, part_last, grad_down)
        stream, grad_tokens, summed = finish(
            grads_qkv, w_query, w_key, w_value, tokens, attn_own, grad_residual, mlp_own, part_last, gain_attn, gain_mlp_part, valid
        )
        gain_rows = width // (n_dp * n_mp)
        ours = lax.dynamic_index_in_dim(summed[:2].reshape(2, n_dp, n_mp, gain_rows), me, 2, False)
        squares = jnp.sum(summed[2:5], axis=1)
        parts = []
        for bit in range(n_dp):
            theirs = lax.dynamic_index_in_dim(ours, jnp.bitwise_xor(dp, bit), 1, False)
            part = jnp.concatenate([theirs.reshape(-1), squares])
            parts.append(lax.ppermute(part, "dp", [(i, i ^ bit) for i in range(n_dp)]) if bit else part)
        grad_up = after(sum_up, stream).astype(F32)
        out_tokens, grad_tokens = stream.astype(BF), grad_tokens.astype(BF)
        while len(parts) > 1:
            parts = [low + high for low, high in zip(parts[::2], parts[1::2])]
        gain_sums, squares = parts[0][:2 * gain_rows].reshape(2, gain_rows), parts[0][2 * gain_rows:]
    else:
        grad_down = sum_dp(dot_tn(hidden, grad_rows), 1).astype(F32)
        grad_pre = (gelu_pair(dot_nn(normed_mlp, w_up))[1] * dot_nt(grad_rows, w_down)).astype(BF)
        part_up = dot_tn(normed_mlp, grad_pre)
        grad_up = sum_dp(part_up, 0).astype(F32)
        gain_mlp_part = jnp.sum(part_up * w_up.astype(F32), axis=1)
        grad_residual = grad_out.astype(F32) + norm_back(residual, gain_mlp, sum_mp(dot_nt(grad_pre, w_up)))
        grad_branch = over_mp(grad_residual.astype(BF))
        grad_mixed = dot_nt(grad_branch, w_out).astype(BF)
        grads_qkv = jnp.concatenate(attn_bwd(qkv, grad_mixed, mixed, lse, order, row_key, col_key, heads, own_rows), 1)
        grad_out_proj = sum_dp(dot_tn(mixed, grad_branch), 1).astype(F32)
        part_qkv = dot_tn(normed, grads_qkv)
        grad_qkv = jnp.split(sum_dp(part_qkv, 0).astype(F32), 3, axis=1)
        w_qkv = jnp.concatenate([w_query, w_key, w_value], 1)
        gain_attn_part = jnp.sum(part_qkv * w_qkv.astype(F32), axis=1)
        mlp_own = sum_mp(dot_nn(hidden, w_down))
        grad_normed_attn = sum_mp(dot_nt(grads_qkv, w_qkv))
        stream = residual + mlp_own
        out_tokens = stream.astype(BF)
        grad_tokens = (grad_residual + norm_back(tokens32, gain_attn, grad_normed_attn)).astype(BF)
        mask_own = valid_own.astype(F32)[:, None]
        squares = [jnp.sum(mask_own * part * part, axis=0) for part in (stream, attn_own, mlp_own)]
        summed = lax.psum(jnp.stack([gain_attn_part, gain_mlp_part, *squares]), ("dp", "mp"))
    counted = jnp.maximum(jnp.sum(valid).astype(F32) * width, 1.0)
    gain_rows = width // (n_dp * n_mp)
    place = (dp * n_mp + me) * gain_rows
    if not cube:
        gain_sums = lax.dynamic_slice_in_dim(summed[:2], place, gain_rows, 1)
        squares = jnp.sum(summed[2:5], axis=1)
    rms = jnp.sqrt(squares / counted)
    gains = [
        gain_sums[k] / lax.dynamic_slice_in_dim(gain, place, gain_rows) for k, gain in enumerate((gain_attn, gain_mlp))
    ]
    if cube:
        grad_last, *_ = lax.optimization_barrier((grad_last, grad_up, out_tokens, grad_tokens, rms, gains))
        *grad_qkv, grad_out_proj = unpack(grad_last, heads * HD)
    return (
        out_tokens,
        grad_tokens,
        gains[0],
        *grad_qkv,
        grad_out_proj,
        gains[1],
        grad_up,
        grad_down,
        rms[0],
        rms[1],
        rms[2],
    )


def solution(mesh):
    tokens_spec = P(("dp", "mp"), None)
    cols, rows = P(None, "mp"), P("mp", None)
    return jax.shard_map(
        on_device,
        mesh=mesh,
        in_specs=(tokens_spec, P("dp"), P(), P(), cols, cols, cols, rows, P(), cols, rows, tokens_spec),
        out_specs=(
            tokens_spec,
            tokens_spec,
            P(("dp", "mp")),
            P("dp", "mp"),
            P("dp", "mp"),
            P("dp", "mp"),
            P("mp", "dp"),
            P(("dp", "mp")),
            P("dp", "mp"),
            P("mp", "dp"),
            P(),
            P(),
            P(),
        ),
        check_vma=False,
    )
```

```python
import functools

import jax
import jax.numpy as jnp
from jax import lax
from jax.experimental import pallas as pl
from jax.experimental.pallas import tpu as pltpu
from jax.sharding import PartitionSpec as P

HD = 128
NEGATIVE = -1e30
LOG2E = 1.4426950408889634
EPSILON = 1e-05
BF = jnp.bfloat16
F32 = jnp.float32
MIB = 2**20


def dot_nn(a, b):
    return jnp.dot(a, b, preferred_element_type=F32)


def dot_tn(a, b):
    return lax.dot_general(a, b, (((0,), (0,)), ((), ())), preferred_element_type=F32)


def dot_nt(a, b):
    return lax.dot_general(a, b, (((1,), (1,)), ((), ())), preferred_element_type=F32)


def diagonal(blk):
    rows = lax.broadcasted_iota(jnp.int32, (blk, blk), 0)
    cols = lax.broadcasted_iota(jnp.int32, (blk, blk), 1)
    return cols < rows, cols == rows


def attend_head(blk, count, place, queries, keys, values, rk_ref, ck_ref, put_mixed, put_lse, ks, vs):
    c = HD ** -0.5 * LOG2E
    for a in range(count):
        ks[a * blk:(a + 1) * blk, :] = keys(place(a))
        vs[a * blk:(a + 1) * blk, :] = values(place(a))
    earlier, itself = diagonal(blk)
    for a in range(count):
        end = (a + 1) * blk
        low = end - blk
        s = dot_nt(queries(place(a)), ks[:end, :])
        ok = rk_ref[low:end, 0:1] == ck_ref[:, :end]
        sd = jnp.where((ok[:, low:] & earlier) | itself, s[:, low:], NEGATIVE)
        m = jnp.max(sd, axis=1, keepdims=True)
        if a:
            so = jnp.where(ok[:, :low], s[:, :low], NEGATIVE)
            m = jnp.maximum(m, jnp.max(so, axis=1, keepdims=True))
        pd = jnp.exp2((sd - m) * c)
        total = jnp.sum(pd, axis=1, keepdims=True)
        o = dot_nn(pd.astype(BF), vs[low:end, :])
        if a:
            po = jnp.exp2((so - m) * c)
            total += jnp.sum(po, axis=1, keepdims=True)
            o += dot_nn(po.astype(BF), vs[:low, :])
        put_mixed(place(a), (o / total).astype(BF))
        put_lse(a, m * c + jnp.log2(total))


def attn_fwd_body(blk, count, order_ref, q_ref, k_ref, v_ref, rk_ref, ck_ref, mix_ref, lse_ref, ks, vs):
    def place(a):
        return pl.multiple_of(order_ref[a] * blk, blk)

    def put_mixed(at, value):
        mix_ref[pl.ds(at, blk), :] = value

    def put_lse(a, value):
        lse_ref[0, a * blk:(a + 1) * blk, :] = value

    attend_head(
        blk, count, place, lambda at: q_ref[pl.ds(at, blk), :], lambda at: k_ref[pl.ds(at, blk), :],
        lambda at: v_ref[pl.ds(at, blk), :], rk_ref, ck_ref, put_mixed, put_lse, ks, vs,
    )


def attn_fwd(qkv, order, rowkey, colkey, heads, blk):
    seq = qkv.shape[0]
    part = lambda off: pl.BlockSpec((seq, HD), lambda h, o: (0, off * heads + h))
    return pl.pallas_call(
        functools.partial(attn_fwd_body, blk, seq // blk), name="attn_fwd",
        grid_spec=pltpu.PrefetchScalarGridSpec(
            num_scalar_prefetch=1, grid=(heads,),
            in_specs=[part(0), part(1), part(2), pl.BlockSpec((seq, 1), lambda h, o: (0, 0)),
                      pl.BlockSpec((1, seq), lambda h, o: (0, 0))],
            out_specs=[part(0), pl.BlockSpec((1, seq, 1), lambda h, o: (h, 0, 0))],
            scratch_shapes=[pltpu.VMEM((seq, HD), BF)] * 2),
        out_shape=[jax.ShapeDtypeStruct((seq, heads * HD), BF), jax.ShapeDtypeStruct((heads, seq, 1), F32)],
        compiler_params=pltpu.CompilerParams(vmem_limit_bytes=48 * MIB),
        cost_estimate=pl.CostEstimate(
            flops=2 * seq * seq * HD * heads, bytes_accessed=8 * seq * HD * heads, transcendentals=seq * seq * heads // 2),
    )(order, qkv, qkv, qkv, rowkey, colkey)


def unattend_head(blk, count, place, queries, keys, values, grads, mixes, lses, rk_ref, ck_ref, put_q, put_k, put_v, ks, vs, dks, dvs,
                  between=None):
    scale = HD ** -0.5
    c = scale * LOG2E
    for a in range(count):
        ks[a * blk:(a + 1) * blk, :] = keys(place(a))
        vs[a * blk:(a + 1) * blk, :] = values(place(a))
    earlier, itself = diagonal(blk)

    def add(ref, lo, hi, value, fresh):
        if fresh:
            ref[lo:hi, :] = value
        else:
            ref[lo:hi, :] += value

    for a in reversed(range(count)):
        end = (a + 1) * blk
        low = end - blk
        fresh = a == count - 1
        at = place(a)
        q, do = queries(at), grads(at)
        delta = jnp.sum(do.astype(F32) * mixes(at).astype(F32), axis=1, keepdims=True)
        p = jnp.exp2(dot_nt(q, ks[:end, :]) * c - lses(a))
        dp = dot_nt(do, vs[:end, :])
        ok = rk_ref[low:end, 0:1] == ck_ref[:, :end]
        pd = jnp.where((ok[:, low:] & earlier) | itself, p[:, low:], 0.0)
        dsd = (pd * (dp[:, low:] - delta)).astype(BF)
        dq = dot_nn(dsd, ks[low:end, :])
        add(dks, low, end, dot_tn(dsd, q), fresh)
        add(dvs, low, end, dot_tn(pd.astype(BF), do), fresh)
        if a:
            po = jnp.where(ok[:, :low], p[:, :low], 0.0)
            dso = (po * (dp[:, :low] - delta)).astype(BF)
            dq += dot_nn(dso, ks[:low, :])
            add(dks, 0, low, dot_tn(dso, q), fresh)
            add(dvs, 0, low, dot_tn(po.astype(BF), do), fresh)
        put_q(at, (dq * scale).astype(BF))
        if between is not None:
            between(a)
    for a in range(count):
        put_k(place(a), (dks[a * blk:(a + 1) * blk, :] * scale).astype(BF))
        put_v(place(a), dvs[a * blk:(a + 1) * blk, :].astype(BF))


def attn_bwd_body(blk, count, order_ref, q_ref, k_ref, v_ref, do_ref, mix_ref, lse_ref, rk_ref, ck_ref, dq_ref, dk_ref, dv_ref,
                  ks, vs, dks, dvs):
    def place(a):
        return pl.multiple_of(order_ref[a] * blk, blk)

    def load(ref):
        return lambda at: ref[pl.ds(at, blk), :]

    def save(ref):
        def put(at, value):
            ref[pl.ds(at, blk), :] = value
        return put

    unattend_head(
        blk, count, place, load(q_ref), load(k_ref), load(v_ref), load(do_ref), load(mix_ref),
        lambda a: lse_ref[0, a * blk:(a + 1) * blk, :], rk_ref, ck_ref, save(dq_ref), save(dk_ref), save(dv_ref), ks, vs, dks, dvs,
    )


def attn_bwd(qkv, do, mixed, lse, order, rowkey, colkey, heads, blk):
    seq = qkv.shape[0]
    part = lambda off: pl.BlockSpec((seq, HD), lambda h, o: (0, off * heads + h))
    return pl.pallas_call(
        functools.partial(attn_bwd_body, blk, seq // blk), name="attn_bwd",
        grid_spec=pltpu.PrefetchScalarGridSpec(
            num_scalar_prefetch=1, grid=(heads,),
            in_specs=[part(0), part(1), part(2), part(0), part(0), pl.BlockSpec((1, seq, 1), lambda h, o: (h, 0, 0)),
                      pl.BlockSpec((seq, 1), lambda h, o: (0, 0)), pl.BlockSpec((1, seq), lambda h, o: (0, 0))],
            out_specs=[part(0), part(0), part(0)],
            scratch_shapes=[pltpu.VMEM((seq, HD), BF)] * 2 + [pltpu.VMEM((seq, HD), F32)] * 2),
        out_shape=[jax.ShapeDtypeStruct((seq, heads * HD), BF)] * 3,
        compiler_params=pltpu.CompilerParams(vmem_limit_bytes=56 * MIB),
        cost_estimate=pl.CostEstimate(
            flops=5 * seq * seq * HD * heads, bytes_accessed=16 * seq * HD * heads, transcendentals=seq * seq * heads // 2),
    )(order, qkv, qkv, qkv, do, mixed, lse, rowkey, colkey)


def row_scale(values):
    return lax.rsqrt(jnp.mean(values * values, axis=-1, keepdims=True) + EPSILON)


def norm_rows(values, norm_gain):
    return values * row_scale(values) * norm_gain


def norm_back(values, norm_gain, grad_norm):
    scale = row_scale(values)
    normal = values * scale
    grad_hat = grad_norm * norm_gain
    inner = jnp.mean(grad_hat * normal, axis=-1, keepdims=True)
    return scale * (grad_hat - normal * inner)


def gelu_fn(values):
    return jax.nn.gelu(values, approximate=True)


MESH = pl.DeviceIdType.MESH
HBM_SPACE = pl.ANY
VMEM_SPACE = pltpu.VMEM


def neighbours():
    dp, me = lax.axis_index("dp"), lax.axis_index("mp")
    core, along_x, along_y = me % 2, (me // 2) % 2, me // 4
    by_x, by_y = me + 2 - 4 * along_x, me + 4 - 8 * along_y
    first = (1 - core) * by_y + core * by_x
    second = (1 - core) * by_x + core * by_y
    return core, (dp, me + 1 - 2 * core), (dp, first), (dp, second)


def greet(*others):
    barrier = pltpu.get_barrier_semaphore()
    for other in others:
        pl.semaphore_signal(barrier, inc=1, device_id=other, device_id_type=MESH)
    pl.semaphore_wait(barrier, len(others))


class Gather:
    COPIES = 11

    def __init__(self, buf, sends, recvs, sib, first, second):
        rows = buf.shape[1]
        low, high, whole = pl.ds(0, rows // 2), pl.ds(rows // 2, rows // 2), pl.ds(0, rows)

        def copy(i, source, target, part, device):
            return pltpu.make_async_remote_copy(
                src_ref=buf.at[source, part], dst_ref=buf.at[target, part],
                send_sem=sends.at[i], recv_sem=recvs.at[i], device_id=device, device_id_type=MESH,
            )

        self.copies = [
            copy(0, 0, 4, high, first), copy(1, 0, 4, low, first),
            copy(2, 0, 2, low, second), copy(3, 0, 2, high, second),
            copy(4, 0, 1, whole, sib),
            copy(5, 2, 6, low, first), copy(6, 4, 6, high, second),
            copy(7, 4, 3, whole, sib), copy(8, 2, 5, whole, sib),
            copy(9, 6, 7, low, sib), copy(10, 6, 7, high, sib),
        ]

    def start(self):
        self.start_low()
        self.start_high()

    def start_low(self):
        for i in (1, 2):
            self.copies[i].start()

    def start_high(self):
        for i in (0, 3, 4):
            self.copies[i].start()

    def pair(self):
        self.copies[4].wait_recv()

    def forward(self, both=True):
        for arrived, onward in ((2, 5), (0, 6)):
            self.copies[arrived].wait_recv()
            if both:
                self.copies[onward].start()
        for arrived, onward in ((1, 7), (3, 8)):
            self.copies[arrived].wait_recv()
            self.copies[onward].start()

    def onward(self):
        self.copies[5].start()
        self.copies[6].start()

    def middle(self):
        self.copies[7].wait_recv()
        self.copies[8].wait_recv()

    def finish(self):
        for arrived, onward in ((5, 9), (6, 10)):
            self.copies[arrived].wait_recv()
            self.copies[onward].start()
        self.copies[9].wait_recv()
        self.copies[10].wait_recv()

    def drain(self):
        for one in self.copies:
            one.wait_send()

class Scatter:
    def __init__(self, product, own_ref, bufs, sems, core, sib, first, second):
        self.product, self.own_ref, self.core = product, own_ref, core
        self.sent = 0
        self.away_ref, self.r0, self.s1, self.r1, self.s2, self.r2, self.s3, self.r3 = bufs
        self.chunks, _, self.rows, self.step = self.away_ref.shape
        self.half = self.chunks * self.step
        sends, recvs = sems

        def copy(source, target, j, k, device):
            return pltpu.make_async_remote_copy(
                src_ref=source.at[j], dst_ref=target.at[j], send_sem=sends.at[j, k], recv_sem=recvs.at[j, k],
                device_id=device, device_id_type=MESH,
            )

        self.copies = [
            [copy(self.away_ref, self.r0, j, 0, sib), copy(self.s1, self.r1, j, 1, first),
             copy(self.s2, self.r2, j, 2, second), copy(self.s3, self.r3, j, 3, sib)]
            for j in range(self.chunks)
        ]

    def column(self, j, core):
        return pl.multiple_of(core * self.half + j * self.step, self.step)

    def away(self, j):
        col = self.column(j, 1 - self.core)

        def some(p, carry):
            self.away_ref[j, p] = self.product(p, col).astype(BF)
            return carry

        lax.fori_loop(0, 8, some, 0)
        self.copies[j][0].start()

    def kept(self, j, p):
        came = 4 * ((p // 2) % 2) + 2 * (p // 4) + 1 - p % 2
        return self.product(p, self.column(j, self.core)) + self.r0[j, came].astype(F32)

    def one(self, j):
        self.copies[j][0].wait_recv()

        def some(p, carry):
            self.s1[j, p - 4] = self.kept(j, p).astype(BF)
            return carry

        lax.fori_loop(4, 8, some, 0)
        self.copies[j][1].start()

    def two(self, j):
        self.copies[j][1].wait_recv()

        def some(p, carry):
            self.s2[j, p - 2] = (self.kept(j, p) + self.r1[j, p].astype(F32)).astype(BF)
            return carry

        lax.fori_loop(2, 4, some, 0)
        self.copies[j][2].start()

    def three(self, j):
        self.copies[j][2].wait_recv()

        def last(p):
            return self.kept(j, p) + self.r1[j, p].astype(F32) + self.r2[j, p].astype(F32)

        self.s3[j] = last(1).astype(BF)
        self.copies[j][3].start()
        self.own_ref[:, pl.ds(self.column(j, self.core), self.step)] = last(0)

    def four(self, j):
        self.copies[j][3].wait_recv()
        self.own_ref[:, pl.ds(self.column(j, 1 - self.core), self.step)] = self.r3[j].astype(F32)

    def each(self, stage):
        for j in range(self.chunks):
            stage(j)

    def release(self, j):
        self.copies[j][0].wait_send()
        self.sent = 1

    def drain(self):
        for copies in self.copies:
            for one in copies[self.sent:]:
                one.wait_send()


def scatter_scratch(rows, width, chunks):
    step = width // 2 // chunks
    sizes = [(8, rows, step)] * 2 + [(4, rows, step)] * 2 + [(2, rows, step)] * 2 + [(rows, step)] * 2
    return [pltpu.VMEM((chunks,) + size, BF) for size in sizes] + [pltpu.SemaphoreType.DMA((chunks, 4))] * 2


def gather_scratch(rows, width):
    return [pltpu.VMEM((8, rows, width), BF), pltpu.SemaphoreType.DMA((11,)), pltpu.SemaphoreType.DMA((11,))]


def rows_loop(rows, step, body, begin=0):
    def some(i, carry):
        body(pl.ds(pl.multiple_of(i * step, step), step))
        return carry

    lax.fori_loop(begin // step, rows // step, some, 0)


def send_as_ready(ring, rows, body):
    rows_loop(rows // 2, 32, body)
    ring.start_low()
    rows_loop(rows, 32, body, rows // 2)
    ring.start_high()


def block_place(a, rows):
    me = lax.axis_index("mp")
    core = me % 2
    by_c = (a % 2 + core) % 2
    by_x = (a // 2 + me // 2) % 2
    by_y = (a // 4 + me // 4) % 2
    position = 4 * (by_y + core * (by_x - by_y)) + 2 * (by_x + core * (by_y - by_x)) + by_c
    return pl.multiple_of(position * rows, rows)


def gelu_pair(x):
    c = 0.7978845608028654
    square = x * x
    t = jnp.tanh(c * (x + 0.044715 * (x * square)))
    upper = 0.5 * (1.0 + t)
    return x * upper, upper + 0.5 * x * (1.0 - t * t) * (c + (3 * 0.044715 * c) * square)


def fill_keys(seg_ref, valid_ref, rk, ck):
    seq = seg_ref.shape[1]
    here = pl.ds(pl.multiple_of(lax.axis_index("dp") * seq, seq), seq)
    numbers = seg_ref[...].astype(F32)
    ck[...] = jnp.where(valid_ref[:, here] > 0, numbers, -1.0)
    step = 256
    for i in range(0, seq, step):
        rk[i:i + step, :] = jnp.transpose(jnp.broadcast_to(numbers[:, i:i + step], (128, step)))


def forward_body(
    heads, tok_hbm, grad_hbm, wq_hbm, wk_hbm, wv_hbm, w_out_hbm, w_up_hbm, w_down_hbm, gain_attn_ref, gain_ref, seg_ref, valid_ref,
    qkv_hbm, first_hbm, mixed_hbm, lse_ref, attn_hbm, normed_hbm, hidden_hbm, pre_hbm, rows_hbm,
    qkv, w_out, w_up, w_down, mixed, own, hidden, pre, rk_ref, ck_ref, ks, vs, loads, stores,
    asend, arecv, nbuf, nsend, nrecv, gbuf, gsend, grecv, *scatter,
):
    core, sib, first, second = neighbours()
    rows, width = own.shape
    local = pltpu.make_async_copy
    cols = wq_hbm.shape[1]
    fetch = [
        local(grad_hbm, gbuf.at[0], loads.at[0]), local(tok_hbm, nbuf.at[0], loads.at[1]), local(w_out_hbm, w_out, loads.at[2]),
        local(tok_hbm, nbuf.at[0], loads.at[3]), local(w_up_hbm, w_up, loads.at[4]), local(w_down_hbm, w_down, loads.at[5]),
    ]
    projections = [
        local(w, w_up.at[:, pl.ds(k * cols, cols)], loads.at[6 + k]) for k, w in enumerate((wq_hbm, wk_hbm, wv_hbm))
    ]
    for one in [fetch[1], *projections, fetch[0], fetch[2], fetch[5]]:
        one.start()
    greet(sib, first, second)
    fetch[1].wait()

    def at(s):
        return pl.ds(pl.multiple_of(s * rows, rows), rows)

    def norm_first(part):
        nbuf[0, part, :] = norm_rows(nbuf[0, part, :].astype(F32), gain_attn_ref[...]).astype(BF)

    opening = Gather(nbuf, asend, arecv, sib, first, second)
    send_as_ready(opening, rows, norm_first)
    fill_keys(seg_ref, valid_ref, rk_ref, ck_ref)
    for one in projections:
        one.wait()

    def first_copy(s):
        return local(nbuf.at[s], first_hbm.at[at(s)], stores.at[14 + s])

    def projected(s, carry):
        first_copy(s).start()
        qkv[at(s), :] = dot_nn(nbuf[s], w_up[:, :3 * cols]).astype(BF)
        return carry

    opening.pair()
    lax.fori_loop(0, 2, projected, 0)
    opening.forward()
    opening.middle()
    lax.fori_loop(2, 6, projected, 0)
    opening.finish()
    fetch[0].wait()
    grads = Gather(gbuf, gsend, grecv, sib, first, second)
    grads.start()
    lax.fori_loop(6, 8, projected, 0)
    fetch[4].start()
    qkv_out = local(qkv, qkv_hbm, stores.at[22])
    qkv_out.start()

    def head(h, carry):
        def part(k):
            return lambda at: qkv[pl.ds(at, rows), pl.ds(pl.multiple_of((k * heads + h) * HD, HD), HD)]

        def put_mixed(at, value):
            mixed[pl.ds(at, rows), pl.ds(pl.multiple_of(h * HD, HD), HD)] = value

        def put_lse(a, value):
            lse_ref[h, a * rows:(a + 1) * rows, :] = value

        attend_head(rows, 8, lambda a: block_place(a, rows), part(0), part(1), part(2), rk_ref, ck_ref, put_mixed, put_lse, ks, vs)
        return carry

    lax.fori_loop(0, heads, head, 0)
    mixed_out = local(mixed, mixed_hbm, stores.at[0])
    mixed_out.start()

    def product(p, col):
        return dot_nn(mixed[pl.ds(pl.multiple_of(p * rows, rows), rows), :], w_out[:, pl.ds(col, net.step)])

    fetch[2].wait()
    net = Scatter(product, own, scatter[:8], scatter[8:], core, sib, first, second)
    net.each(net.away)
    for s in range(8):
        first_copy(s).wait()
    opening.drain()
    fetch[3].start()
    net.each(net.one)
    grads.pair()
    fetch[5].wait()
    net.each(net.release)
    slopes = net.away_ref
    tile = net.step

    def back(s, carry):
        for t in range(net.chunks):
            slopes[t, s] = dot_nt(gbuf[s], w_down[t * tile:(t + 1) * tile, :]).astype(BF)
        return carry

    lax.fori_loop(0, 2, back, 0)
    grads.forward(False)
    grads.middle()
    lax.fori_loop(2, 6, back, 0)
    net.each(net.two)
    grads.onward()
    net.each(net.three)
    net.each(net.four)
    attn_out = local(own, attn_hbm, stores.at[1])
    attn_out.start()

    fetch[3].wait()

    def norm(part):
        residual = nbuf[0, part, :].astype(F32) + own[part, :]
        nbuf[0, part, :] = norm_rows(residual, gain_ref[...]).astype(BF)

    ring = Gather(nbuf, nsend, nrecv, sib, first, second)
    send_as_ready(ring, rows, norm)
    fetch[4].wait()
    rows_out = [local(gbuf.at[s], rows_hbm.at[pl.ds(s * rows, rows)], stores.at[6 + s]) for s in range(8)]
    for one in rows_out[:6]:
        one.start()
    def normed_copy(s):
        return local(nbuf.at[s], normed_hbm.at[at(s)], stores.at[14 + s])

    def moved(s):
        return (
            local(hidden.at[s % 2], hidden_hbm.at[at(s)], stores.at[2 + s % 2]),
            local(pre.at[s % 2], pre_hbm.at[at(s)], stores.at[4 + s % 2]),
        )

    def slot(s, carry):
        normed_copy(s).start()

        @pl.when(s >= 2)
        def _():
            for one in moved(s - 2):
                one.wait()

        small = tile // 2
        for t in range(net.chunks):
            for i in range(0, tile, small):
                col = slice(t * tile + i, t * tile + i + small)
                value, slope = gelu_pair(dot_nn(nbuf[s], w_up[:, col]))
                hidden[s % 2, :, col] = value.astype(BF)
                pre[s % 2, :, col] = (slope * slopes[t, s, :, i:i + small].astype(F32)).astype(BF)

        for one in moved(s):
            one.start()
        return carry

    ring.pair()
    lax.fori_loop(0, 2, slot, 0)
    grads.finish()
    lax.fori_loop(6, 8, back, 0)
    for one in rows_out[6:]:
        one.start()
    ring.forward()
    ring.middle()
    lax.fori_loop(2, 6, slot, 0)
    ring.finish()
    lax.fori_loop(6, 8, slot, 0)
    for s in range(8):
        normed_copy(s).wait()
    for one in [*moved(6), *moved(7), *rows_out, mixed_out, attn_out, qkv_out]:
        one.wait()
    ring.drain()
    grads.drain()
    net.drain()


def forward(tokens, grad_out, w_query, w_key, w_value, w_out, w_up, w_down, gain_attn, gain_mlp, segment, valid, heads):
    rows, width = tokens.shape
    seq, hidden = 8 * rows, w_up.shape[1]
    hbm, vmem = pl.BlockSpec(memory_space=HBM_SPACE), pl.BlockSpec(memory_space=VMEM_SPACE)
    shape = jax.ShapeDtypeStruct
    return pl.pallas_call(
        functools.partial(forward_body, heads), name="forward_layer",
        in_specs=[hbm] * 8 + [vmem] * 4,
        out_specs=[hbm, hbm, hbm, vmem, hbm, hbm, hbm, hbm, hbm],
        out_shape=[
            shape((seq, 3 * heads * HD), BF), shape((seq, width), BF),
            shape((seq, heads * HD), BF), shape((heads, seq, 1), F32), shape((rows, width), F32), shape((seq, width), BF),
            shape((seq, hidden), BF), shape((seq, hidden), BF), shape((seq, width), BF),
        ],
        scratch_shapes=[
            pltpu.VMEM((seq, 3 * heads * HD), BF), pltpu.VMEM((heads * HD, width), BF),
            pltpu.VMEM((width, hidden), BF), pltpu.VMEM((hidden, width), BF), pltpu.VMEM((seq, heads * HD), BF),
            pltpu.VMEM((rows, width), F32), pltpu.VMEM((2, rows, hidden), BF), pltpu.VMEM((2, rows, hidden), BF),
            pltpu.VMEM((seq, 128), F32), pltpu.VMEM((1, seq), F32),
            pltpu.VMEM((seq, HD), BF), pltpu.VMEM((seq, HD), BF),
            pltpu.SemaphoreType.DMA((9,)), pltpu.SemaphoreType.DMA((23,)),
            pltpu.SemaphoreType.DMA((11,)), pltpu.SemaphoreType.DMA((11,)),
        ] + gather_scratch(rows, width) * 2 + scatter_scratch(rows, width, 2),
        compiler_params=pltpu.CompilerParams(collective_id=2, has_side_effects=True, vmem_limit_bytes=63 * MIB),
        cost_estimate=pl.CostEstimate(flops=40 * 10**9, bytes_accessed=250 * MIB, transcendentals=0),
    )(tokens, grad_out, w_query, w_key, w_value, w_out, w_up, w_down, gain_attn[None, :], gain_mlp[None, :], segment[None, :],
      valid[None, :])

def row_sums(product):
    part = sum(product[:, i:i + 128] for i in range(0, product.shape[1], 128))
    return lax.dot_general(
        jnp.ones((8, 128), F32), part, (((1,), (1,)), ((), ())), preferred_element_type=F32, precision=lax.Precision.HIGHEST
    )[0:1]


def middle_body(
    pre_hbm, w_up_hbm, normed_hbm, dnorm_hbm, up_hbm, gain_ref, pre, w_up, tiles, ups, dnorm, loads, stores, *scatter
):
    core, sib, first, second = neighbours()
    rows, width = dnorm.shape
    local = pltpu.make_async_copy
    tile = tiles.shape[2]
    count = width // tile
    fetch = [local(pre_hbm, pre, loads.at[0]), local(w_up_hbm, w_up, loads.at[1])]

    def strip(t):
        return pl.ds(pl.multiple_of(t * tile, tile), tile)

    def load_tile(t):
        return local(normed_hbm.at[:, strip(t)], tiles.at[t % 2], loads.at[2 + t % 2])

    def save_tile(t):
        return local(ups.at[t % 2], up_hbm.at[strip(t)], stores.at[1 + t % 2])

    for one in fetch:
        one.start()
    load_tile(0).start()
    greet(sib, first, second)

    def up_back(p, col):
        return dot_nt(pre[pl.ds(pl.multiple_of(p * rows, rows), rows), :], w_up[pl.ds(col, net.step), :])

    net = Scatter(up_back, dnorm, scatter[:8], scatter[8:], core, sib, first, second)
    fetch[0].wait()
    fetch[1].wait()
    net.each(net.away)
    net.each(net.one)

    def weight(t, carry):
        load_tile(t).wait()

        @pl.when(t < count - 1)
        def _():
            load_tile(t + 1).start()

        @pl.when(t >= 2)
        def _():
            save_tile(t - 2).wait()

        value = dot_tn(tiles[t % 2], pre[...])
        ups[t % 2] = value.astype(BF)
        save_tile(t).start()
        gain_ref[:, strip(t)] = row_sums(value * w_up[strip(t), :].astype(F32))
        return carry

    half = count // 2
    lax.fori_loop(0, half, weight, 0)
    net.two(0)
    lax.fori_loop(half, count, weight, 0)
    net.two(1)
    net.each(net.three)
    net.each(net.four)
    out = local(dnorm, dnorm_hbm, stores.at[0])
    out.start()
    out.wait()
    save_tile(count - 2).wait()
    save_tile(count - 1).wait()
    net.drain()


def middle(pre, w_up, normed):
    seq, inner = pre.shape
    width = w_up.shape[0]
    rows = seq // 8
    tile = 256
    hbm, vmem = pl.BlockSpec(memory_space=HBM_SPACE), pl.BlockSpec(memory_space=VMEM_SPACE)
    shape = jax.ShapeDtypeStruct
    return pl.pallas_call(
        middle_body, name="middle_layer",
        in_specs=[hbm] * 3,
        out_specs=[hbm] * 2 + [vmem],
        out_shape=[shape((rows, width), F32), shape((width, inner), BF), shape((1, width), F32)],
        scratch_shapes=[
            pltpu.VMEM((seq, inner), BF), pltpu.VMEM((width, inner), BF),
            pltpu.VMEM((2, seq, tile), BF), pltpu.VMEM((2, tile, inner), BF), pltpu.VMEM((rows, width), F32),
            pltpu.SemaphoreType.DMA((4,)), pltpu.SemaphoreType.DMA((3,)),
        ] + scatter_scratch(rows, width, 2),
        compiler_params=pltpu.CompilerParams(collective_id=5, has_side_effects=True, vmem_limit_bytes=56 * MIB),
        cost_estimate=pl.CostEstimate(flops=45 * 10**9, bytes_accessed=200 * MIB, transcendentals=0),
    )(pre, w_up, normed)


def turn_body(
    heads, dnorm_hbm, attn_hbm, tok_hbm, grad_hbm, w_out_hbm, qkv_hbm, mixed_hbm, hidden_hbm, w_down_hbm,
    gain_ref, lse_ref, seg_ref, valid_ref,
    branch_hbm, dqkv_hbm, residual_hbm, mlp_hbm,
    own, attn, tok, grad, w_out, qkv, mixed, hidden, w_down, dmixed, dqkv, rk_ref, ck_ref, ks, vs, dks, dvs, loads, stores,
    bbuf, bsend, brecv, *scatter,
):
    core, sib, first, second = neighbours()
    rows, width = tok.shape
    local = pltpu.make_async_copy
    fetch = [
        local(source, target, loads.at[i])
        for i, (source, target) in enumerate((
            (dnorm_hbm, own), (attn_hbm, attn), (tok_hbm, tok), (grad_hbm, grad), (w_out_hbm, w_out), (qkv_hbm, qkv),
            (mixed_hbm, mixed), (hidden_hbm, hidden), (w_down_hbm, w_down),
        ))
    ]
    for one in fetch:
        one.start()
    greet(sib, first, second)
    for one in fetch[:4]:
        one.wait()

    def norm(part):
        residual = tok[part, :].astype(F32) + attn[part, :]
        total = grad[part, :].astype(F32) + norm_back(residual, gain_ref[...], own[part, :])
        own[part, :] = total
        bbuf[0, part, :] = total.astype(BF)

    ring = Gather(bbuf, bsend, brecv, sib, first, second)
    send_as_ready(ring, rows, norm)
    residual_out = local(own, residual_hbm, stores.at[0])
    residual_out.start()
    fill_keys(seg_ref, valid_ref, rk_ref, ck_ref)
    fetch[4].wait()

    def moved(s):
        return local(bbuf.at[s], branch_hbm.at[pl.ds(pl.multiple_of(s * rows, rows), rows)], stores.at[2 + s])

    def slot(s, carry):
        moved(s).start()
        dmixed[pl.ds(pl.multiple_of(s * rows, rows), rows), :] = dot_nt(bbuf[s], w_out[...]).astype(BF)
        return carry

    def down(p, col):
        return dot_nn(hidden[pl.ds(pl.multiple_of(p * rows, rows), rows), :], w_down[:, pl.ds(col, net.step)])

    net = Scatter(down, attn, scatter[:8], scatter[8:], core, sib, first, second)
    ring.pair()
    lax.fori_loop(0, 2, slot, 0)
    fetch[7].wait()
    fetch[8].wait()
    net.each(net.away)
    ring.forward()
    ring.middle()
    lax.fori_loop(2, 6, slot, 0)
    net.each(net.one)
    ring.finish()
    lax.fori_loop(6, 8, slot, 0)
    fetch[5].wait()
    fetch[6].wait()

    def head(h, carry):
        def load(ref, k):
            return lambda at: ref[pl.ds(at, rows), pl.ds(pl.multiple_of((k * heads + h) * HD, HD), HD)]

        def save(k):
            def put(at, value):
                dqkv[pl.ds(at, rows), pl.ds(pl.multiple_of((k * heads + h) * HD, HD), HD)] = value
            return put

        unattend_head(
            rows, 8, lambda a: block_place(a, rows), load(qkv, 0), load(qkv, 1), load(qkv, 2), load(dmixed, 0), load(mixed, 0),
            lambda a: lse_ref[h, a * rows:(a + 1) * rows, :], rk_ref, ck_ref, save(0), save(1), save(2), ks, vs, dks, dvs,
        )

        return carry

    lax.fori_loop(0, heads, head, 0)
    dqkv_out = local(dqkv, dqkv_hbm, stores.at[1])
    dqkv_out.start()
    net.each(net.two)
    net.each(net.three)
    net.each(net.four)
    mlp_out = local(attn, mlp_hbm, stores.at[10])
    mlp_out.start()
    for s in range(8):
        moved(s).wait()
    for one in (residual_out, dqkv_out, mlp_out):
        one.wait()
    ring.drain()
    net.drain()


def turn(dnorm, attn_own, tokens, grad_out, w_out, qkv, mixed, hidden, w_down, gain, lse, segment, valid, heads):
    rows, width = tokens.shape
    seq = 8 * rows
    hbm, vmem = pl.BlockSpec(memory_space=HBM_SPACE), pl.BlockSpec(memory_space=VMEM_SPACE)
    shape = jax.ShapeDtypeStruct
    cols = heads * HD
    return pl.pallas_call(
        functools.partial(turn_body, heads), name="turn_layer",
        in_specs=[hbm] * 9 + [vmem] * 4,
        out_specs=[hbm] * 4,
        out_shape=[shape((seq, width), BF), shape((seq, 3 * cols), BF), shape((rows, width), F32), shape((rows, width), F32)],
        scratch_shapes=[
            pltpu.VMEM((rows, width), F32), pltpu.VMEM((rows, width), F32), pltpu.VMEM((rows, width), BF),
            pltpu.VMEM((rows, width), BF), pltpu.VMEM((cols, width), BF), pltpu.VMEM((seq, 3 * cols), BF),
            pltpu.VMEM((seq, cols), BF), pltpu.VMEM(hidden.shape, BF), pltpu.VMEM(w_down.shape, BF),
            pltpu.VMEM((seq, cols), BF), pltpu.VMEM((seq, 3 * cols), BF), pltpu.VMEM((seq, 128), F32), pltpu.VMEM((1, seq), F32),
            pltpu.VMEM((seq, HD), BF), pltpu.VMEM((seq, HD), BF), pltpu.VMEM((seq, HD), F32), pltpu.VMEM((seq, HD), F32),
            pltpu.SemaphoreType.DMA((9,)), pltpu.SemaphoreType.DMA((11,)),
        ] + gather_scratch(rows, width) + scatter_scratch(rows, width, 2),
        compiler_params=pltpu.CompilerParams(collective_id=3, has_side_effects=True, vmem_limit_bytes=63 * MIB),
        cost_estimate=pl.CostEstimate(flops=45 * 10**9, bytes_accessed=200 * MIB, transcendentals=0),
    )(dnorm, attn_own, tokens, grad_out, w_out, qkv, mixed, hidden, w_down, gain[None, :], lse, segment[None, :], valid[None, :])


def down_body(hidden_ref, grad_ref, out_ref):
    out_ref[...] = dot_tn(hidden_ref[...], grad_ref[...]).astype(BF)


def down_weights(hidden, grads):
    seq, inner = hidden.shape
    width = grads.shape[1]
    tile = 512
    return pl.pallas_call(
        down_body, name="down_weights", grid=(width // tile,),
        in_specs=[pl.BlockSpec((seq, inner), lambda t: (0, 0)), pl.BlockSpec((seq, tile), lambda t: (0, t))],
        out_specs=pl.BlockSpec((inner, tile), lambda t: (0, t)),
        out_shape=jax.ShapeDtypeStruct((inner, width), BF),
        compiler_params=pltpu.CompilerParams(vmem_limit_bytes=63 * MIB),
        cost_estimate=pl.CostEstimate(flops=2 * seq * width * inner, bytes_accessed=16 * MIB, transcendentals=0),
    )(hidden, grads)


def weights_body(normed_ref, branch_ref, dqkv_ref, mixed_ref, out_ref):
    cols = mixed_ref.shape[1]
    out_ref[:, :3 * cols] = dot_tn(normed_ref[...], dqkv_ref[...]).astype(BF)
    out_ref[:, 3 * cols:] = dot_tn(mixed_ref[...], branch_ref[...]).astype(BF)


def weights(normed, branch, dqkv, mixed):
    seq, width = normed.shape
    cols = mixed.shape[1]
    tile = cols
    full = lambda c: pl.BlockSpec((seq, c), lambda t: (0, 0))
    strip = pl.BlockSpec((seq, tile), lambda t: (0, t))
    return pl.pallas_call(
        weights_body, name="weight_gradients", grid=(width // tile,),
        in_specs=[strip, strip, full(3 * cols), full(cols)],
        out_specs=pl.BlockSpec((tile, 4 * cols), lambda t: (t, 0)),
        out_shape=jax.ShapeDtypeStruct((width, 4 * cols), BF),
        compiler_params=pltpu.CompilerParams(vmem_limit_bytes=63 * MIB),
        cost_estimate=pl.CostEstimate(flops=2 * seq * width * 4 * cols, bytes_accessed=30 * MIB, transcendentals=0),
    )(normed, branch, dqkv, mixed)


def unpack_body(sum_ref, q_ref, k_ref, v_ref, out_ref):
    cols = q_ref.shape[1]
    for k, ref in enumerate((q_ref, k_ref, v_ref)):
        ref[...] = sum_ref[:, k * cols:(k + 1) * cols].astype(F32)
    for i in range(sum_ref.shape[0] // cols):
        out_ref[:, i * cols:(i + 1) * cols] = sum_ref[i * cols:(i + 1) * cols, 3 * cols:].astype(F32)


def unpack(summed, cols):
    rows = summed.shape[0]
    vmem = pl.BlockSpec(memory_space=VMEM_SPACE)
    shapes = [jax.ShapeDtypeStruct((rows, cols), F32)] * 3 + [jax.ShapeDtypeStruct((cols, rows), F32)]
    return pl.pallas_call(unpack_body, name="unpack", in_specs=[vmem], out_specs=[vmem] * 4, out_shape=shapes)(summed)


class Total:
    def __init__(self, vec, got, sends, recvs, sib, first, second):
        self.vec, self.got = vec, got
        self.partners = [sib, first, second]
        self.copies = [
            pltpu.make_async_remote_copy(
                src_ref=vec, dst_ref=got.at[k], send_sem=sends.at[k], recv_sem=recvs.at[k], device_id=other, device_id_type=MESH,
            )
            for k, other in enumerate(self.partners)
        ]

    def start(self, k):
        self.copies[k].start()

    def add(self, k):
        self.copies[k].wait()
        self.vec[...] += self.got[k]
        if k + 1 < len(self.copies):
            self.copies[k + 1].start()


def finish_body(
    dqkv_hbm, wq_hbm, wk_hbm, wv_hbm, tok_hbm, attn_hbm, gres_hbm, mlp_hbm, part_hbm, gain_ref, part_mlp_ref,
    valid_ref, tokens_hbm, grads_hbm, total_ref,
    dqkv, w_qkv, part_ref, tok, attn, gres, out, mlp, dnorm, vec, got, sends, recvs, loads, stores, *scatter,
):
    core, sib, first, second = neighbours()
    rows, width = mlp.shape
    cols = wq_hbm.shape[1]
    local = pltpu.make_async_copy
    pairs = [(dqkv_hbm, dqkv)]
    pairs += [(w, w_qkv.at[:, pl.ds(k * cols, cols)]) for k, w in enumerate((wq_hbm, wk_hbm, wv_hbm))]
    pairs += [(tok_hbm, tok), (attn_hbm, attn), (gres_hbm, gres), (mlp_hbm, mlp), (part_hbm, part_ref)]
    fetch = [local(source, target, loads.at[i]) for i, (source, target) in enumerate(pairs)]
    for one in fetch:
        one.start()
    total = Total(vec, got, sends, recvs, sib, first, second)
    greet(*total.partners)

    def project_back(p, col):
        return dot_nt(dqkv[pl.ds(pl.multiple_of(p * rows, rows), rows), :], w_qkv[pl.ds(col, net.step), :])

    net = Scatter(project_back, dnorm, scatter[:8], scatter[8:], core, sib, first, second)
    for one in fetch[:4]:
        one.wait()
    net.each(net.away)
    net.each(net.one)
    for one in fetch[4:]:
        one.wait()
    own = pl.ds(pl.multiple_of((lax.axis_index("dp") * 8 + lax.axis_index("mp")) * rows, rows), rows)
    mask = jnp.transpose(jnp.broadcast_to(valid_ref[:, own].astype(F32), (128, rows)))
    vec[...] = jnp.zeros_like(vec)
    vec[1:2, :] = part_mlp_ref[...]
    step = 64
    for i in range(0, rows, step):
        part = slice(i, i + step)
        attn_part, mlp_part = attn[part, :], mlp[part, :]
        stream = tok[part, :].astype(F32) + attn_part + mlp_part
        out[0, part, :] = stream
        for k, value in enumerate((stream, attn_part, mlp_part)):
            vec[2 + k:3 + k, :] += jnp.sum(mask[part, 0:1] * value * value, axis=0, keepdims=True)
    for i in range(0, width, cols):
        tile = slice(i, i + cols)
        vec[0:1, tile] = row_sums(part_ref[tile, :3 * cols].astype(F32) * w_qkv[tile, :].astype(F32))
    tokens_out = local(out.at[0], tokens_hbm, stores.at[0])
    tokens_out.start()
    total.start(0)
    net.each(net.two)
    total.add(0)
    net.each(net.three)
    total.add(1)
    net.each(net.four)

    def last(part):
        back = norm_back(tok[part, :].astype(F32), gain_ref[...], dnorm[part, :])
        out[1, part, :] = gres[part, :] + back

    rows_loop(rows, 32, last)
    grads_out = local(out.at[1], grads_hbm, stores.at[1])
    grads_out.start()
    total.add(2)
    total_ref[...] = vec[...]
    tokens_out.wait()
    grads_out.wait()
    net.drain()


def finish(dqkv, w_query, w_key, w_value, tokens, attn_own, grad_residual, mlp_own, part_last, gain, part_mlp, valid):
    seq = dqkv.shape[0]
    rows, width = tokens.shape
    cols = w_query.shape[1]
    stages = 3
    hbm, vmem = pl.BlockSpec(memory_space=HBM_SPACE), pl.BlockSpec(memory_space=VMEM_SPACE)
    shape = jax.ShapeDtypeStruct
    return pl.pallas_call(
        finish_body, name="last_scatters",
        in_specs=[hbm] * 9 + [vmem] * 3,
        out_specs=[hbm] * 2 + [vmem],
        out_shape=[shape((rows, width), F32), shape((rows, width), F32), shape((8, width), F32)],
        scratch_shapes=[
            pltpu.VMEM((seq, 3 * cols), BF),
            pltpu.VMEM((width, 3 * cols), BF), pltpu.VMEM(part_last.shape, BF), pltpu.VMEM((rows, width), BF), pltpu.VMEM((rows, width), F32),
            pltpu.VMEM((rows, width), F32), pltpu.VMEM((2, rows, width), F32), pltpu.VMEM((rows, width), F32),
            pltpu.VMEM((rows, width), F32), pltpu.VMEM((8, width), F32), pltpu.VMEM((stages, 8, width), F32),
            pltpu.SemaphoreType.DMA((stages,)), pltpu.SemaphoreType.DMA((stages,)),
            pltpu.SemaphoreType.DMA((9,)), pltpu.SemaphoreType.DMA((2,)),
        ] + scatter_scratch(rows, width, 2),
        compiler_params=pltpu.CompilerParams(collective_id=4, has_side_effects=True, vmem_limit_bytes=63 * MIB),
        cost_estimate=pl.CostEstimate(flops=30 * 10**9, bytes_accessed=200 * MIB, transcendentals=0),
    )(dqkv, w_query, w_key, w_value, tokens, attn_own, grad_residual, mlp_own, part_last, gain[None, :], part_mlp,
      valid[None, :])


def after(value, *others):
    return lax.optimization_barrier((value,) + others)[0]


def over_mp(value):
    return lax.all_gather(value, "mp", axis=0, tiled=True)


def sum_mp(value):
    return lax.psum_scatter(value.astype(BF), "mp", scatter_dimension=0, tiled=True).astype(F32)


def sum_dp(value, axis):
    return lax.psum_scatter(value.astype(BF), "dp", scatter_dimension=axis, tiled=True)


def on_device(tokens, segment, valid, gain_attn, w_query, w_key, w_value, w_out, gain_mlp, w_up, w_down, grad_out):
    own_rows, width = tokens.shape
    seq_rows = segment.shape[0]
    heads = w_query.shape[1] // HD
    n_dp, n_mp = lax.axis_size("dp"), lax.axis_size("mp")
    dp, me = lax.axis_index("dp"), lax.axis_index("mp")
    cube = n_mp == 8 and n_dp in (1, 2, 4) and width == 8 * heads * HD
    order = jnp.arange(seq_rows // own_rows, dtype=jnp.int32)
    valid_group = lax.dynamic_slice_in_dim(valid, dp * seq_rows, seq_rows)
    valid_own = lax.dynamic_slice_in_dim(valid_group, me * own_rows, own_rows)
    tokens32 = tokens.astype(F32)

    if cube:
        qkv, normed, mixed, lse, attn_own, normed_mlp, hidden, grad_pre, grad_rows = forward(
            tokens, grad_out, w_query, w_key, w_value, w_out, w_up, w_down, gain_attn, gain_mlp, segment, valid, heads
        )
    else:
        row_key = segment[:, None]
        col_key = jnp.where(valid_group > 0, segment, -1)[None, :]
        normed = over_mp(norm_rows(tokens32, gain_attn).astype(BF))
        qkv = jnp.concatenate([dot_nn(normed, w).astype(BF) for w in (w_query, w_key, w_value)], 1)
        mixed, lse = attn_fwd(qkv, order, row_key, col_key, heads, own_rows)
        grad_rows = over_mp(after(grad_out, qkv))
        attn_own = sum_mp(dot_nn(mixed, w_out))
        normed_mlp = over_mp(norm_rows(tokens32 + attn_own, gain_mlp).astype(BF))
        hidden = gelu_fn(dot_nn(normed_mlp, w_up)).astype(BF)
    residual = tokens32 + attn_own

    if cube:
        part_down = down_weights(hidden, grad_rows)
        sum_down = sum_dp(part_down, 1)
        grad_normed, part_up, gain_mlp_part = middle(after(grad_pre, part_down), w_up, normed_mlp)
        sum_up = sum_dp(part_up, 0)
        grad_branch, grads_qkv, grad_residual, mlp_own = turn(
            grad_normed, attn_own, tokens, grad_out, w_out, qkv, mixed, hidden, w_down, gain_mlp, lse, segment, valid, heads
        )
        grads_qkv, sum_down = lax.optimization_barrier((grads_qkv, sum_down))
        part_last = weights(normed, grad_branch, grads_qkv, mixed)
        grad_last = sum_dp(part_last, 0)
        grad_down = after(sum_down, part_last).astype(F32)
        grads_qkv = after(grads_qkv, part_last, grad_down)
        stream, grad_tokens, summed = finish(
            grads_qkv, w_query, w_key, w_value, tokens, attn_own, grad_residual, mlp_own, part_last, gain_attn, gain_mlp_part, valid
        )
        gain_rows = width // (n_dp * n_mp)
        ours = lax.dynamic_index_in_dim(summed[:2].reshape(2, n_dp, n_mp, gain_rows), me, 2, False)
        squares = jnp.sum(summed[2:5], axis=1)
        parts = []
        for bit in range(n_dp):
            theirs = lax.dynamic_index_in_dim(ours, jnp.bitwise_xor(dp, bit), 1, False)
            part = jnp.concatenate([theirs.reshape(-1), squares])
            parts.append(lax.ppermute(part, "dp", [(i, i ^ bit) for i in range(n_dp)]) if bit else part)
        grad_up = after(sum_up, stream).astype(F32)
        out_tokens, grad_tokens = stream.astype(BF), grad_tokens.astype(BF)
        while len(parts) > 1:
            parts = [low + high for low, high in zip(parts[::2], parts[1::2])]
        gain_sums, squares = parts[0][:2 * gain_rows].reshape(2, gain_rows), parts[0][2 * gain_rows:]
    else:
        grad_down = sum_dp(dot_tn(hidden, grad_rows), 1).astype(F32)
        grad_pre = (gelu_pair(dot_nn(normed_mlp, w_up))[1] * dot_nt(grad_rows, w_down)).astype(BF)
        part_up = dot_tn(normed_mlp, grad_pre)
        grad_up = sum_dp(part_up, 0).astype(F32)
        gain_mlp_part = jnp.sum(part_up * w_up.astype(F32), axis=1)
        grad_residual = grad_out.astype(F32) + norm_back(residual, gain_mlp, sum_mp(dot_nt(grad_pre, w_up)))
        grad_branch = over_mp(grad_residual.astype(BF))
        grad_mixed = dot_nt(grad_branch, w_out).astype(BF)
        grads_qkv = jnp.concatenate(attn_bwd(qkv, grad_mixed, mixed, lse, order, row_key, col_key, heads, own_rows), 1)
        grad_out_proj = sum_dp(dot_tn(mixed, grad_branch), 1).astype(F32)
        part_qkv = dot_tn(normed, grads_qkv)
        grad_qkv = jnp.split(sum_dp(part_qkv, 0).astype(F32), 3, axis=1)
        w_qkv = jnp.concatenate([w_query, w_key, w_value], 1)
        gain_attn_part = jnp.sum(part_qkv * w_qkv.astype(F32), axis=1)
        mlp_own = sum_mp(dot_nn(hidden, w_down))
        grad_normed_attn = sum_mp(dot_nt(grads_qkv, w_qkv))
        stream = residual + mlp_own
        out_tokens = stream.astype(BF)
        grad_tokens = (grad_residual + norm_back(tokens32, gain_attn, grad_normed_attn)).astype(BF)
        mask_own = valid_own.astype(F32)[:, None]
        squares = [jnp.sum(mask_own * part * part, axis=0) for part in (stream, attn_own, mlp_own)]
        summed = lax.psum(jnp.stack([gain_attn_part, gain_mlp_part, *squares]), ("dp", "mp"))
    counted = jnp.maximum(jnp.sum(valid).astype(F32) * width, 1.0)
    gain_rows = width // (n_dp * n_mp)
    place = (dp * n_mp + me) * gain_rows
    if not cube:
        gain_sums = lax.dynamic_slice_in_dim(summed[:2], place, gain_rows, 1)
        squares = jnp.sum(summed[2:5], axis=1)
    rms = jnp.sqrt(squares / counted)
    gains = [
        gain_sums[k] / lax.dynamic_slice_in_dim(gain, place, gain_rows) for k, gain in enumerate((gain_attn, gain_mlp))
    ]
    if cube:
        grad_last, *_ = lax.optimization_barrier((grad_last, grad_up, out_tokens, grad_tokens, rms, gains))
        *grad_qkv, grad_out_proj = unpack(grad_last, heads * HD)
    return (
        out_tokens,
        grad_tokens,
        gains[0],
        *grad_qkv,
        grad_out_proj,
        gains[1],
        grad_up,
        grad_down,
        rms[0],
        rms[1],
        rms[2],
    )


def solution(mesh):
    tokens_spec = P(("dp", "mp"), None)
    cols, rows = P(None, "mp"), P("mp", None)
    return jax.shard_map(
        on_device,
        mesh=mesh,
        in_specs=(tokens_spec, P("dp"), P(), P(), cols, cols, cols, rows, P(), cols, rows, tokens_spec),
        out_specs=(
            tokens_spec,
            tokens_spec,
            P(("dp", "mp")),
            P("dp", "mp"),
            P("dp", "mp"),
            P("dp", "mp"),
            P("mp", "dp"),
            P(("dp", "mp")),
            P("dp", "mp"),
            P("mp", "dp"),
            P(),
            P(),
            P(),
        ),
        check_vma=False,
    )
```
